32 devices in a mesh: obj: 16 (over z, x, core), ep: 2 (over y).
Axes of the slice: x: 2, y: 2, z: 4, core: 2. Of those that a mesh axis runs over, the one named last changes fastest.
Arguments:
- light_curves: float32 [2048, 256], P('obj', 'ep'), may hold values from -40 to 40
- valid: int32 [2048, 256], P('obj', 'ep'), may hold values 0 or 1
- pixel: int32 [2048], P('obj'), may hold values from 0 to 63, never falling along the last dimension, each value on 1 to 64 neighbouring positions
- inv_sigma: float32 [2048], P('obj'), may hold values from 0.5 to 4
- modes_init: float32 [256, 16], P('ep'), may hold values from -6 to 6
- epoch_jitter: float32 [256], replicated, may hold values from 0 to 0.9
- freq_index: int32 [2048], replicated, may hold values from 4 to 511
Outputs:
- residual: float32 [2048, 256], P('obj', 'ep')
- power: float32 [2048, 2048], P(('obj', 'ep'))
The draws below stay inside these ranges and needn't reach their ends.
Inputs may be any that keep to these rules, and one draw needn't show every extreme that they name: Pixels never decrease along the objects; each pixel holds 1 to 64 objects, and some pixel exactly 64.
All inputs are finite; a program needn't handle non-finite values. No bound on the sum of `valid` on one device may be relied on, other than what follows from the above.
Results may differ from the reference program's by a relative error of at most 0.0052.
Values may be sent and summed in bfloat16 or wider, within the bound.
A program may use at most 64 MiB of HBM per device.

```python
import math
import jax
import jax.numpy as jnp
import numpy as np
from jax import lax

K = 16
F = 2048
ITERS = 2
NOBJ = 2048
NEP = 256
NPIX = 64
MOST = 64
N_OBJ = 16


def draw_light_curves(key, part):
    key_strength = jax.random.fold_in(key, 101)
    key_amp = jax.random.fold_in(key, 102)
    key_mode = jax.random.fold_in(key, 103)
    key_noise = jax.random.fold_in(key, 104)
    key_jump = jax.random.fold_in(key, 105)
    key_size = jax.random.fold_in(key, 106)
    strength = jnp.exp(jax.random.uniform(key_strength, (K,), jnp.float32, math.log(0.3), math.log(3.0)))
    amplitude = jax.random.normal(key_amp, (NOBJ, K), jnp.float32) * strength[None, :]
    pattern = jax.random.normal(key_mode, (NEP, K), jnp.float32)
    trend = jnp.dot(amplitude, pattern.T, precision=lax.Precision.HIGHEST) * (1.5 / math.sqrt(K))
    noise = jax.random.normal(key_noise, (NOBJ, NEP), jnp.float32)
    jumps = jnp.where(jax.random.uniform(key_jump, (NOBJ, NEP), jnp.float32) < 0.02, 6.0 * jax.random.normal(key_size, (NOBJ, NEP), jnp.float32), 0.0)
    return jnp.clip(trend + noise + jumps, -40.0, 40.0).astype(jnp.float32)


def with_ends(drawn, rng, low, high):
    dims = drawn.shape
    spot = [jax.random.randint(jax.random.fold_in(rng, axis), (), 0, dims[axis]) for axis in range(len(dims))]
    drawn = drawn.at[tuple(spot)].set(low)
    longest = dims.index(max(dims))
    spot[longest] = (spot[longest] + 1) % dims[longest]
    return drawn.at[tuple(spot)].set(high)


def block_scale(own_key, dims, split, smallest, largest):
    loudness, own = 1.0, jax.random.fold_in(own_key, 6)
    for axis_at, blocks in split:
        steps = jnp.exp(jax.random.uniform(jax.random.fold_in(own, axis_at), (blocks,), jnp.float32, smallest / len(split), largest / len(split)))
        loudness = loudness * jnp.repeat(steps, dims[axis_at] // blocks).reshape([-1 if axis == axis_at else 1 for axis in range(len(dims))])
    return loudness


def split_up(amount, total, most, slope):
    loads = [(1 << 20) // math.isqrt(standing ** slope) + 1 for standing in range(2, amount + 1)]
    spare, holding = total - most - (amount - 1), [1] * (amount - 1)
    while spare > 0:
        candidates = [i for i in range(amount - 1) if holding[i] < most]
        mass, remaining = sum([loads[i] for i in candidates]), spare
        for i in candidates:
            extra = min(most - holding[i], max(1, remaining * loads[i] // mass), spare)
            holding[i] = holding[i] + extra
            spare = spare - extra
    return np.array([most] + holding)


def uneven(stream_key, amount, total, bound, lean):
    if amount == 2:
        one = jax.random.randint(stream_key, (), max(1, total - bound), min(bound, total - 1) + 1)
        return jnp.stack([one, total - one])
    lengths = jnp.asarray(split_up(amount, total, bound, lean), jnp.int32)
    twos = (amount - 1) // 2
    donor, receiver = lengths[1:1 + 2 * twos:2], lengths[2:2 + 2 * twos:2]
    margin = jnp.minimum(donor - 1, bound - receiver)
    shifted = jax.random.randint(jax.random.fold_in(stream_key, 1), (twos,), 0, 1 << 20) % (margin + 1)
    lengths = lengths.at[1:1 + 2 * twos:2].set(donor - shifted).at[2:2 + 2 * twos:2].set(receiver + shifted)
    return lengths[jax.random.permutation(jax.random.fold_in(stream_key, 2), amount)]


def bell_draw(rng, extent, deviation, most, cuts=(), held_as=jnp.bfloat16):
    factor_of = block_scale(rng, extent, cuts, -0.22, 0.18) if cuts else 1.0
    array = jax.random.normal(rng, extent, jnp.float32) * deviation * factor_of
    return jnp.minimum(jnp.maximum(array, -most), most).astype(held_as)


def setup_inputs(seed: int = 0) -> dict:
    key_of = jax.random.split(jax.random.key(seed), 8)
    return {
        "light_curves": draw_light_curves(jax.random.fold_in(key_of[7], 71), 0),
        "valid": with_ends((jax.random.randint(key_of[1], (NOBJ, NEP), 0, 4) < 3).astype(jnp.int32), jax.random.fold_in(key_of[1], 1), 0, 1),
        "pixel": jnp.searchsorted(jnp.cumsum(uneven(key_of[2], NPIX, NOBJ, MOST, 2)), jnp.arange(NOBJ), side="right").astype(jnp.int32),
        "inv_sigma": jnp.clip(jnp.exp(math.log(4.0) - 2.0794415 * jax.random.uniform(key_of[3], (NOBJ,), jnp.float32) ** block_scale(key_of[3], (NOBJ,), ((0, 16),), -0.2, 0.2)), 0.5, 4.0),
        "modes_init": bell_draw(key_of[4], (NEP, K), 1.0, 6.0, ((0, 2),), jnp.float32),
        "epoch_jitter": jnp.clip(jax.random.uniform(key_of[5], (NEP,), jnp.float32, 0.0, 0.9), 0.0, 0.9),
        "freq_index": with_ends(jax.random.randint(key_of[6], (F,), 4, 2 * NEP), jax.random.fold_in(key_of[6], 1), 4, (2 * NEP) - 1).astype(jnp.int32),
    }


HUBER = 1.345
DAMP = 2.0
RIDGE = 0.05
HIGHEST = lax.Precision.HIGHEST

def robust_weights(resid, mask_f, inv_sigma, pixel, npix):
    scaled = resid * inv_sigma[:, None]
    squares = lax.optimization_barrier(jnp.sum(mask_f * scaled * scaled, axis=1))
    valid_count = lax.optimization_barrier(jnp.sum(mask_f, axis=1))
    member = (pixel[None, :] == jnp.arange(npix, dtype=jnp.int32)[:, None]).astype(jnp.float32)
    sums = jnp.dot(member, squares, precision=HIGHEST)
    counts = jnp.dot(member, valid_count, precision=HIGHEST)
    spread = jnp.sqrt(sums / jnp.maximum(counts, 1.0) + 1e-06)
    object_spread = jnp.dot(spread, member, precision=HIGHEST)
    zscore = scaled / object_spread[:, None]
    huber = HUBER / jnp.maximum(jnp.abs(zscore), HUBER)
    return mask_f * huber * (inv_sigma * inv_sigma)[:, None]

def damped_solve(gram, target):
    order = target.shape[1]
    identity = jnp.eye(order, dtype=gram.dtype)
    return jnp.linalg.solve(gram + DAMP * identity, target[..., None])[..., 0]

def spectrum_sums(weighted, weight, times, freqs):
    cycles = times[:, None] * freqs[None, :]
    angle = 2.0 * math.pi * (cycles - jnp.floor(cycles))
    basis = jnp.concatenate([jnp.cos(angle), jnp.sin(angle), jnp.cos(2.0 * angle), jnp.sin(2.0 * angle)], axis=1).astype(jnp.bfloat16)
    width = freqs.shape[0]
    by_weight = jnp.dot(weight.astype(jnp.float32), basis.astype(jnp.float32), preferred_element_type=jnp.float32)
    by_value = jnp.dot(weighted.astype(jnp.float32), basis[:, :2 * width].astype(jnp.float32), preferred_element_type=jnp.float32)
    return (by_weight, by_value)

def powers(by_weight, by_value, total, level):
    width = by_value.shape[1] // 2
    cosine = by_weight[:, :width]
    sine = by_weight[:, width:2 * width]
    cosine_two = by_weight[:, 2 * width:3 * width]
    sine_two = by_weight[:, 3 * width:]
    mean_level = level / total
    ycos = by_value[:, :width] - mean_level * cosine
    ysin = by_value[:, width:] - mean_level * sine
    cc_term = 0.5 * (total + cosine_two) - cosine * cosine / total + RIDGE * total
    ss_term = 0.5 * (total - cosine_two) - sine * sine / total + RIDGE * total
    cs_term = 0.5 * sine_two - cosine * sine / total
    determinant = cc_term * ss_term - cs_term * cs_term
    return (ss_term * ycos * ycos + cc_term * ysin * ysin - 2.0 * cs_term * ycos * ysin) / determinant

def reference(light_curves, valid, pixel, inv_sigma, modes_init, epoch_jitter, freq_index):
    npix = 4 * N_OBJ
    mask_f = valid.astype(jnp.float32)
    modes = modes_init
    coef = jnp.zeros((NOBJ, K), jnp.float32)
    for iteration in range(ITERS):
        resid = light_curves - jnp.dot(coef, modes.T, precision=HIGHEST)
        weight = robust_weights(resid, mask_f, inv_sigma, pixel, npix)
        outer = (modes[:, :, None] * modes[:, None, :]).reshape(NEP, K * K)
        gram = jnp.dot(weight, outer, precision=HIGHEST).reshape(NOBJ, K, K)
        target = jnp.dot(weight * light_curves, modes, precision=HIGHEST)
        coef = damped_solve(gram, target)
        resid = light_curves - jnp.dot(coef, modes.T, precision=HIGHEST)
        weight = robust_weights(resid, mask_f, inv_sigma, pixel, npix)
        outer = (coef[:, :, None] * coef[:, None, :]).reshape(NOBJ, K * K)
        gram = jnp.dot(weight.T, outer, precision=HIGHEST).reshape(NEP, K, K)
        target = jnp.dot((weight * light_curves).T, coef, precision=HIGHEST)
        modes = damped_solve(gram, target)
    residual = light_curves - jnp.dot(coef, modes.T, precision=HIGHEST)
    final_weight = robust_weights(residual, mask_f, inv_sigma, pixel, npix)
    weighted = (final_weight * residual).astype(jnp.bfloat16)
    weight_b = final_weight.astype(jnp.bfloat16)
    total = lax.optimization_barrier(jnp.sum(weight_b, axis=1, keepdims=True, dtype=jnp.float32))
    level = lax.optimization_barrier(jnp.sum(weighted, axis=1, keepdims=True, dtype=jnp.float32))
    times = jnp.arange(NEP, dtype=jnp.int32).astype(jnp.float32) + epoch_jitter
    freqs = (freq_index + 1).astype(jnp.float32) / (4.0 * NEP)
    size = math.gcd(F, 512)
    blocks = freqs.reshape(F // size, size)

    def one_block(block_freqs):
        by_weight, by_value = spectrum_sums(weighted, weight_b, times, block_freqs)
        return powers(by_weight, by_value, total, level)
    power = lax.map(one_block, blocks)
    power = jnp.transpose(power, (1, 0, 2)).reshape(NOBJ, F)
    return (residual, power)
```

```python
import functools
import math

import jax
import jax.numpy as jnp
from jax import lax
from jax.experimental import pallas as pl
from jax.experimental.pallas import tpu as pltpu
from jax.sharding import PartitionSpec as P

ITERS = 2


HUBER = 1.345
DAMP = 2.0
RIDGE = 0.05
HIGHEST = lax.Precision.HIGHEST
LANES = 128
SUB = 8
GROUP = 4
ABSENT = 1e30
F32 = jnp.float32
BF16 = jnp.bfloat16
STRIP = 32
MESH = pl.DeviceIdType.MESH


def halves(values):
    high = values.astype(BF16)
    return high, (values - high.astype(F32)).astype(BF16)


def cyclic_outer(vectors):
    order = vectors.shape[0]
    parts = [vectors * vectors]
    for shift in range(1, order // 2 + 1):
        turned = jnp.concatenate([vectors[shift:], vectors[:shift]], axis=0)
        part = vectors * turned
        parts.append(part if shift < order // 2 else part[: order // 2])
    return jnp.concatenate(parts, axis=0)


def cyclic_row(i, j, order):
    ahead = (j - i) % order
    if ahead == order // 2:
        return ahead * order + min(i, j)
    return ahead * order + i if ahead < order // 2 else (order - ahead) * order + j


def damped_solve(load, order):
    pairs = order * order // 2 + order // 2
    entry = {}
    for i in range(order):
        for j in range(i + 1):
            entry[i, j] = load(cyclic_row(i, j, order))
        entry[i, i] = entry[i, i] + DAMP
    remain = [load(pairs + i) for i in range(order)]
    inverse = []
    for k in range(order):
        inverse.append(1.0 / entry[k, k])
        for i in range(k + 1, order):
            scaled = entry[i, k] * inverse[k]
            for j in range(k + 1, i + 1):
                entry[i, j] = entry[i, j] - scaled * entry[j, k]
            remain[i] = remain[i] - scaled * remain[k]
    solved = [None] * order
    for k in reversed(range(order)):
        solved[k] = remain[k] * inverse[k]
        for j in range(k):
            remain[j] = remain[j] - entry[k, j] * solved[k]
    return solved


def as_column(row):
    return jnp.broadcast_to(row, (LANES, row.shape[1])).T


def detrend_kernel(
    obj_n, ep_n, order, lc_ref, valid_ref, pixel_ref, sigma_ref, modes_ref,
    jitter_ref, freq_ref, resid_ref, power_ref, basis_s, times_s,
    blk, halo_send, halo, first, lens, mens, sres, coef_s, modes_s, gram_s, tall_s,
    part_send, part_recv, solved_s, mode_send, mode_recv, final_s,
    near_sem, forward_sem, blk_sem, halo_out, halo_forward, halo_sem, first_sem,
    part_sem, mode_sem,
):
    me_o, me_e = lax.axis_index("obj"), lax.axis_index("ep")
    rows, cols = lc_ref.shape
    planes = obj_n // GROUP
    q, r = me_o // GROUP, lax.rem(me_o, GROUP)
    p, core = r // 2, lax.rem(r, 2)
    share = rows // ep_n
    epochs = cols * ep_n
    half = cols // 2
    tiles = GROUP + 1
    slab = cols // GROUP
    pairs = order * order // 2 + order // 2
    depth = pairs + order
    quarter = part_send.shape[1]
    pixels = 4 * obj_n

    def device(plane, chip, side, ep):
        return {"obj": plane * GROUP + chip * 2 + side, "ep": ep}

    def remote(src, dst, send, recv, where):
        return pltpu.make_async_remote_copy(
            src_ref=src, dst_ref=dst, send_sem=send, recv_sem=recv,
            device_id=where, device_id_type=MESH,
        )

    chips = [(dp, de) for dp in range(GROUP // 2) for de in range(ep_n)]
    inner = [(dr, de) for dr in range(GROUP) for de in range(ep_n) if (dr, de) != (0, 0)]

    def turned(dp, de):
        return lax.rem(p + dp, GROUP // 2), lax.rem(me_e + de, ep_n)

    has_prev, has_next = q > 0, q < planes - 1
    barrier = pltpu.get_barrier_semaphore()

    def greet(where):
        pl.semaphore_signal(barrier, inc=1, device_id=where, device_id_type=MESH)

    for dr, de in inner:
        greet({"obj": q * GROUP + lax.rem(r + dr, GROUP), "ep": lax.rem(me_e + de, ep_n)})
    for k in range(1, planes):
        greet({"obj": lax.rem(me_o + k * GROUP, obj_n), "ep": me_e})
    for there, exists in ((q - 1, has_prev), (q + 1, has_next)):
        @pl.when(exists)
        def _():
            for dp, de in chips:
                chip, ep = turned(dp, de)
                greet(device(there, chip, core, ep))

    width = basis_s.shape[3]
    times_s[...] = as_column(
        lax.broadcasted_iota(jnp.int32, (1, epochs), 1).astype(F32) + jitter_ref[...]
    )

    def fill_basis(block):
        begin = pl.multiple_of(block * width, width)
        freqs = (freq_ref[:, pl.ds(begin, width)] + 1).astype(F32) / (4.0 * epochs)

        def strip(step, carry):
            at = pl.ds(pl.multiple_of(step * STRIP, STRIP), STRIP)
            times = jnp.concatenate([times_s[at, :]] * (width // LANES), axis=1)
            for kind, values in enumerate(basis_of(times * freqs)):
                basis_s[block, kind, at, :] = values.astype(BF16)
            return carry

        lax.fori_loop(0, epochs // STRIP, strip, 0)

    blocks = basis_s.shape[0]
    lane = lax.broadcasted_iota(jnp.int32, (1, rows), 1)
    low_half = lane < rows // 2
    own = jnp.where(valid_ref[...] != 0, lc_ref[...], ABSENT).T
    marks = jnp.concatenate(
        [pixel_ref[...].astype(F32), sigma_ref[...], jnp.zeros((SUB - 2, rows), F32)], axis=0
    )
    mine = blk.at[me_e, r]
    blk[me_e, r, :cols] = own
    blk[me_e, r, cols:] = marks
    upper, lower = own[:half], own[half:]
    is_last = r == GROUP - 1
    turned_upper, turned_lower = pltpu.roll(upper, rows // 2, 1), pltpu.roll(lower, rows // 2, 1)
    halo_send[:half] = jnp.where(
        is_last,
        jnp.where(low_half, turned_upper, lower),
        jnp.where(low_half, upper, turned_lower),
    )
    halo_send[half:] = jnp.where(is_last, pltpu.roll(marks, rows // 2, 1), marks)
    first[me_e] = modes_ref[...]
    missing = jnp.concatenate(
        [jnp.full((half, rows), ABSENT, F32), jnp.full((1, rows), -1.0, F32),
         jnp.ones((SUB - 1, rows), F32)], axis=0,
    )
    for kind, exists in ((0, has_prev), (1, has_next)):
        @pl.when(jnp.logical_not(exists))
        def _():
            for ep in range(ep_n):
                halo[kind, ep] = missing

    def early(block, carry):
        fill_basis(block)
        return carry

    lax.fori_loop(0, blocks // 2, early, 0)
    pl.semaphore_wait(
        barrier,
        len(inner) + planes - 1 + len(chips) * (has_prev.astype(jnp.int32) + has_next.astype(jnp.int32)),
    )

    partner = device(q, p, 1 - core, me_e)
    near = []
    for n, (dp, de) in enumerate(chips):
        if (dp, de) != (0, 0):
            chip, ep = turned(dp, de)
            near.append(remote(mine, mine, near_sem.at[n], blk_sem.at[me_e, r], device(q, chip, core, ep)))
            near[-1].start()
    forwards = [remote(mine, mine, forward_sem.at[0], blk_sem.at[me_e, r], partner)]
    forwards[0].start()
    greetings = []
    for de in range(1, ep_n):
        greetings.append(remote(
            modes_ref, first.at[me_e], first_sem.at[0, de], first_sem.at[1, me_e],
            device(q, p, core, lax.rem(me_e + de, ep_n)),
        ))
        greetings[-1].start()

    halo_kinds = (
        (0, q + 1, jnp.logical_and(r == GROUP - 1, has_next), has_prev, core == 1),
        (1, q - 1, jnp.logical_and(r == 0, has_prev), has_next, core == 0),
    )

    def halo_copies(kind, there):
        made = []
        for n, (dp, de) in enumerate(chips):
            chip, ep = turned(dp, de)
            made.append(remote(
                halo_send, halo.at[kind, me_e], halo_out.at[n], halo_sem.at[kind, me_e],
                device(there, chip, core, ep),
            ))
        return made

    for kind, there, sends, _, _ in halo_kinds:
        @pl.when(sends)
        def _():
            for copy in halo_copies(kind, there):
                copy.start()

    def halo_step(kind, ep):
        slot = halo.at[kind, ep]
        return remote(slot, slot, halo_forward.at[ep], halo_sem.at[kind, ep], partner)

    for n, (dp, de) in enumerate(chips):
        if (dp, de) != (0, 0):
            chip, ep = turned(dp, de)
            slot = blk.at[ep, chip * 2 + core]
            forward = remote(slot, slot, forward_sem.at[n], blk_sem.at[ep, chip * 2 + core], partner)
            forward.wait_recv()
            forward.start()
            forwards.append(forward)
    for kind, _, _, arrives, passes in halo_kinds:
        @pl.when(jnp.logical_and(arrives, passes))
        def _():
            for ep in range(ep_n):
                step = halo_step(kind, ep)
                step.wait_recv()
                step.start()

    def late(block, carry):
        fill_basis(block)
        return carry

    lax.fori_loop(blocks // 2, blocks, late, 0)
    for dp, de in chips:
        chip, ep = turned(dp, de)
        slot = blk.at[ep, chip * 2 + 1 - core]
        remote(slot, slot, forward_sem.at[0], blk_sem.at[ep, chip * 2 + 1 - core], partner).wait_recv()
    for kind, _, _, arrives, passes in halo_kinds:
        @pl.when(jnp.logical_and(arrives, jnp.logical_not(passes)))
        def _():
            for ep in range(ep_n):
                halo_step(kind, ep).wait_recv()
    for de in range(1, ep_n):
        ep = lax.rem(me_e + de, ep_n)
        remote(modes_ref, first.at[ep], first_sem.at[0, de], first_sem.at[1, ep], partner).wait_recv()
    for copy in near + forwards + greetings:
        copy.wait_send()
    for kind, there, sends, _, _ in halo_kinds:
        @pl.when(sends)
        def _():
            for copy in halo_copies(kind, there):
                copy.wait_send()
    for kind, _, _, arrives, passes in halo_kinds:
        @pl.when(jnp.logical_and(arrives, passes))
        def _():
            for ep in range(ep_n):
                halo_step(kind, ep).wait_send()

    pixel_level = lax.broadcasted_iota(jnp.int32, (pixels, rows), 0).astype(F32)
    marked = [blk[0, t, cols:] for t in range(GROUP)]
    before, after = halo[0, 0, half:], pltpu.roll(halo[1, 0, half:], rows // 2, 1)
    marked.append(jnp.where(low_half, before, after))
    pixel_row = [m[0:1] for m in marked]
    sigma_row = [m[1:2] for m in marked]
    totals = []
    for t in range(tiles):
        total = jnp.zeros((1, rows), F32)
        for ep in range(ep_n):
            if t < GROUP:
                value = blk[ep, t, :cols]
            else:
                prev, follow = halo[0, ep, :half], halo[1, ep, :half]
                value = jnp.concatenate([
                    jnp.where(low_half, prev, pltpu.roll(follow, rows // 2, 1)),
                    jnp.where(low_half, pltpu.roll(prev, rows // 2, 1), follow),
                ], axis=0)
            seen = value < 0.5 * ABSENT
            scale = jnp.where(seen, sigma_row[t], 0.0)
            at = slice(ep * cols, (ep + 1) * cols)
            mens[t, at] = scale
            lens[t, at] = value * scale
            total = total + jnp.sum(seen.astype(F32), axis=0, keepdims=True)
        totals.append(total)

    def by_pixel(tile_rows, tile_pixels):
        gathered = jnp.zeros((pixels, rows), F32)
        for row, where in zip(tile_rows, tile_pixels):
            gathered = gathered + jnp.where(where == pixel_level, row, 0.0)
        return jnp.sum(gathered, axis=1, keepdims=True)

    inverse_count = 1.0 / jnp.maximum(by_pixel(totals, pixel_row), 1.0)

    def limits(squares, tile_pixels, wanted):
        sums = by_pixel(squares, tile_pixels)
        spread = HUBER * jnp.sqrt(sums * inverse_count + 1e-06)
        return [
            jnp.maximum(
                jnp.sum(jnp.where(where == pixel_level, spread, 0.0), axis=0, keepdims=True), 1e-3
            )
            for where in wanted
        ]

    def modes_factor():
        high, low = halves(modes_s[...])
        stacked = jnp.concatenate([high, high, low], axis=0).astype(F32)
        stacked = jnp.concatenate(
            [stacked, jnp.zeros((LANES - 3 * order, epochs), F32)], axis=0
        )
        tall_s[...] = stacked.T.astype(BF16)

    def fitted(coef):
        high, low = halves(coef)
        wide = jnp.concatenate(
            [high, low, high, jnp.zeros((LANES - 3 * order, coef.shape[1]), BF16)], axis=0
        )
        return jnp.dot(tall_s[...], wide, preferred_element_type=F32)

    def scaled_residuals():
        squares = []
        for t in range(tiles):
            left = lens[t] - mens[t] * fitted(coef_s[t * order : (t + 1) * order])
            sres[t] = left
            squares.append(jnp.sum(left * left, axis=0, keepdims=True))
        return squares

    def reach(left, limit, sigma):
        return (sigma * limit) / jnp.maximum(jnp.abs(left), limit)

    coef_s[...] = jnp.zeros_like(coef_s)
    for ep in range(ep_n):
        modes_s[:, ep * cols : (ep + 1) * cols] = first[ep]
    modes_factor()

    def iteration(it, carry):
        limit = limits(scaled_residuals(), pixel_row, pixel_row)
        modes = modes_s[...]
        outer_high, outer_low = halves(cyclic_outer(modes))
        modes_high, modes_low = halves(modes)
        for t in range(tiles):
            factor = reach(sres[t], limit[t], sigma_row[t])
            weight = (mens[t] * factor).astype(BF16)
            value_high, value_low = halves(lens[t] * factor)
            gram = jnp.dot(outer_high, weight, preferred_element_type=F32)
            gram = gram + jnp.dot(outer_low, weight, preferred_element_type=F32)
            target = jnp.dot(modes_high, value_high, preferred_element_type=F32)
            target = target + jnp.dot(modes_low, value_high, preferred_element_type=F32)
            target = target + jnp.dot(modes_high, value_low, preferred_element_type=F32)
            gram_s[t * depth : t * depth + pairs] = gram
            gram_s[t * depth + pairs : (t + 1) * depth] = target
        solved = damped_solve(lambda row: gram_s[pl.ds(row, tiles, stride=depth), :], order)
        for k in range(order):
            coef_s[pl.ds(k, tiles, stride=order), :] = solved[k]

        limit = limits(scaled_residuals(), pixel_row, pixel_row[:GROUP])
        at = pl.ds(pl.multiple_of(me_e * cols + r * slab, slab), slab)
        weights, value_highs, value_lows, outers, coefs = [], [], [], [], []
        for t in range(GROUP):
            factor = reach(sres[t, at], limit[t], sigma_row[t])
            weights.append((mens[t, at] * factor).astype(BF16))
            value_high, value_low = halves(lens[t, at] * factor)
            value_highs.append(value_high)
            value_lows.append(value_low)
            coef = coef_s[t * order : (t + 1) * order]
            outers.append(halves(cyclic_outer(coef)))
            coefs.append(halves(coef))

        def copied(parts):
            return jnp.concatenate([jnp.concatenate(parts, axis=1)] * GROUP, axis=0)

        def across(left, right):
            return lax.dot_general(
                left, right, (((1,), (1,)), ((), ())), preferred_element_type=F32
            )

        weight, value_high, value_low = copied(weights), copied(value_highs), copied(value_lows)
        outer_high = jnp.concatenate([pair[0] for pair in outers], axis=1)
        outer_low = jnp.concatenate([pair[1] for pair in outers], axis=1)
        coef_high = jnp.concatenate([pair[0] for pair in coefs], axis=1)
        coef_low = jnp.concatenate([pair[1] for pair in coefs], axis=1)
        gram = across(outer_high, weight) + across(outer_low, weight)
        target = across(coef_high, value_high) + across(coef_low, value_high)
        target = target + across(coef_high, value_low)
        whole = jnp.concatenate(
            [gram, target, jnp.zeros((GROUP * quarter - depth, rows), F32)], axis=0
        )
        packed = whole[:quarter]
        for k in range(1, GROUP):
            packed = jnp.where(lane >= k * slab, whole[k * quarter : (k + 1) * quarter], packed)
        part_send[it] = packed
        copies = []
        for k in range(1, planes):
            copies.append(remote(
                part_send.at[it], part_recv.at[it, k - 1],
                part_sem.at[0, it, k - 1], part_sem.at[1, it, k - 1],
                {"obj": lax.rem(me_o + k * GROUP, obj_n), "ep": me_e},
            ))
            copies[-1].start()
        for k in range(1, planes):
            copies[k - 1].wait()
            packed = packed + part_recv[it, k - 1]
        gram_s[:quarter] = packed
        for k in range(1, GROUP):
            gram_s[k * quarter : (k + 1) * quarter] = pltpu.roll(packed, rows - k * slab, 1)
        solved = damped_solve(lambda row: gram_s[row : row + 1, :], order)
        for k in range(order):
            solved_s[k : k + 1] = solved[k]
        fresh = pltpu.roll(solved_s[...], r * slab, 1)
        mode_send[it] = fresh
        mode_recv[it, me_e, r] = fresh
        copies = []
        for n, (dr, de) in enumerate(inner):
            copies.append(remote(
                mode_send.at[it], mode_recv.at[it, me_e, r],
                mode_sem.at[0, it, n], mode_sem.at[1, it, n],
                {"obj": q * GROUP + lax.rem(r + dr, GROUP), "ep": lax.rem(me_e + de, ep_n)},
            ))
            copies[-1].start()
        for copy in copies:
            copy.wait()
        for ep in range(ep_n):
            joined = mode_recv[it, ep, 0]
            for k in range(1, GROUP):
                joined = jnp.where(lane >= k * slab, mode_recv[it, ep, k], joined)
            modes_s[:, ep * cols : (ep + 1) * cols] = joined
        modes_factor()
        return carry

    lax.fori_loop(0, ITERS, iteration, 0)
    own_coef = coef_s[pl.ds(pl.multiple_of(r * order, order), order), :]
    beside = jnp.where(
        me_e < ep_n // 2, jnp.where(r == 0, GROUP, r - 1), r + 1
    )
    side_coef = coef_s[pl.ds(pl.multiple_of(beside * order, order), order), :]
    both_pixels, squares = [], []
    lefts = []
    for t, coef in ((r, own_coef), (beside, side_coef)):
        left = lens[t] - mens[t] * fitted(coef)
        lefts.append(left)
        squares.append(jnp.sum(left * left, axis=0, keepdims=True))
    for t, name in ((r, 0), (beside, 1)):
        chosen = pixel_row[0]
        for k in range(1, tiles):
            chosen = jnp.where(t == k, pixel_row[k], chosen)
        both_pixels.append(chosen)
    own_sigma = sigma_ref[...]
    (limit,) = limits(squares, both_pixels, both_pixels[:1])
    factor = reach(lefts[0], limit, own_sigma)
    final_s[0] = (mens[r] * factor).T.astype(BF16)
    final_s[1] = (lefts[0] * factor).T.astype(BF16)
    own_modes = modes_s[:, pl.ds(pl.multiple_of(me_e * cols, cols), cols)]
    resid_ref[...] = lc_ref[...] - lax.dot_general(
        own_coef, own_modes, (((0,), (0,)), ((), ())),
        precision=HIGHEST, preferred_element_type=F32,
    )
    mine_at = pl.ds(pl.multiple_of(me_e * share, share), share)
    weights, values = final_s[0, mine_at, :], final_s[1, mine_at, :]
    both = jnp.concatenate([weights, values], axis=0)
    total = jnp.sum(weights.astype(F32), axis=1, keepdims=True)
    level = jnp.sum(values.astype(F32), axis=1, keepdims=True)

    def spectrum(block, carry):
        at = pl.ds(pl.multiple_of(block * width, width), width)
        power_ref[:, at] = powers(
            jnp.dot(both, basis_s[block, 0], preferred_element_type=F32),
            jnp.dot(both, basis_s[block, 1], preferred_element_type=F32),
            jnp.dot(weights, basis_s[block, 2], preferred_element_type=F32),
            jnp.dot(weights, basis_s[block, 3], preferred_element_type=F32),
            total,
            level,
        )
        return carry

    lax.fori_loop(0, blocks, spectrum, 0)


SIN_TERMS = [(-1.0) ** n / math.factorial(2 * n + 1) for n in range(7)]
COS_TERMS = [(-1.0) ** n / math.factorial(2 * n) for n in range(8)]


def series(square, terms):
    value = jnp.full_like(square, terms[-1])
    for term in terms[-2::-1]:
        value = value * square + term
    return value


def basis_of(cycles):
    cycles = cycles - jnp.floor(cycles)
    turn = jnp.where(cycles >= 0.5, cycles - 1.0, cycles)
    angle = (2.0 * math.pi) * (jnp.abs(turn) - 0.25)
    square = angle * angle
    cosine = -angle * series(square, SIN_TERMS)
    size = series(square, COS_TERMS)
    sine = jnp.where(turn < 0.0, -size, size)
    return cosine, sine, 2.0 * cosine * cosine - 1.0, 2.0 * sine * cosine


def powers(by_cos, by_sin, cosine_two, sine_two, total, level):
    count = cosine_two.shape[0]
    cosine, sine = by_cos[:count], by_sin[:count]
    inverse = 1.0 / total
    mean_level = level * inverse
    ycos = by_cos[count:] - mean_level * cosine
    ysin = by_sin[count:] - mean_level * sine
    cc_term = 0.5 * (total + cosine_two) - cosine * cosine * inverse + RIDGE * total
    ss_term = 0.5 * (total - cosine_two) - sine * sine * inverse + RIDGE * total
    cs_term = 0.5 * sine_two - cosine * sine * inverse
    determinant = cc_term * ss_term - cs_term * cs_term
    return (
        ss_term * ycos * ycos + cc_term * ysin * ysin - 2.0 * cs_term * ycos * ysin
    ) / determinant


def per_device(light_curves, valid, pixel, inv_sigma, modes_init, epoch_jitter, freq_index):
    obj_n = lax.axis_size("obj")
    ep_n = lax.axis_size("ep")
    order = modes_init.shape[1]
    rows, cols = light_curves.shape
    share = rows // ep_n
    epochs = epoch_jitter.shape[0]
    planes = obj_n // GROUP
    tiles = GROUP + 1
    half = cols // 2
    depth = order * order // 2 + order // 2 + order
    quarter = -(-depth // (GROUP * SUB)) * SUB
    chips = GROUP // 2 * ep_n
    inner = GROUP * ep_n - 1
    vmem = pl.BlockSpec(memory_space=pltpu.VMEM)
    sem = pltpu.SemaphoreType.DMA
    count = freq_index.shape[0]
    parts = 4 * ITERS
    return pl.pallas_call(
        functools.partial(detrend_kernel, obj_n, ep_n, order),
        out_shape=(
            jax.ShapeDtypeStruct((rows, cols), F32),
            jax.ShapeDtypeStruct((share, count), F32),
        ),
        in_specs=[vmem] * 7,
        out_specs=(vmem,) * 2,
        scratch_shapes=[
            pltpu.VMEM((parts, 4, epochs, count // parts), BF16),
            pltpu.VMEM((epochs, LANES), F32),
            pltpu.VMEM((ep_n, GROUP, cols + SUB, rows), F32),
            pltpu.VMEM((half + SUB, rows), F32),
            pltpu.VMEM((2, ep_n, half + SUB, rows), F32),
            pltpu.VMEM((ep_n, order, cols), F32),
            pltpu.VMEM((tiles, epochs, rows), F32),
            pltpu.VMEM((tiles, epochs, rows), F32),
            pltpu.VMEM((tiles, epochs, rows), F32),
            pltpu.VMEM((tiles * order, rows), F32),
            pltpu.VMEM((order, epochs), F32),
            pltpu.VMEM((tiles * depth, rows), F32),
            pltpu.VMEM((epochs, LANES), BF16),
            pltpu.VMEM((ITERS, quarter, rows), F32),
            pltpu.VMEM((ITERS, planes - 1, quarter, rows), F32),
            pltpu.VMEM((order, rows), F32),
            pltpu.VMEM((ITERS, order, rows), F32),
            pltpu.VMEM((ITERS, ep_n, GROUP, order, rows), F32),
            pltpu.VMEM((2, rows, epochs), BF16),
            sem((chips,)),
            sem((chips,)),
            sem((ep_n, GROUP)),
            sem((chips,)),
            sem((ep_n,)),
            sem((2, ep_n)),
            sem((2, ep_n)),
            sem((2, ITERS, planes - 1)),
            sem((2, ITERS, inner)),
        ],
        compiler_params=pltpu.CompilerParams(collective_id=0, has_side_effects=True),
    )(
        light_curves, valid, pixel[None], inv_sigma[None], modes_init.T,
        epoch_jitter[None], freq_index[None],
    )


def solution(mesh):
    in_specs = (P("obj", "ep"), P("obj", "ep"), P("obj"), P("obj"), P("ep", None), P(), P())
    out_specs = (P("obj", "ep"), P(("obj", "ep"), None))
    return jax.shard_map(
        per_device, mesh=mesh, in_specs=in_specs, out_specs=out_specs, check_vma=False
    )
```

```python
import functools
import math

import jax
import jax.numpy as jnp
from jax import lax
from jax.experimental import pallas as pl
from jax.experimental.pallas import tpu as pltpu
from jax.sharding import PartitionSpec as P

ITERS = 2


HUBER = 1.345
DAMP = 2.0
RIDGE = 0.05
HIGHEST = lax.Precision.HIGHEST
LANES = 128
SUB = 8
UNROLL = 2
ROOM = 24 << 20
GROUP = 4
ABSENT = 1e30
F32 = jnp.float32
BF16 = jnp.bfloat16
STRIP = 32
MESH = pl.DeviceIdType.MESH


def halves(values):
    high = values.astype(BF16)
    return high, (values - high.astype(F32)).astype(BF16)


def cyclic_outer(vectors):
    order = vectors.shape[0]
    parts = [vectors * vectors]
    for shift in range(1, order // 2 + 1):
        turned = jnp.concatenate([vectors[shift:], vectors[:shift]], axis=0)
        part = vectors * turned
        parts.append(part if shift < order // 2 else part[: order // 2])
    return jnp.concatenate(parts, axis=0)


def cyclic_row(i, j, order):
    ahead = (j - i) % order
    if ahead == order // 2:
        return ahead * order + min(i, j)
    return ahead * order + i if ahead < order // 2 else (order - ahead) * order + j


def damped_solve(load, order):
    pairs = order * order // 2 + order // 2
    entry = {}
    for i in range(order):
        for j in range(i + 1):
            entry[i, j] = load(cyclic_row(i, j, order))
        entry[i, i] = entry[i, i] + DAMP
    remain = [load(pairs + i) for i in range(order)]
    inverse = []
    for k in range(order):
        inverse.append(1.0 / entry[k, k])
        for i in range(k + 1, order):
            scaled = entry[i, k] * inverse[k]
            for j in range(k + 1, i + 1):
                entry[i, j] = entry[i, j] - scaled * entry[j, k]
            remain[i] = remain[i] - scaled * remain[k]
    solved = [None] * order
    for k in reversed(range(order)):
        solved[k] = remain[k] * inverse[k]
        for j in range(k):
            remain[j] = remain[j] - entry[k, j] * solved[k]
    return solved


def as_column(row):
    return jnp.broadcast_to(row, (LANES, row.shape[1])).T


def detrend_kernel(
    obj_n, ep_n, order, lc_hbm, valid_hbm, pixel_hbm, sigma_hbm, modes_hbm,
    jitter_hbm, freq_hbm, resid_ref, ready_ref, basis_s,
    lc_ref, valid_ref, pixel_ref, sigma_ref, jitter_ref, freq_ref, times_s,
    blk, halo_send, halo, first, lens, mens, sres, coef_s, modes_s, gram_s, tall_s,
    part_send, part_recv, solved_s, mode_send, mode_recv, final_s,
    load_sem, near_sem, forward_sem, blk_sem, halo_out, halo_forward, halo_sem, first_sem,
    part_sem, mode_sem,
):
    me_o, me_e = lax.axis_index("obj"), lax.axis_index("ep")
    rows, cols = lc_ref.shape
    planes = obj_n // GROUP
    q, r = me_o // GROUP, lax.rem(me_o, GROUP)
    p, core = r // 2, lax.rem(r, 2)
    share = rows // ep_n
    epochs = cols * ep_n
    half = cols // 2
    tiles = GROUP + 1
    slab = cols // GROUP
    pairs = order * order // 2 + order // 2
    depth = pairs + order
    quarter = part_send.shape[1]
    pixels = 4 * obj_n

    def device(plane, chip, side, ep):
        return {"obj": plane * GROUP + chip * 2 + side, "ep": ep}

    def remote(src, dst, send, recv, where):
        return pltpu.make_async_remote_copy(
            src_ref=src, dst_ref=dst, send_sem=send, recv_sem=recv,
            device_id=where, device_id_type=MESH,
        )

    chips = sorted(
        ((dp, de) for dp in range(GROUP // 2) for de in range(ep_n)),
        key=lambda step: (min(step[0], 1) + min(step[1], 1)) % 3 * -1,
    )
    inner = [(dr, de) for dr in range(GROUP) for de in range(ep_n) if (dr, de) != (0, 0)]

    def turned(dp, de):
        return lax.rem(p + dp, GROUP // 2), lax.rem(me_e + de, ep_n)

    has_prev, has_next = q > 0, q < planes - 1
    barrier = pltpu.get_barrier_semaphore()

    def greet(where):
        pl.semaphore_signal(barrier, inc=1, device_id=where, device_id_type=MESH)

    for dr, de in inner:
        greet({"obj": q * GROUP + lax.rem(r + dr, GROUP), "ep": lax.rem(me_e + de, ep_n)})
    for k in range(1, planes):
        greet({"obj": lax.rem(me_o + k * GROUP, obj_n), "ep": me_e})
    for there, exists in ((q - 1, has_prev), (q + 1, has_next)):
        @pl.when(exists)
        def _():
            for dp, de in chips:
                chip, ep = turned(dp, de)
                greet(device(there, chip, core, ep))

    loads = [
        pltpu.make_async_copy(source, target, load_sem.at[n])
        for n, (source, target) in enumerate((
            (lc_hbm, lc_ref), (valid_hbm, valid_ref), (pixel_hbm, pixel_ref),
            (sigma_hbm, sigma_ref), (modes_hbm, first.at[me_e]), (jitter_hbm, jitter_ref),
            (freq_hbm, freq_ref),
        ))
    ]
    for load in loads:
        load.start()
    for load in loads:
        load.wait()

    width = basis_s.shape[3]
    times_s[...] = as_column(
        lax.broadcasted_iota(jnp.int32, (1, epochs), 1).astype(F32) + jitter_ref[...]
    )

    def fill_basis(block):
        begin = pl.multiple_of(block * width, width)
        freqs = (freq_ref[:, pl.ds(begin, width)] + 1).astype(F32) / (4.0 * epochs)

        def strip(step, carry):
            at = pl.ds(pl.multiple_of(step * STRIP, STRIP), STRIP)
            times = jnp.concatenate([times_s[at, :]] * (width // LANES), axis=1)
            for kind, values in enumerate(basis_of(times * freqs)):
                basis_s[block, kind, at, :] = values.astype(BF16)
            return carry

        lax.fori_loop(0, epochs // STRIP, strip, 0)

    blocks = basis_s.shape[0]
    lane = lax.broadcasted_iota(jnp.int32, (1, rows), 1)
    low_half = lane < rows // 2
    own = jnp.where(valid_ref[...] != 0, lc_ref[...], ABSENT).T
    marks = jnp.concatenate(
        [pixel_ref[...].astype(F32), sigma_ref[...], jnp.zeros((SUB - 2, rows), F32)], axis=0
    )
    mine = blk.at[me_e, r]
    blk[me_e, r, :cols] = own
    blk[me_e, r, cols:] = marks
    upper, lower = own[:half], own[half:]
    is_last = r == GROUP - 1
    turned_upper, turned_lower = pltpu.roll(upper, rows // 2, 1), pltpu.roll(lower, rows // 2, 1)
    halo_send[:half] = jnp.where(
        is_last,
        jnp.where(low_half, turned_upper, lower),
        jnp.where(low_half, upper, turned_lower),
    )
    halo_send[half:] = jnp.where(is_last, pltpu.roll(marks, rows // 2, 1), marks)
    missing = jnp.concatenate(
        [jnp.full((half, rows), ABSENT, F32), jnp.full((1, rows), -1.0, F32),
         jnp.ones((SUB - 1, rows), F32)], axis=0,
    )
    for kind, exists in ((0, has_prev), (1, has_next)):
        @pl.when(jnp.logical_not(exists))
        def _():
            for ep in range(ep_n):
                halo[kind, ep] = missing

    def early(block, carry):
        fill_basis(block)
        return carry

    lax.fori_loop(0, blocks // 2, early, 0)
    pl.semaphore_wait(
        barrier,
        len(inner) + planes - 1 + len(chips) * (has_prev.astype(jnp.int32) + has_next.astype(jnp.int32)),
    )

    partner = device(q, p, 1 - core, me_e)
    near = []
    for n, (dp, de) in enumerate(chips):
        if (dp, de) != (0, 0):
            chip, ep = turned(dp, de)
            near.append(remote(mine, mine, near_sem.at[n], blk_sem.at[me_e, r], device(q, chip, core, ep)))
            near[-1].start()
    forwards = [remote(mine, mine, forward_sem.at[0], blk_sem.at[me_e, r], partner)]
    forwards[0].start()
    greetings = []
    for de in range(1, ep_n):
        greetings.append(remote(
            first.at[me_e], first.at[me_e], first_sem.at[0, de], first_sem.at[1, me_e],
            device(q, p, core, lax.rem(me_e + de, ep_n)),
        ))
        greetings[-1].start()

    halo_kinds = (
        (0, q + 1, jnp.logical_and(r == GROUP - 1, has_next), has_prev, core == 1),
        (1, q - 1, jnp.logical_and(r == 0, has_prev), has_next, core == 0),
    )

    def halo_copies(kind, there):
        made = []
        for n, (dp, de) in enumerate(chips):
            chip, ep = turned(dp, de)
            made.append(remote(
                halo_send, halo.at[kind, me_e], halo_out.at[n], halo_sem.at[kind, me_e],
                device(there, chip, core, ep),
            ))
        return made

    for kind, there, sends, _, _ in halo_kinds:
        @pl.when(sends)
        def _():
            for copy in halo_copies(kind, there):
                copy.start()

    def halo_step(kind, ep):
        slot = halo.at[kind, ep]
        return remote(slot, slot, halo_forward.at[ep], halo_sem.at[kind, ep], partner)

    for n, (dp, de) in enumerate(chips):
        if (dp, de) != (0, 0):
            chip, ep = turned(dp, de)
            slot = blk.at[ep, chip * 2 + core]
            forward = remote(slot, slot, forward_sem.at[n], blk_sem.at[ep, chip * 2 + core], partner)
            forward.wait_recv()
            forward.start()
            forwards.append(forward)
    for kind, _, _, arrives, passes in halo_kinds:
        @pl.when(jnp.logical_and(arrives, passes))
        def _():
            for ep in range(ep_n):
                step = halo_step(kind, ep)
                step.wait_recv()
                step.start()

    def late(block, carry):
        fill_basis(block)
        return carry

    lax.fori_loop(blocks // 2, blocks, late, 0)
    for dp, de in chips:
        chip, ep = turned(dp, de)
        slot = blk.at[ep, chip * 2 + 1 - core]
        remote(slot, slot, forward_sem.at[0], blk_sem.at[ep, chip * 2 + 1 - core], partner).wait_recv()
    for kind, _, _, arrives, passes in halo_kinds:
        @pl.when(jnp.logical_and(arrives, jnp.logical_not(passes)))
        def _():
            for ep in range(ep_n):
                halo_step(kind, ep).wait_recv()
    for de in range(1, ep_n):
        ep = lax.rem(me_e + de, ep_n)
        remote(first.at[ep], first.at[ep], first_sem.at[0, de], first_sem.at[1, ep], partner).wait_recv()
    for copy in near + forwards + greetings:
        copy.wait_send()
    for kind, there, sends, _, _ in halo_kinds:
        @pl.when(sends)
        def _():
            for copy in halo_copies(kind, there):
                copy.wait_send()
    for kind, _, _, arrives, passes in halo_kinds:
        @pl.when(jnp.logical_and(arrives, passes))
        def _():
            for ep in range(ep_n):
                halo_step(kind, ep).wait_send()

    pixel_level = lax.broadcasted_iota(jnp.int32, (pixels, rows), 0).astype(F32)
    marked = [blk[0, t, cols:] for t in range(GROUP)]
    before, after = halo[0, 0, half:], pltpu.roll(halo[1, 0, half:], rows // 2, 1)
    marked.append(jnp.where(low_half, before, after))
    pixel_row = [m[0:1] for m in marked]
    sigma_row = [m[1:2] for m in marked]
    totals = []
    for t in range(tiles):
        total = jnp.zeros((1, rows), F32)
        for ep in range(ep_n):
            if t < GROUP:
                value = blk[ep, t, :cols]
            else:
                prev, follow = halo[0, ep, :half], halo[1, ep, :half]
                value = jnp.concatenate([
                    jnp.where(low_half, prev, pltpu.roll(follow, rows // 2, 1)),
                    jnp.where(low_half, pltpu.roll(prev, rows // 2, 1), follow),
                ], axis=0)
            seen = value < 0.5 * ABSENT
            scale = jnp.where(seen, sigma_row[t], 0.0)
            at = slice(ep * cols, (ep + 1) * cols)
            mens[t, at] = scale
            lens[t, at] = value * scale
            total = total + jnp.sum(seen.astype(F32), axis=0, keepdims=True)
        totals.append(total)

    def by_pixel(tile_rows, tile_pixels):
        gathered = jnp.zeros((pixels, rows), F32)
        for row, where in zip(tile_rows, tile_pixels):
            gathered = gathered + jnp.where(where == pixel_level, row, 0.0)
        return jnp.sum(gathered, axis=1, keepdims=True)

    inverse_count = 1.0 / jnp.maximum(by_pixel(totals, pixel_row), 1.0)

    def limits(squares, tile_pixels, wanted):
        sums = by_pixel(squares, tile_pixels)
        spread = HUBER * jnp.sqrt(sums * inverse_count + 1e-06)
        return [
            jnp.maximum(
                jnp.sum(jnp.where(where == pixel_level, spread, 0.0), axis=0, keepdims=True), 1e-3
            )
            for where in wanted
        ]

    def modes_factor():
        high, low = halves(modes_s[...])
        stacked = jnp.concatenate([high, high, low], axis=0).astype(F32)
        stacked = jnp.concatenate(
            [stacked, jnp.zeros((LANES - 3 * order, epochs), F32)], axis=0
        )
        tall_s[...] = stacked.T.astype(BF16)

    def fitted(coef):
        high, low = halves(coef)
        wide = jnp.concatenate(
            [high, low, high, jnp.zeros((LANES - 3 * order, coef.shape[1]), BF16)], axis=0
        )
        return jnp.dot(tall_s[...], wide, preferred_element_type=F32)

    def scaled_residuals():
        squares = []
        for t in range(tiles):
            left = lens[t] - mens[t] * fitted(coef_s[t * order : (t + 1) * order])
            sres[t] = left
            squares.append(jnp.sum(left * left, axis=0, keepdims=True))
        return squares

    def reach(left, limit, sigma):
        return (sigma * limit) / jnp.maximum(jnp.abs(left), limit)

    coef_s[...] = jnp.zeros_like(coef_s)
    for ep in range(ep_n):
        modes_s[:, ep * cols : (ep + 1) * cols] = first[ep]
    modes_factor()

    def iteration(it, carry):
        limit = limits(scaled_residuals(), pixel_row, pixel_row)
        modes = modes_s[...]
        outer_high, outer_low = halves(cyclic_outer(modes))
        modes_high, modes_low = halves(modes)
        for t in range(tiles):
            factor = reach(sres[t], limit[t], sigma_row[t])
            weight, weight_low = halves(mens[t] * factor)
            value_high, value_low = halves(lens[t] * factor)
            gram = jnp.dot(outer_high, weight, preferred_element_type=F32)
            gram = gram + jnp.dot(outer_low, weight, preferred_element_type=F32)
            gram = gram + jnp.dot(outer_high, weight_low, preferred_element_type=F32)
            target = jnp.dot(modes_high, value_high, preferred_element_type=F32)
            target = target + jnp.dot(modes_low, value_high, preferred_element_type=F32)
            target = target + jnp.dot(modes_high, value_low, preferred_element_type=F32)
            gram_s[t * depth : t * depth + pairs] = gram
            gram_s[t * depth + pairs : (t + 1) * depth] = target
        solved = damped_solve(lambda row: gram_s[pl.ds(row, tiles, stride=depth), :], order)
        for k in range(order):
            coef_s[pl.ds(k, tiles, stride=order), :] = solved[k]

        limit = limits(scaled_residuals(), pixel_row, pixel_row[:GROUP])
        at = pl.ds(pl.multiple_of(me_e * cols + r * slab, slab), slab)
        weights, weight_lows, value_highs, value_lows, outers, coefs = [], [], [], [], [], []
        for t in range(GROUP):
            factor = reach(sres[t, at], limit[t], sigma_row[t])
            weight, weight_low = halves(mens[t, at] * factor)
            weights.append(weight)
            weight_lows.append(weight_low)
            value_high, value_low = halves(lens[t, at] * factor)
            value_highs.append(value_high)
            value_lows.append(value_low)
            coef = coef_s[t * order : (t + 1) * order]
            outers.append(halves(cyclic_outer(coef)))
            coefs.append(halves(coef))

        def copied(parts):
            return jnp.concatenate([jnp.concatenate(parts, axis=1)] * GROUP, axis=0)

        def across(left, right):
            return lax.dot_general(
                left, right, (((1,), (1,)), ((), ())), preferred_element_type=F32
            )

        weight, weight_low = copied(weights), copied(weight_lows)
        value_high, value_low = copied(value_highs), copied(value_lows)
        outer_high = jnp.concatenate([pair[0] for pair in outers], axis=1)
        outer_low = jnp.concatenate([pair[1] for pair in outers], axis=1)
        coef_high = jnp.concatenate([pair[0] for pair in coefs], axis=1)
        coef_low = jnp.concatenate([pair[1] for pair in coefs], axis=1)
        gram = across(outer_high, weight) + across(outer_low, weight)
        gram = gram + across(outer_high, weight_low)
        target = across(coef_high, value_high) + across(coef_low, value_high)
        target = target + across(coef_high, value_low)
        whole = jnp.concatenate(
            [gram, target, jnp.zeros((GROUP * quarter - depth, rows), F32)], axis=0
        )
        packed = whole[:quarter]
        for k in range(1, GROUP):
            packed = jnp.where(lane >= k * slab, whole[k * quarter : (k + 1) * quarter], packed)
        part_send[it] = packed
        copies = []
        for k in range(1, planes):
            copies.append(remote(
                part_send.at[it], part_recv.at[it, k - 1],
                part_sem.at[0, it, k - 1], part_sem.at[1, it, k - 1],
                {"obj": lax.rem(me_o + k * GROUP, obj_n), "ep": me_e},
            ))
            copies[-1].start()
        for k in range(1, planes):
            copies[k - 1].wait()
            packed = packed + part_recv[it, k - 1]
        gram_s[:quarter] = packed
        for k in range(1, GROUP):
            gram_s[k * quarter : (k + 1) * quarter] = pltpu.roll(packed, rows - k * slab, 1)
        solved = damped_solve(lambda row: gram_s[row : row + 1, :], order)
        for k in range(order):
            solved_s[k : k + 1] = solved[k]
        fresh = pltpu.roll(solved_s[...], r * slab, 1)
        mode_send[it] = fresh
        mode_recv[it, me_e, r] = fresh
        copies = []
        for n, (dr, de) in enumerate(inner):
            copies.append(remote(
                mode_send.at[it], mode_recv.at[it, me_e, r],
                mode_sem.at[0, it, n], mode_sem.at[1, it, n],
                {"obj": q * GROUP + lax.rem(r + dr, GROUP), "ep": lax.rem(me_e + de, ep_n)},
            ))
            copies[-1].start()
        for copy in copies:
            copy.wait()
        for ep in range(ep_n):
            joined = mode_recv[it, ep, 0]
            for k in range(1, GROUP):
                joined = jnp.where(lane >= k * slab, mode_recv[it, ep, k], joined)
            modes_s[:, ep * cols : (ep + 1) * cols] = joined
        modes_factor()
        return carry

    lax.fori_loop(0, ITERS, iteration, 0)
    own_coef = coef_s[pl.ds(pl.multiple_of(r * order, order), order), :]
    beside = jnp.where(
        me_e < ep_n // 2, jnp.where(r == 0, GROUP, r - 1), r + 1
    )
    side_coef = coef_s[pl.ds(pl.multiple_of(beside * order, order), order), :]
    both_pixels, squares = [], []
    lefts = []
    for t, coef in ((r, own_coef), (beside, side_coef)):
        left = lens[t] - mens[t] * fitted(coef)
        lefts.append(left)
        squares.append(jnp.sum(left * left, axis=0, keepdims=True))
    for t, name in ((r, 0), (beside, 1)):
        chosen = pixel_row[0]
        for k in range(1, tiles):
            chosen = jnp.where(t == k, pixel_row[k], chosen)
        both_pixels.append(chosen)
    own_sigma = sigma_ref[...]
    (limit,) = limits(squares, both_pixels, both_pixels[:1])
    factor = reach(lefts[0], limit, own_sigma)
    final_s[0] = (mens[r] * factor).T.astype(BF16)
    final_s[1] = (lefts[0] * factor).T.astype(BF16)
    own_modes = modes_s[:, pl.ds(pl.multiple_of(me_e * cols, cols), cols)]
    resid_ref[...] = lc_ref[...] - lax.dot_general(
        own_coef, own_modes, (((0,), (0,)), ((), ())),
        precision=HIGHEST, preferred_element_type=F32,
    )
    mine_at = pl.ds(pl.multiple_of(me_e * share, share), share)
    ready_ref[...] = final_s[:, mine_at, :]


def spectrum_kernel(left_ref, ready_ref, basis_ref, resid_hbm, power_hbm, power_s, sems):
    weights, values = ready_ref[0], ready_ref[1]
    blocks, width = power_s.shape[0], power_s.shape[2]
    kept = pltpu.make_async_copy(left_ref, resid_hbm, sems.at[blocks])
    kept.start()
    both = jnp.concatenate([weights, values], axis=0)
    total = jnp.sum(weights.astype(F32), axis=1, keepdims=True)
    level = jnp.sum(values.astype(F32), axis=1, keepdims=True)

    def out(block):
        at = pl.ds(pl.multiple_of(block * width, width), width)
        return pltpu.make_async_copy(power_s.at[block], power_hbm.at[:, at], sems.at[block])

    def spectrum(block, carry):
        power_s[block] = powers(
            jnp.dot(both, basis_ref[block, 0], preferred_element_type=F32),
            jnp.dot(both, basis_ref[block, 1], preferred_element_type=F32),
            jnp.dot(weights, basis_ref[block, 2], preferred_element_type=F32),
            jnp.dot(weights, basis_ref[block, 3], preferred_element_type=F32),
            total,
            level,
        )
        out(block).start()
        return carry

    lax.fori_loop(0, blocks, spectrum, 0, unroll=UNROLL)
    kept.wait()
    for block in range(blocks):
        out(block).wait()


SIN_TERMS = [(-1.0) ** n / math.factorial(2 * n + 1) for n in range(7)]
COS_TERMS = [(-1.0) ** n / math.factorial(2 * n) for n in range(8)]


def series(square, terms):
    value = jnp.full_like(square, terms[-1])
    for term in terms[-2::-1]:
        value = value * square + term
    return value


def basis_of(cycles):
    cycles = cycles - jnp.floor(cycles)
    turn = jnp.where(cycles >= 0.5, cycles - 1.0, cycles)
    angle = (2.0 * math.pi) * (jnp.abs(turn) - 0.25)
    square = angle * angle
    cosine = -angle * series(square, SIN_TERMS)
    size = series(square, COS_TERMS)
    sine = jnp.where(turn < 0.0, -size, size)
    return cosine, sine, 2.0 * cosine * cosine - 1.0, 2.0 * sine * cosine


def powers(by_cos, by_sin, cosine_two, sine_two, total, level):
    count = cosine_two.shape[0]
    cosine, sine = by_cos[:count], by_sin[:count]
    inverse = 1.0 / total
    mean_level = level * inverse
    ycos = by_cos[count:] - mean_level * cosine
    ysin = by_sin[count:] - mean_level * sine
    cc_term = 0.5 * (total + cosine_two) - cosine * cosine * inverse + RIDGE * total
    ss_term = 0.5 * (total - cosine_two) - sine * sine * inverse + RIDGE * total
    cs_term = 0.5 * sine_two - cosine * sine * inverse
    determinant = cc_term * ss_term - cs_term * cs_term
    return (
        ss_term * ycos * ycos + cc_term * ysin * ysin - 2.0 * cs_term * ycos * ysin
    ) / determinant


def per_device(light_curves, valid, pixel, inv_sigma, modes_init, epoch_jitter, freq_index):
    obj_n = lax.axis_size("obj")
    ep_n = lax.axis_size("ep")
    order = modes_init.shape[1]
    rows, cols = light_curves.shape
    share = rows // ep_n
    epochs = epoch_jitter.shape[0]
    planes = obj_n // GROUP
    tiles = GROUP + 1
    half = cols // 2
    depth = order * order // 2 + order // 2 + order
    quarter = -(-depth // (GROUP * SUB)) * SUB
    chips = GROUP // 2 * ep_n
    inner = GROUP * ep_n - 1
    vmem = pl.BlockSpec(memory_space=pltpu.VMEM)
    hbm = pl.BlockSpec(memory_space=pltpu.HBM)
    sem = pltpu.SemaphoreType.DMA
    count = freq_index.shape[0]
    parts = 4 * ITERS
    left, ready, basis = pl.pallas_call(
        functools.partial(detrend_kernel, obj_n, ep_n, order),
        out_shape=(
            jax.ShapeDtypeStruct((rows, cols), F32),
            jax.ShapeDtypeStruct((2, share, epochs), BF16),
            jax.ShapeDtypeStruct((parts, 4, epochs, count // parts), BF16),
        ),
        in_specs=[hbm] * 7,
        out_specs=(vmem,) * 3,
        scratch_shapes=[
            pltpu.VMEM((rows, cols), F32),
            pltpu.VMEM((rows, cols), jnp.int32),
            pltpu.VMEM((1, rows), jnp.int32),
            pltpu.VMEM((1, rows), F32),
            pltpu.VMEM((1, epochs), F32),
            pltpu.VMEM((1, count), jnp.int32),
            pltpu.VMEM((epochs, LANES), F32),
            pltpu.VMEM((ep_n, GROUP, cols + SUB, rows), F32),
            pltpu.VMEM((half + SUB, rows), F32),
            pltpu.VMEM((2, ep_n, half + SUB, rows), F32),
            pltpu.VMEM((ep_n, order, cols), F32),
            pltpu.VMEM((tiles, epochs, rows), F32),
            pltpu.VMEM((tiles, epochs, rows), F32),
            pltpu.VMEM((tiles, epochs, rows), F32),
            pltpu.VMEM((tiles * order, rows), F32),
            pltpu.VMEM((order, epochs), F32),
            pltpu.VMEM((tiles * depth, rows), F32),
            pltpu.VMEM((epochs, LANES), BF16),
            pltpu.VMEM((ITERS, quarter, rows), F32),
            pltpu.VMEM((ITERS, planes - 1, quarter, rows), F32),
            pltpu.VMEM((order, rows), F32),
            pltpu.VMEM((ITERS, order, rows), F32),
            pltpu.VMEM((ITERS, ep_n, GROUP, order, rows), F32),
            pltpu.VMEM((2, rows, epochs), BF16),
            sem((7,)),
            sem((chips,)),
            sem((chips,)),
            sem((ep_n, GROUP)),
            sem((chips,)),
            sem((ep_n,)),
            sem((2, ep_n)),
            sem((2, ep_n)),
            sem((2, ITERS, planes - 1)),
            sem((2, ITERS, inner)),
        ],
        compiler_params=pltpu.CompilerParams(
            collective_id=0, has_side_effects=True, vmem_limit_bytes=ROOM
        ),
    )(
        *(pltpu.with_memory_space_constraint(given, pltpu.HBM) for given in (
            light_curves, valid, pixel[None], inv_sigma[None], modes_init.T,
            epoch_jitter[None], freq_index[None],
        ))
    )
    return pl.pallas_call(
        spectrum_kernel,
        out_shape=(
            jax.ShapeDtypeStruct((rows, cols), F32),
            jax.ShapeDtypeStruct((share, count), F32),
        ),
        in_specs=[vmem] * 3,
        out_specs=(hbm,) * 2,
        scratch_shapes=[
            pltpu.VMEM((parts, share, count // parts), F32),
            sem((parts + 1,)),
        ],
        compiler_params=pltpu.CompilerParams(vmem_limit_bytes=ROOM // 2),
    )(left, ready, basis)


def solution(mesh):
    in_specs = (P("obj", "ep"), P("obj", "ep"), P("obj"), P("obj"), P("ep", None), P(), P())
    out_specs = (P("obj", "ep"), P(("obj", "ep"), None))
    return jax.shard_map(
        per_device, mesh=mesh, in_specs=in_specs, out_specs=out_specs, check_vma=False
    )
```

```python
import functools
import math

import jax
import jax.numpy as jnp
from jax import lax
from jax.experimental import pallas as pl
from jax.experimental.pallas import tpu as pltpu
from jax.sharding import PartitionSpec as P

ITERS = 2


HUBER = 1.345
DAMP = 2.0
RIDGE = 0.05
HIGHEST = lax.Precision.HIGHEST
LANES = 128
SUB = 8
UNROLL = 4
ROOM = 24 << 20
GROUP = 4
ABSENT = 1e30
F32 = jnp.float32
BF16 = jnp.bfloat16
STRIP = 32
MESH = pl.DeviceIdType.MESH


def halves(values):
    high = values.astype(BF16)
    return high, (values - high.astype(F32)).astype(BF16)


def cyclic_outer(vectors):
    order = vectors.shape[0]
    parts = [vectors * vectors]
    for shift in range(1, order // 2 + 1):
        turned = jnp.concatenate([vectors[shift:], vectors[:shift]], axis=0)
        part = vectors * turned
        parts.append(part if shift < order // 2 else part[: order // 2])
    return jnp.concatenate(parts, axis=0)


def cyclic_row(i, j, order):
    ahead = (j - i) % order
    if ahead == order // 2:
        return ahead * order + min(i, j)
    return ahead * order + i if ahead < order // 2 else (order - ahead) * order + j


def damped_solve(load, order):
    pairs = order * order // 2 + order // 2
    entry = {}
    for i in range(order):
        for j in range(i + 1):
            entry[i, j] = load(cyclic_row(i, j, order))
        entry[i, i] = entry[i, i] + DAMP
    remain = [load(pairs + i) for i in range(order)]
    factor = {}
    for k in range(order):
        inverse = 1.0 / entry[k, k]
        for i in range(k + 1, order):
            factor[i, k] = entry[i, k] * inverse
            for j in range(k + 1, i + 1):
                entry[i, j] = entry[i, j] - factor[i, k] * entry[j, k]
            remain[i] = remain[i] - factor[i, k] * remain[k]
        remain[k] = remain[k] * inverse
    for k in reversed(range(order)):
        for j in range(k):
            remain[j] = remain[j] - factor[k, j] * remain[k]
    return remain


def as_column(row):
    return jnp.broadcast_to(row, (LANES, row.shape[1])).T


def detrend_kernel(
    obj_n, ep_n, order, lc_hbm, valid_hbm, pixel_hbm, sigma_hbm, modes_hbm,
    jitter_hbm, freq_hbm, resid_ref, ready_ref, basis_s,
    lc_ref, valid_ref, pixel_ref, sigma_ref, jitter_ref, freq_ref, times_s,
    blk, halo_send, halo, first, lens, mens, sres, coef_s, modes_s, gram_s, tall_s,
    part_send, part_recv, solved_s, mode_send, mode_recv, final_s,
    load_sem, near_sem, forward_sem, blk_sem, halo_out, halo_forward, halo_sem, first_sem,
    part_sem, mode_sem,
):
    me_o, me_e = lax.axis_index("obj"), lax.axis_index("ep")
    rows, cols = lc_ref.shape
    planes = obj_n // GROUP
    q, r = me_o // GROUP, lax.rem(me_o, GROUP)
    p, core = r // 2, lax.rem(r, 2)
    share = rows // ep_n
    epochs = cols * ep_n
    half = cols // 2
    tiles = GROUP + 1
    slab = cols // GROUP
    pairs = order * order // 2 + order // 2
    depth = pairs + order
    quarter = part_send.shape[1]
    pixels = 4 * obj_n

    def device(plane, chip, side, ep):
        return {"obj": plane * GROUP + chip * 2 + side, "ep": ep}

    def remote(src, dst, send, recv, where):
        return pltpu.make_async_remote_copy(
            src_ref=src, dst_ref=dst, send_sem=send, recv_sem=recv,
            device_id=where, device_id_type=MESH,
        )

    chips = sorted(
        ((dp, de) for dp in range(GROUP // 2) for de in range(ep_n)),
        key=lambda step: (min(step[0], 1) + min(step[1], 1)) % 3 * -1,
    )
    inner = [(dr, de) for dr in range(GROUP) for de in range(ep_n) if (dr, de) != (0, 0)]

    def turned(dp, de):
        return lax.rem(p + dp, GROUP // 2), lax.rem(me_e + de, ep_n)

    has_prev, has_next = q > 0, q < planes - 1
    barrier = pltpu.get_barrier_semaphore()

    def greet(where):
        pl.semaphore_signal(barrier, inc=1, device_id=where, device_id_type=MESH)

    for dr, de in inner:
        greet({"obj": q * GROUP + lax.rem(r + dr, GROUP), "ep": lax.rem(me_e + de, ep_n)})
    for k in range(1, planes):
        greet({"obj": lax.rem(me_o + k * GROUP, obj_n), "ep": me_e})
    for there, exists in ((q - 1, has_prev), (q + 1, has_next)):
        @pl.when(exists)
        def _():
            for dp, de in chips:
                chip, ep = turned(dp, de)
                greet(device(there, chip, core, ep))

    loads = [
        pltpu.make_async_copy(source, target, load_sem.at[n])
        for n, (source, target) in enumerate((
            (lc_hbm, lc_ref), (valid_hbm, valid_ref), (pixel_hbm, pixel_ref),
            (sigma_hbm, sigma_ref), (modes_hbm, first.at[me_e]), (jitter_hbm, jitter_ref),
            (freq_hbm, freq_ref),
        ))
    ]
    for load in loads:
        load.start()
    for load in loads:
        load.wait()

    width = basis_s.shape[3]
    times_s[...] = as_column(
        lax.broadcasted_iota(jnp.int32, (1, epochs), 1).astype(F32) + jitter_ref[...]
    )

    def fill_basis(block):
        begin = pl.multiple_of(block * width, width)
        freqs = (freq_ref[:, pl.ds(begin, width)] + 1).astype(F32) / (4.0 * epochs)

        def strip(step, carry):
            at = pl.ds(pl.multiple_of(step * STRIP, STRIP), STRIP)
            times = jnp.concatenate([times_s[at, :]] * (width // LANES), axis=1)
            for kind, values in enumerate(basis_of(times * freqs)):
                basis_s[block, kind, at, :] = values.astype(BF16)
            return carry

        lax.fori_loop(0, epochs // STRIP, strip, 0)

    blocks = basis_s.shape[0]
    lane = lax.broadcasted_iota(jnp.int32, (1, rows), 1)
    low_half = lane < rows // 2
    own = jnp.where(valid_ref[...] != 0, lc_ref[...], ABSENT).T
    marks = jnp.concatenate(
        [pixel_ref[...].astype(F32), sigma_ref[...], jnp.zeros((SUB - 2, rows), F32)], axis=0
    )
    mine = blk.at[me_e, r]
    blk[me_e, r, :cols] = own
    blk[me_e, r, cols:] = marks
    upper, lower = own[:half], own[half:]
    is_last = r == GROUP - 1
    turned_upper, turned_lower = pltpu.roll(upper, rows // 2, 1), pltpu.roll(lower, rows // 2, 1)
    halo_send[:half] = jnp.where(
        is_last,
        jnp.where(low_half, turned_upper, lower),
        jnp.where(low_half, upper, turned_lower),
    )
    halo_send[half:] = jnp.where(is_last, pltpu.roll(marks, rows // 2, 1), marks)
    missing = jnp.concatenate(
        [jnp.full((half, rows), ABSENT, F32), jnp.full((1, rows), -1.0, F32),
         jnp.ones((SUB - 1, rows), F32)], axis=0,
    )
    for kind, exists in ((0, has_prev), (1, has_next)):
        @pl.when(jnp.logical_not(exists))
        def _():
            for ep in range(ep_n):
                halo[kind, ep] = missing

    def early(block, carry):
        fill_basis(block)
        return carry

    lax.fori_loop(0, blocks // 4, early, 0)
    pl.semaphore_wait(
        barrier,
        len(inner) + planes - 1 + len(chips) * (has_prev.astype(jnp.int32) + has_next.astype(jnp.int32)),
    )

    partner = device(q, p, 1 - core, me_e)
    near = []
    for n, (dp, de) in enumerate(chips):
        if (dp, de) != (0, 0):
            chip, ep = turned(dp, de)
            near.append(remote(mine, mine, near_sem.at[n], blk_sem.at[me_e, r], device(q, chip, core, ep)))
            near[-1].start()
    forwards = [remote(mine, mine, forward_sem.at[0], blk_sem.at[me_e, r], partner)]
    forwards[0].start()
    greetings = []
    for de in range(1, ep_n):
        greetings.append(remote(
            first.at[me_e], first.at[me_e], first_sem.at[0, de], first_sem.at[1, me_e],
            device(q, p, core, lax.rem(me_e + de, ep_n)),
        ))
        greetings[-1].start()

    halo_kinds = (
        (0, q + 1, jnp.logical_and(r == GROUP - 1, has_next), has_prev, core == 1),
        (1, q - 1, jnp.logical_and(r == 0, has_prev), has_next, core == 0),
    )

    def halo_copies(kind, there):
        made = []
        for n, (dp, de) in enumerate(chips):
            chip, ep = turned(dp, de)
            made.append(remote(
                halo_send, halo.at[kind, me_e], halo_out.at[n], halo_sem.at[kind, me_e],
                device(there, chip, core, ep),
            ))
        return made

    for kind, there, sends, _, _ in halo_kinds:
        @pl.when(sends)
        def _():
            for copy in halo_copies(kind, there):
                copy.start()

    def late(block, carry):
        fill_basis(block)
        return carry

    lax.fori_loop(blocks // 4, blocks // 2, late, 0)

    def halo_step(kind, ep):
        slot = halo.at[kind, ep]
        return remote(slot, slot, halo_forward.at[ep], halo_sem.at[kind, ep], partner)

    for n, (dp, de) in enumerate(chips):
        if (dp, de) != (0, 0):
            chip, ep = turned(dp, de)
            slot = blk.at[ep, chip * 2 + core]
            forward = remote(slot, slot, forward_sem.at[n], blk_sem.at[ep, chip * 2 + core], partner)
            forward.wait_recv()
            forward.start()
            forwards.append(forward)
    for kind, _, _, arrives, passes in halo_kinds:
        @pl.when(jnp.logical_and(arrives, passes))
        def _():
            for ep in range(ep_n):
                step = halo_step(kind, ep)
                step.wait_recv()
                step.start()

    for dp, de in chips:
        chip, ep = turned(dp, de)
        slot = blk.at[ep, chip * 2 + 1 - core]
        remote(slot, slot, forward_sem.at[0], blk_sem.at[ep, chip * 2 + 1 - core], partner).wait_recv()
    for kind, _, _, arrives, passes in halo_kinds:
        @pl.when(jnp.logical_and(arrives, jnp.logical_not(passes)))
        def _():
            for ep in range(ep_n):
                halo_step(kind, ep).wait_recv()
    for de in range(1, ep_n):
        ep = lax.rem(me_e + de, ep_n)
        remote(first.at[ep], first.at[ep], first_sem.at[0, de], first_sem.at[1, ep], partner).wait_recv()
    for copy in near + forwards + greetings:
        copy.wait_send()
    for kind, there, sends, _, _ in halo_kinds:
        @pl.when(sends)
        def _():
            for copy in halo_copies(kind, there):
                copy.wait_send()
    for kind, _, _, arrives, passes in halo_kinds:
        @pl.when(jnp.logical_and(arrives, passes))
        def _():
            for ep in range(ep_n):
                halo_step(kind, ep).wait_send()

    pixel_level = lax.broadcasted_iota(jnp.int32, (pixels, rows), 0).astype(F32)
    marked = [blk[0, t, cols:] for t in range(GROUP)]
    before, after = halo[0, 0, half:], pltpu.roll(halo[1, 0, half:], rows // 2, 1)
    marked.append(jnp.where(low_half, before, after))
    pixel_row = [m[0:1] for m in marked]
    sigma_row = [m[1:2] for m in marked]
    totals = []
    for t in range(tiles):
        total = jnp.zeros((1, rows), F32)
        for ep in range(ep_n):
            if t < GROUP:
                value = blk[ep, t, :cols]
            else:
                prev, follow = halo[0, ep, :half], halo[1, ep, :half]
                value = jnp.concatenate([
                    jnp.where(low_half, prev, pltpu.roll(follow, rows // 2, 1)),
                    jnp.where(low_half, pltpu.roll(prev, rows // 2, 1), follow),
                ], axis=0)
            seen = value < 0.5 * ABSENT
            scale = jnp.where(seen, sigma_row[t], 0.0)
            at = slice(ep * cols, (ep + 1) * cols)
            mens[t, at] = scale
            lens[t, at] = value * scale
            total = total + jnp.sum(seen.astype(F32), axis=0, keepdims=True)
        totals.append(total)

    def by_pixel(tile_rows, tile_pixels):
        gathered = jnp.zeros((pixels, rows), F32)
        for row, where in zip(tile_rows, tile_pixels):
            gathered = gathered + jnp.where(where == pixel_level, row, 0.0)
        return jnp.sum(gathered, axis=1, keepdims=True)

    inverse_count = 1.0 / jnp.maximum(by_pixel(totals, pixel_row), 1.0)

    def limits(squares, tile_pixels, wanted):
        sums = by_pixel(squares, tile_pixels)
        spread = HUBER * jnp.sqrt(sums * inverse_count + 1e-06)
        return [
            jnp.maximum(
                jnp.sum(jnp.where(where == pixel_level, spread, 0.0), axis=0, keepdims=True), 1e-3
            )
            for where in wanted
        ]

    def modes_factor():
        high, low = halves(modes_s[...])
        stacked = jnp.concatenate([high, high, low], axis=0).astype(F32)
        stacked = jnp.concatenate(
            [stacked, jnp.zeros((LANES - 3 * order, epochs), F32)], axis=0
        )
        tall_s[...] = stacked.T.astype(BF16)

    def fitted(coef):
        high, low = halves(coef)
        wide = jnp.concatenate(
            [high, low, high, jnp.zeros((LANES - 3 * order, coef.shape[1]), BF16)], axis=0
        )
        return jnp.dot(tall_s[...], wide, preferred_element_type=F32)

    def scaled_residuals():
        squares = []
        for t in range(tiles):
            left = lens[t] - mens[t] * fitted(coef_s[t * order : (t + 1) * order])
            sres[t] = left
            squares.append(jnp.sum(left * left, axis=0, keepdims=True))
        return squares

    def reach(left, limit, sigma):
        return (sigma * limit) / jnp.maximum(jnp.abs(left), limit)

    coef_s[...] = jnp.zeros_like(coef_s)
    for ep in range(ep_n):
        modes_s[:, ep * cols : (ep + 1) * cols] = first[ep]
    modes_factor()

    def iteration(it, carry):
        limit = limits(scaled_residuals(), pixel_row, pixel_row)
        modes = modes_s[...]
        outer_high, outer_low = halves(cyclic_outer(modes))
        modes_high, modes_low = halves(modes)
        for t in range(tiles):
            factor = reach(sres[t], limit[t], sigma_row[t])
            weight, weight_low = halves(mens[t] * factor)
            value_high, value_low = halves(lens[t] * factor)
            gram = jnp.dot(outer_high, weight, preferred_element_type=F32)
            gram = gram + jnp.dot(outer_low, weight, preferred_element_type=F32)
            gram = gram + jnp.dot(outer_high, weight_low, preferred_element_type=F32)
            target = jnp.dot(modes_high, value_high, preferred_element_type=F32)
            target = target + jnp.dot(modes_low, value_high, preferred_element_type=F32)
            target = target + jnp.dot(modes_high, value_low, preferred_element_type=F32)
            gram_s[t * depth : t * depth + pairs] = gram
            gram_s[t * depth + pairs : (t + 1) * depth] = target
        solved = damped_solve(lambda row: gram_s[pl.ds(row, tiles, stride=depth), :], order)
        for k in range(order):
            coef_s[pl.ds(k, tiles, stride=order), :] = solved[k]

        limit = limits(scaled_residuals(), pixel_row, pixel_row[:GROUP])
        at = pl.ds(pl.multiple_of(me_e * cols + r * slab, slab), slab)
        weights, weight_lows, value_highs, value_lows, outers, coefs = [], [], [], [], [], []
        for t in range(GROUP):
            factor = reach(sres[t, at], limit[t], sigma_row[t])
            weight, weight_low = halves(mens[t, at] * factor)
            weights.append(weight)
            weight_lows.append(weight_low)
            value_high, value_low = halves(lens[t, at] * factor)
            value_highs.append(value_high)
            value_lows.append(value_low)
            coef = coef_s[t * order : (t + 1) * order]
            outers.append(halves(cyclic_outer(coef)))
            coefs.append(halves(coef))

        def copied(parts):
            return jnp.concatenate([jnp.concatenate(parts, axis=1)] * GROUP, axis=0)

        def across(left, right):
            return lax.dot_general(
                left, right, (((1,), (1,)), ((), ())), preferred_element_type=F32
            )

        weight, weight_low = copied(weights), copied(weight_lows)
        value_high, value_low = copied(value_highs), copied(value_lows)
        outer_high = jnp.concatenate([pair[0] for pair in outers], axis=1)
        outer_low = jnp.concatenate([pair[1] for pair in outers], axis=1)
        coef_high = jnp.concatenate([pair[0] for pair in coefs], axis=1)
        coef_low = jnp.concatenate([pair[1] for pair in coefs], axis=1)
        gram = across(outer_high, weight) + across(outer_low, weight)
        gram = gram + across(outer_high, weight_low)
        target = across(coef_high, value_high) + across(coef_low, value_high)
        target = target + across(coef_high, value_low)
        whole = jnp.concatenate(
            [gram, target, jnp.zeros((GROUP * quarter - depth, rows), F32)], axis=0
        )
        packed = whole[:quarter]
        for k in range(1, GROUP):
            packed = jnp.where(lane >= k * slab, whole[k * quarter : (k + 1) * quarter], packed)
        part_send[it] = packed
        copies = []
        for k in range(1, planes):
            copies.append(remote(
                part_send.at[it], part_recv.at[it, k - 1],
                part_sem.at[0, it, k - 1], part_sem.at[1, it, k - 1],
                {"obj": lax.rem(me_o + k * GROUP, obj_n), "ep": me_e},
            ))
            copies[-1].start()
        fill_basis(blocks // 2 + 2 * it)
        for k in range(1, planes):
            copies[k - 1].wait()
            packed = packed + part_recv[it, k - 1]
        gram_s[:quarter] = packed
        for k in range(1, GROUP):
            gram_s[k * quarter : (k + 1) * quarter] = pltpu.roll(packed, rows - k * slab, 1)
        solved = damped_solve(lambda row: gram_s[row : row + 1, :], order)
        for k in range(order):
            solved_s[k : k + 1] = solved[k]
        fresh = pltpu.roll(solved_s[...], r * slab, 1)
        mode_send[it] = fresh
        mode_recv[it, me_e, r] = fresh
        copies = []
        for n, (dr, de) in enumerate(inner):
            copies.append(remote(
                mode_send.at[it], mode_recv.at[it, me_e, r],
                mode_sem.at[0, it, n], mode_sem.at[1, it, n],
                {"obj": q * GROUP + lax.rem(r + dr, GROUP), "ep": lax.rem(me_e + de, ep_n)},
            ))
            copies[-1].start()
        fill_basis(blocks // 2 + 2 * it + 1)
        for copy in copies:
            copy.wait()
        for ep in range(ep_n):
            joined = mode_recv[it, ep, 0]
            for k in range(1, GROUP):
                joined = jnp.where(lane >= k * slab, mode_recv[it, ep, k], joined)
            modes_s[:, ep * cols : (ep + 1) * cols] = joined
        modes_factor()
        return carry

    lax.fori_loop(0, ITERS, iteration, 0)
    own_coef = coef_s[pl.ds(pl.multiple_of(r * order, order), order), :]
    beside = jnp.where(
        me_e < ep_n // 2, jnp.where(r == 0, GROUP, r - 1), r + 1
    )
    side_coef = coef_s[pl.ds(pl.multiple_of(beside * order, order), order), :]
    both_pixels, squares = [], []
    lefts = []
    for t, coef in ((r, own_coef), (beside, side_coef)):
        left = lens[t] - mens[t] * fitted(coef)
        lefts.append(left)
        squares.append(jnp.sum(left * left, axis=0, keepdims=True))
    for t, name in ((r, 0), (beside, 1)):
        chosen = pixel_row[0]
        for k in range(1, tiles):
            chosen = jnp.where(t == k, pixel_row[k], chosen)
        both_pixels.append(chosen)
    own_sigma = sigma_ref[...]
    (limit,) = limits(squares, both_pixels, both_pixels[:1])
    factor = reach(lefts[0], limit, own_sigma)
    final_s[0] = (mens[r] * factor).T.astype(BF16)
    final_s[1] = (lefts[0] * factor).T.astype(BF16)
    own_modes = modes_s[:, pl.ds(pl.multiple_of(me_e * cols, cols), cols)]
    resid_ref[...] = lc_ref[...] - lax.dot_general(
        own_coef, own_modes, (((0,), (0,)), ((), ())),
        precision=HIGHEST, preferred_element_type=F32,
    )
    mine_at = pl.ds(pl.multiple_of(me_e * share, share), share)
    ready_ref[...] = final_s[:, mine_at, :]


def spectrum_kernel(left_ref, ready_ref, basis_ref, resid_hbm, power_hbm, power_s, sems):
    weights, values = ready_ref[0], ready_ref[1]
    blocks, width = power_s.shape[0], power_s.shape[2]
    kept = pltpu.make_async_copy(left_ref, resid_hbm, sems.at[blocks])
    kept.start()
    both = jnp.concatenate([weights, values], axis=0)
    total = jnp.sum(weights.astype(F32), axis=1, keepdims=True)
    level = jnp.sum(values.astype(F32), axis=1, keepdims=True)

    def out(block):
        at = pl.ds(pl.multiple_of(block * width, width), width)
        return pltpu.make_async_copy(power_s.at[block], power_hbm.at[:, at], sems.at[block])

    def spectrum(block, carry):
        power_s[block] = powers(
            jnp.dot(both, basis_ref[block, 0], preferred_element_type=F32),
            jnp.dot(both, basis_ref[block, 1], preferred_element_type=F32),
            jnp.dot(weights, basis_ref[block, 2], preferred_element_type=F32),
            jnp.dot(weights, basis_ref[block, 3], preferred_element_type=F32),
            total,
            level,
        )
        out(block).start()
        return carry

    lax.fori_loop(0, blocks, spectrum, 0, unroll=UNROLL)
    kept.wait()
    for block in range(blocks):
        out(block).wait()


SIN_TERMS = [(-1.0) ** n / math.factorial(2 * n + 1) for n in range(7)]
COS_TERMS = [(-1.0) ** n / math.factorial(2 * n) for n in range(8)]


def series(square, terms):
    value = jnp.full_like(square, terms[-1])
    for term in terms[-2::-1]:
        value = value * square + term
    return value


def basis_of(cycles):
    cycles = cycles - jnp.floor(cycles)
    turn = jnp.where(cycles >= 0.5, cycles - 1.0, cycles)
    angle = (2.0 * math.pi) * (jnp.abs(turn) - 0.25)
    square = angle * angle
    cosine = -angle * series(square, SIN_TERMS)
    size = series(square, COS_TERMS)
    sine = jnp.where(turn < 0.0, -size, size)
    return cosine, sine, 2.0 * cosine * cosine - 1.0, 2.0 * sine * cosine


def powers(by_cos, by_sin, cosine_two, sine_two, total, level):
    count = cosine_two.shape[0]
    cosine, sine = by_cos[:count], by_sin[:count]
    inverse = 1.0 / total
    mean_level = level * inverse
    ycos = by_cos[count:] - mean_level * cosine
    ysin = by_sin[count:] - mean_level * sine
    cc_term = 0.5 * (total + cosine_two) - cosine * cosine * inverse + RIDGE * total
    ss_term = 0.5 * (total - cosine_two) - sine * sine * inverse + RIDGE * total
    cs_term = 0.5 * sine_two - cosine * sine * inverse
    determinant = cc_term * ss_term - cs_term * cs_term
    return (
        ss_term * ycos * ycos + cc_term * ysin * ysin - 2.0 * cs_term * ycos * ysin
    ) / determinant


def per_device(light_curves, valid, pixel, inv_sigma, modes_init, epoch_jitter, freq_index):
    obj_n = lax.axis_size("obj")
    ep_n = lax.axis_size("ep")
    order = modes_init.shape[1]
    rows, cols = light_curves.shape
    share = rows // ep_n
    epochs = epoch_jitter.shape[0]
    planes = obj_n // GROUP
    tiles = GROUP + 1
    half = cols // 2
    depth = order * order // 2 + order // 2 + order
    quarter = -(-depth // (GROUP * SUB)) * SUB
    chips = GROUP // 2 * ep_n
    inner = GROUP * ep_n - 1
    vmem = pl.BlockSpec(memory_space=pltpu.VMEM)
    hbm = pl.BlockSpec(memory_space=pltpu.HBM)
    sem = pltpu.SemaphoreType.DMA
    count = freq_index.shape[0]
    parts = 4 * ITERS
    left, ready, basis = pl.pallas_call(
        functools.partial(detrend_kernel, obj_n, ep_n, order),
        out_shape=(
            jax.ShapeDtypeStruct((rows, cols), F32),
            jax.ShapeDtypeStruct((2, share, epochs), BF16),
            jax.ShapeDtypeStruct((parts, 4, epochs, count // parts), BF16),
        ),
        in_specs=[hbm] * 7,
        out_specs=(vmem,) * 3,
        scratch_shapes=[
            pltpu.VMEM((rows, cols), F32),
            pltpu.VMEM((rows, cols), jnp.int32),
            pltpu.VMEM((1, rows), jnp.int32),
            pltpu.VMEM((1, rows), F32),
            pltpu.VMEM((1, epochs), F32),
            pltpu.VMEM((1, count), jnp.int32),
            pltpu.VMEM((epochs, LANES), F32),
            pltpu.VMEM((ep_n, GROUP, cols + SUB, rows), F32),
            pltpu.VMEM((half + SUB, rows), F32),
            pltpu.VMEM((2, ep_n, half + SUB, rows), F32),
            pltpu.VMEM((ep_n, order, cols), F32),
            pltpu.VMEM((tiles, epochs, rows), F32),
            pltpu.VMEM((tiles, epochs, rows), F32),
            pltpu.VMEM((tiles, epochs, rows), F32),
            pltpu.VMEM((tiles * order, rows), F32),
            pltpu.VMEM((order, epochs), F32),
            pltpu.VMEM((tiles * depth, rows), F32),
            pltpu.VMEM((epochs, LANES), BF16),
            pltpu.VMEM((ITERS, quarter, rows), F32),
            pltpu.VMEM((ITERS, planes - 1, quarter, rows), F32),
            pltpu.VMEM((order, rows), F32),
            pltpu.VMEM((ITERS, order, rows), F32),
            pltpu.VMEM((ITERS, ep_n, GROUP, order, rows), F32),
            pltpu.VMEM((2, rows, epochs), BF16),
            sem((7,)),
            sem((chips,)),
            sem((chips,)),
            sem((ep_n, GROUP)),
            sem((chips,)),
            sem((ep_n,)),
            sem((2, ep_n)),
            sem((2, ep_n)),
            sem((2, ITERS, planes - 1)),
            sem((2, ITERS, inner)),
        ],
        compiler_params=pltpu.CompilerParams(
            collective_id=0, has_side_effects=True, vmem_limit_bytes=ROOM
        ),
    )(
        *(pltpu.with_memory_space_constraint(given, pltpu.HBM) for given in (
            light_curves, valid, pixel[None], inv_sigma[None], modes_init.T,
            epoch_jitter[None], freq_index[None],
        ))
    )
    return pl.pallas_call(
        spectrum_kernel,
        out_shape=(
            jax.ShapeDtypeStruct((rows, cols), F32),
            jax.ShapeDtypeStruct((share, count), F32),
        ),
        in_specs=[vmem] * 3,
        out_specs=(hbm,) * 2,
        scratch_shapes=[
            pltpu.VMEM((parts, share, count // parts), F32),
            sem((parts + 1,)),
        ],
        compiler_params=pltpu.CompilerParams(vmem_limit_bytes=ROOM // 2),
    )(left, ready, basis)


def solution(mesh):
    in_specs = (P("obj", "ep"), P("obj", "ep"), P("obj"), P("obj"), P("ep", None), P(), P())
    out_specs = (P("obj", "ep"), P(("obj", "ep"), None))
    return jax.shard_map(
        per_device, mesh=mesh, in_specs=in_specs, out_specs=out_specs, check_vma=False
    )
```

```python
import functools
import math

import jax
import jax.numpy as jnp
from jax import lax
from jax.experimental import pallas as pl
from jax.experimental.pallas import tpu as pltpu
from jax.sharding import PartitionSpec as P

ITERS = 2


HUBER = 1.345
DAMP = 2.0
RIDGE = 0.05
HIGHEST = lax.Precision.HIGHEST
LANES = 128
SUB = 8
UNROLL = 4
ROOM = 24 << 20
GROUP = 4
ABSENT = 1e30
F32 = jnp.float32
BF16 = jnp.bfloat16
STRIP = 32
MESH = pl.DeviceIdType.MESH


def halves(values):
    high = values.astype(BF16)
    return high, (values - high.astype(F32)).astype(BF16)


def left_parts(parts, axis):
    return jnp.concatenate([parts[0], parts[1], parts[0]], axis=axis)


def right_parts(parts, axis):
    return jnp.concatenate([parts[0], parts[0], parts[1]], axis=axis)


def cyclic_outer(vectors):
    order = vectors.shape[0]
    parts = [vectors * vectors]
    for shift in range(1, order // 2 + 1):
        turned = jnp.concatenate([vectors[shift:], vectors[:shift]], axis=0)
        part = vectors * turned
        parts.append(part if shift < order // 2 else part[: order // 2])
    return jnp.concatenate(parts, axis=0)


def cyclic_row(i, j, order):
    ahead = (j - i) % order
    if ahead == order // 2:
        return ahead * order + min(i, j)
    return ahead * order + i if ahead < order // 2 else (order - ahead) * order + j


def damped_solve(load, order):
    pairs = order * order // 2 + order // 2
    entry = {}
    for i in range(order):
        for j in range(i + 1):
            entry[i, j] = load(cyclic_row(i, j, order))
        entry[i, i] = entry[i, i] + DAMP
    remain = [load(pairs + i) for i in range(order)]
    factor = {}
    for k in range(order):
        inverse = 1.0 / entry[k, k]
        for i in range(k + 1, order):
            factor[i, k] = entry[i, k] * inverse
            for j in range(k + 1, i + 1):
                entry[i, j] = entry[i, j] - factor[i, k] * entry[j, k]
            remain[i] = remain[i] - factor[i, k] * remain[k]
        remain[k] = remain[k] * inverse
    for k in reversed(range(order)):
        for j in range(k):
            remain[j] = remain[j] - factor[k, j] * remain[k]
    return remain


def as_column(row):
    return jnp.broadcast_to(row, (LANES, row.shape[1])).T


def detrend_kernel(
    obj_n, ep_n, order, lc_hbm, valid_hbm, pixel_hbm, sigma_hbm, modes_hbm,
    jitter_hbm, freq_hbm, resid_ref, ready_ref, basis_s,
    lc_ref, valid_ref, pixel_ref, sigma_ref, jitter_ref, freq_ref, times_s,
    blk, halo_send, halo, first, lens, mens, sres, coef_s, modes_s, gram_s, tall_s, square_s,
    part_send, part_recv, solved_s, mode_send, mode_recv, final_s,
    load_sem, near_sem, forward_sem, blk_sem, halo_out, halo_forward, halo_sem, first_sem,
    part_sem, mode_sem,
):
    me_o, me_e = lax.axis_index("obj"), lax.axis_index("ep")
    rows, cols = lc_ref.shape
    planes = obj_n // GROUP
    q, r = me_o // GROUP, lax.rem(me_o, GROUP)
    p, core = r // 2, lax.rem(r, 2)
    share = rows // ep_n
    epochs = cols * ep_n
    half = cols // 2
    tiles = GROUP + 1
    slab = cols // GROUP
    pairs = order * order // 2 + order // 2
    depth = pairs + order
    quarter = part_send.shape[1]
    pixels = 4 * obj_n

    def device(plane, chip, side, ep):
        return {"obj": plane * GROUP + chip * 2 + side, "ep": ep}

    def remote(src, dst, send, recv, where):
        return pltpu.make_async_remote_copy(
            src_ref=src, dst_ref=dst, send_sem=send, recv_sem=recv,
            device_id=where, device_id_type=MESH,
        )

    chips = sorted(
        ((dp, de) for dp in range(GROUP // 2) for de in range(ep_n)),
        key=lambda step: (min(step[0], 1) + min(step[1], 1)) % 3 * -1,
    )
    inner = [(dr, de) for dr in range(GROUP) for de in range(ep_n) if (dr, de) != (0, 0)]

    def turned(dp, de):
        return lax.rem(p + dp, GROUP // 2), lax.rem(me_e + de, ep_n)

    has_prev, has_next = q > 0, q < planes - 1
    barrier = pltpu.get_barrier_semaphore()

    def greet(where):
        pl.semaphore_signal(barrier, inc=1, device_id=where, device_id_type=MESH)

    for dr, de in inner:
        greet({"obj": q * GROUP + lax.rem(r + dr, GROUP), "ep": lax.rem(me_e + de, ep_n)})
    for k in range(1, planes):
        greet({"obj": lax.rem(me_o + k * GROUP, obj_n), "ep": me_e})
    for there, exists in ((q - 1, has_prev), (q + 1, has_next)):
        @pl.when(exists)
        def _():
            for dp, de in chips:
                chip, ep = turned(dp, de)
                greet(device(there, chip, core, ep))

    loads = [
        pltpu.make_async_copy(source, target, load_sem.at[n])
        for n, (source, target) in enumerate((
            (lc_hbm, lc_ref), (valid_hbm, valid_ref), (pixel_hbm, pixel_ref),
            (sigma_hbm, sigma_ref), (modes_hbm, first.at[me_e]), (jitter_hbm, jitter_ref),
            (freq_hbm, freq_ref),
        ))
    ]
    for load in loads:
        load.start()
    for load in loads:
        load.wait()

    width = basis_s.shape[3]
    times_s[...] = as_column(
        lax.broadcasted_iota(jnp.int32, (1, epochs), 1).astype(F32) + jitter_ref[...]
    )

    def fill_basis(block):
        begin = pl.multiple_of(block * width, width)
        freqs = (freq_ref[:, pl.ds(begin, width)] + 1).astype(F32) / (4.0 * epochs)

        def strip(step, carry):
            at = pl.ds(pl.multiple_of(step * STRIP, STRIP), STRIP)
            times = jnp.concatenate([times_s[at, :]] * (width // LANES), axis=1)
            for kind, values in enumerate(basis_of(times * freqs)):
                basis_s[block, kind, at, :] = values.astype(BF16)
            return carry

        lax.fori_loop(0, epochs // STRIP, strip, 0)

    blocks = basis_s.shape[0]
    lane = lax.broadcasted_iota(jnp.int32, (1, rows), 1)
    low_half = lane < rows // 2
    own = jnp.where(valid_ref[...] != 0, lc_ref[...], ABSENT).T
    marks = jnp.concatenate(
        [pixel_ref[...].astype(F32), sigma_ref[...], jnp.zeros((SUB - 2, rows), F32)], axis=0
    )
    mine = blk.at[me_e, r]
    blk[me_e, r, :cols] = own
    blk[me_e, r, cols:] = marks
    upper, lower = own[:half], own[half:]
    is_last = r == GROUP - 1
    turned_upper, turned_lower = pltpu.roll(upper, rows // 2, 1), pltpu.roll(lower, rows // 2, 1)
    halo_send[:half] = jnp.where(
        is_last,
        jnp.where(low_half, turned_upper, lower),
        jnp.where(low_half, upper, turned_lower),
    )
    halo_send[half:] = jnp.where(is_last, pltpu.roll(marks, rows // 2, 1), marks)
    missing = jnp.concatenate(
        [jnp.full((half, rows), ABSENT, F32), jnp.full((1, rows), -1.0, F32),
         jnp.ones((SUB - 1, rows), F32)], axis=0,
    )
    for kind, exists in ((0, has_prev), (1, has_next)):
        @pl.when(jnp.logical_not(exists))
        def _():
            for ep in range(ep_n):
                halo[kind, ep] = missing

    def early(block, carry):
        fill_basis(block)
        return carry

    lax.fori_loop(0, blocks // 4, early, 0)
    pl.semaphore_wait(
        barrier,
        len(inner) + planes - 1 + len(chips) * (has_prev.astype(jnp.int32) + has_next.astype(jnp.int32)),
    )

    partner = device(q, p, 1 - core, me_e)
    near = []
    for n, (dp, de) in enumerate(chips):
        if (dp, de) != (0, 0):
            chip, ep = turned(dp, de)
            near.append(remote(mine, mine, near_sem.at[n], blk_sem.at[me_e, r], device(q, chip, core, ep)))
            near[-1].start()
    forwards = [remote(mine, mine, forward_sem.at[0], blk_sem.at[me_e, r], partner)]
    forwards[0].start()
    greetings = []
    for de in range(1, ep_n):
        greetings.append(remote(
            first.at[me_e], first.at[me_e], first_sem.at[0, de], first_sem.at[1, me_e],
            device(q, p, core, lax.rem(me_e + de, ep_n)),
        ))
        greetings[-1].start()

    halo_kinds = (
        (0, q + 1, jnp.logical_and(r == GROUP - 1, has_next), has_prev, core == 1),
        (1, q - 1, jnp.logical_and(r == 0, has_prev), has_next, core == 0),
    )

    def halo_copies(kind, there):
        made = []
        for n, (dp, de) in enumerate(chips):
            chip, ep = turned(dp, de)
            made.append(remote(
                halo_send, halo.at[kind, me_e], halo_out.at[n], halo_sem.at[kind, me_e],
                device(there, chip, core, ep),
            ))
        return made

    for kind, there, sends, _, _ in halo_kinds:
        @pl.when(sends)
        def _():
            for copy in halo_copies(kind, there):
                copy.start()

    def late(block, carry):
        fill_basis(block)
        return carry

    lax.fori_loop(blocks // 4, blocks // 2, late, 0)

    def halo_step(kind, ep):
        slot = halo.at[kind, ep]
        return remote(slot, slot, halo_forward.at[ep], halo_sem.at[kind, ep], partner)

    for n, (dp, de) in enumerate(chips):
        if (dp, de) != (0, 0):
            chip, ep = turned(dp, de)
            slot = blk.at[ep, chip * 2 + core]
            forward = remote(slot, slot, forward_sem.at[n], blk_sem.at[ep, chip * 2 + core], partner)
            forward.wait_recv()
            forward.start()
            forwards.append(forward)
    for kind, _, _, arrives, passes in halo_kinds:
        @pl.when(jnp.logical_and(arrives, passes))
        def _():
            for ep in range(ep_n):
                step = halo_step(kind, ep)
                step.wait_recv()
                step.start()

    def unpack(t, values, sigma):
        total = square = jnp.zeros((1, rows), F32)
        for ep, value in enumerate(values):
            seen = value < 0.5 * ABSENT
            scale = jnp.where(seen, sigma, 0.0)
            at = slice(ep * cols, (ep + 1) * cols)
            mens[t, at] = scale
            scaled = value * scale
            lens[t, at] = scaled
            sres[t, at] = scaled
            square = square + jnp.sum(scaled * scaled, axis=0, keepdims=True)
            total = total + jnp.sum(seen.astype(F32), axis=0, keepdims=True)
        square_s[t] = square
        return total

    def unpack_block(side):
        for dp in range(GROUP // 2):
            t = lax.rem(p + dp, GROUP // 2) * 2 + side
            total = unpack(
                t, [blk[ep, t, :cols] for ep in range(ep_n)], blk[0, t, cols + 1 : cols + 2]
            )
            totals.append(total)
            total_pixels.append(blk[0, t, cols : cols + 1])

    totals, total_pixels = [], []
    unpack_block(core)
    for dp, de in chips:
        chip, ep = turned(dp, de)
        slot = blk.at[ep, chip * 2 + 1 - core]
        remote(slot, slot, forward_sem.at[0], blk_sem.at[ep, chip * 2 + 1 - core], partner).wait_recv()
    for kind, _, _, arrives, passes in halo_kinds:
        @pl.when(jnp.logical_and(arrives, jnp.logical_not(passes)))
        def _():
            for ep in range(ep_n):
                halo_step(kind, ep).wait_recv()
    for de in range(1, ep_n):
        ep = lax.rem(me_e + de, ep_n)
        remote(first.at[ep], first.at[ep], first_sem.at[0, de], first_sem.at[1, ep], partner).wait_recv()
    for copy in near + forwards + greetings:
        copy.wait_send()
    for kind, there, sends, _, _ in halo_kinds:
        @pl.when(sends)
        def _():
            for copy in halo_copies(kind, there):
                copy.wait_send()
    for kind, _, _, arrives, passes in halo_kinds:
        @pl.when(jnp.logical_and(arrives, passes))
        def _():
            for ep in range(ep_n):
                halo_step(kind, ep).wait_send()

    unpack_block(1 - core)
    pixel_level = lax.broadcasted_iota(jnp.int32, (pixels, rows), 0).astype(F32)
    marked = [blk[0, t, cols:] for t in range(GROUP)]
    before, after = halo[0, 0, half:], pltpu.roll(halo[1, 0, half:], rows // 2, 1)
    marked.append(jnp.where(low_half, before, after))
    pixel_row = [m[0:1] for m in marked]
    sigma_row = [m[1:2] for m in marked]
    around = []
    for ep in range(ep_n):
        prev, follow = halo[0, ep, :half], halo[1, ep, :half]
        around.append(jnp.concatenate([
            jnp.where(low_half, prev, pltpu.roll(follow, rows // 2, 1)),
            jnp.where(low_half, pltpu.roll(prev, rows // 2, 1), follow),
        ], axis=0))
    totals.append(unpack(GROUP, around, sigma_row[GROUP]))
    total_pixels.append(pixel_row[GROUP])
    def by_pixel(tile_rows, tile_pixels):
        gathered = jnp.zeros((pixels, rows), F32)
        for row, where in zip(tile_rows, tile_pixels):
            gathered = gathered + jnp.where(where == pixel_level, row, 0.0)
        return jnp.sum(gathered, axis=1, keepdims=True)

    inverse_count = 1.0 / jnp.maximum(by_pixel(totals, total_pixels), 1.0)

    def limits(squares, tile_pixels, wanted):
        sums = by_pixel(squares, tile_pixels)
        spread = HUBER * jnp.sqrt(sums * inverse_count + 1e-06)
        return [
            jnp.maximum(
                jnp.sum(jnp.where(where == pixel_level, spread, 0.0), axis=0, keepdims=True), 1e-3
            )
            for where in wanted
        ]

    def modes_factor():
        high, low = halves(modes_s[...])
        stacked = jnp.concatenate([high, high, low], axis=0).astype(F32)
        stacked = jnp.concatenate(
            [stacked, jnp.zeros((LANES - 3 * order, epochs), F32)], axis=0
        )
        tall_s[...] = stacked.T.astype(BF16)

    def fitted(coef):
        high, low = halves(coef)
        wide = jnp.concatenate(
            [high, low, high, jnp.zeros((LANES - 3 * order, coef.shape[1]), BF16)], axis=0
        )
        return jnp.dot(tall_s[...], wide, preferred_element_type=F32)

    runs = [list(range(t, min(t + 2, tiles))) for t in range(0, tiles, 2)]

    def scaled_residuals():
        squares = []
        for group in runs:
            fit = fitted(jnp.concatenate(
                [coef_s[t * order : (t + 1) * order] for t in group], axis=1
            ))
            for n, t in enumerate(group):
                left = lens[t] - mens[t] * fit[:, n * rows : (n + 1) * rows]
                sres[t] = left
                squares.append(jnp.sum(left * left, axis=0, keepdims=True))
        return squares

    def reach(left, limit, sigma):
        return (sigma * limit) / jnp.maximum(jnp.abs(left), limit)

    for ep in range(ep_n):
        modes_s[:, ep * cols : (ep + 1) * cols] = first[ep]
    modes_factor()

    def iteration(it, carry):
        @pl.when(it > 0)
        def _():
            for t, square in enumerate(scaled_residuals()):
                square_s[t] = square

        limit = limits([square_s[t] for t in range(tiles)], pixel_row, pixel_row)
        modes = modes_s[...]
        outers = left_parts(halves(cyclic_outer(modes)), 1)
        factors = left_parts(halves(modes), 1)
        for group in runs:
            weight, value = [], []
            for t in group:
                factor = reach(sres[t], limit[t], sigma_row[t])
                weight.append(right_parts(halves(mens[t] * factor), 0))
                value.append(right_parts(halves(lens[t] * factor), 0))
            gram = jnp.dot(outers, jnp.concatenate(weight, axis=1), preferred_element_type=F32)
            target = jnp.dot(factors, jnp.concatenate(value, axis=1), preferred_element_type=F32)
            for n, t in enumerate(group):
                at = slice(n * rows, (n + 1) * rows)
                gram_s[t * depth : t * depth + pairs] = gram[:, at]
                gram_s[t * depth + pairs : (t + 1) * depth] = target[:, at]
        solved = damped_solve(lambda row: gram_s[pl.ds(row, tiles, stride=depth), :], order)
        for k in range(order):
            coef_s[pl.ds(k, tiles, stride=order), :] = solved[k]

        limit = limits(scaled_residuals(), pixel_row, pixel_row[:GROUP])
        at = pl.ds(pl.multiple_of(me_e * cols + r * slab, slab), slab)
        weights, values, outers, coefs = [], [], [], []
        for t in range(GROUP):
            factor = reach(sres[t, at], limit[t], sigma_row[t])
            weights.append(halves(mens[t, at] * factor))
            values.append(halves(lens[t, at] * factor))
            coef = coef_s[t * order : (t + 1) * order]
            outers.append(halves(cyclic_outer(coef)))
            coefs.append(halves(coef))

        def beside(parts):
            return [jnp.concatenate([pair[n] for pair in parts], axis=1) for n in range(2)]

        def across(left, right):
            copied = jnp.concatenate([right_parts(beside(right), 1)] * GROUP, axis=0)
            return lax.dot_general(
                left_parts(beside(left), 1), copied, (((1,), (1,)), ((), ())),
                preferred_element_type=F32,
            )

        gram, target = across(outers, weights), across(coefs, values)
        whole = jnp.concatenate(
            [gram, target, jnp.zeros((GROUP * quarter - depth, rows), F32)], axis=0
        )
        packed = whole[:quarter]
        for k in range(1, GROUP):
            packed = jnp.where(lane >= k * slab, whole[k * quarter : (k + 1) * quarter], packed)
        part_send[it] = packed
        copies = []
        for k in range(1, planes):
            copies.append(remote(
                part_send.at[it], part_recv.at[it, k - 1],
                part_sem.at[0, it, k - 1], part_sem.at[1, it, k - 1],
                {"obj": lax.rem(me_o + k * GROUP, obj_n), "ep": me_e},
            ))
            copies[-1].start()
        fill_basis(blocks // 2 + 2 * it)
        for k in range(1, planes):
            copies[k - 1].wait()
            packed = packed + part_recv[it, k - 1]
        gram_s[:quarter] = packed
        for k in range(1, GROUP):
            gram_s[k * quarter : (k + 1) * quarter] = pltpu.roll(packed, rows - k * slab, 1)
        solved = damped_solve(lambda row: gram_s[row : row + 1, :], order)
        for k in range(order):
            solved_s[k : k + 1] = solved[k]
        fresh = pltpu.roll(solved_s[...], r * slab, 1)
        mode_send[it] = fresh
        mode_recv[it, me_e, r] = fresh
        copies = []
        for n, (dr, de) in enumerate(inner):
            copies.append(remote(
                mode_send.at[it], mode_recv.at[it, me_e, r],
                mode_sem.at[0, it, n], mode_sem.at[1, it, n],
                {"obj": q * GROUP + lax.rem(r + dr, GROUP), "ep": lax.rem(me_e + de, ep_n)},
            ))
            copies[-1].start()
        fill_basis(blocks // 2 + 2 * it + 1)
        for copy in copies:
            copy.wait()
        for ep in range(ep_n):
            joined = mode_recv[it, ep, 0]
            for k in range(1, GROUP):
                joined = jnp.where(lane >= k * slab, mode_recv[it, ep, k], joined)
            modes_s[:, ep * cols : (ep + 1) * cols] = joined
        modes_factor()
        return carry

    lax.fori_loop(0, ITERS, iteration, 0)
    own_coef = coef_s[pl.ds(pl.multiple_of(r * order, order), order), :]
    beside = jnp.where(
        me_e < ep_n // 2, jnp.where(r == 0, GROUP, r - 1), r + 1
    )
    side_coef = coef_s[pl.ds(pl.multiple_of(beside * order, order), order), :]
    both_pixels, squares = [], []
    lefts = []
    for t, coef in ((r, own_coef), (beside, side_coef)):
        left = lens[t] - mens[t] * fitted(coef)
        lefts.append(left)
        squares.append(jnp.sum(left * left, axis=0, keepdims=True))
    for t, name in ((r, 0), (beside, 1)):
        chosen = pixel_row[0]
        for k in range(1, tiles):
            chosen = jnp.where(t == k, pixel_row[k], chosen)
        both_pixels.append(chosen)
    own_sigma = sigma_ref[...]
    (limit,) = limits(squares, both_pixels, both_pixels[:1])
    factor = reach(lefts[0], limit, own_sigma)
    final_s[0] = (mens[r] * factor).T.astype(BF16)
    final_s[1] = (lefts[0] * factor).T.astype(BF16)
    own_modes = modes_s[:, pl.ds(pl.multiple_of(me_e * cols, cols), cols)]
    resid_ref[...] = lc_ref[...] - lax.dot_general(
        own_coef, own_modes, (((0,), (0,)), ((), ())),
        precision=HIGHEST, preferred_element_type=F32,
    )
    mine_at = pl.ds(pl.multiple_of(me_e * share, share), share)
    ready_ref[...] = final_s[:, mine_at, :]


def spectrum_kernel(left_ref, ready_ref, basis_ref, resid_hbm, power_hbm, power_s, sems):
    weights, values = ready_ref[0], ready_ref[1]
    blocks, width = power_s.shape[0], power_s.shape[2]
    kept = pltpu.make_async_copy(left_ref, resid_hbm, sems.at[blocks])
    kept.start()
    both = jnp.concatenate([weights, values], axis=0)
    total = jnp.sum(weights.astype(F32), axis=1, keepdims=True)
    level = jnp.sum(values.astype(F32), axis=1, keepdims=True)

    def out(block):
        at = pl.ds(pl.multiple_of(block * width, width), width)
        return pltpu.make_async_copy(power_s.at[block], power_hbm.at[:, at], sems.at[block])

    def spectrum(block, carry):
        power_s[block] = powers(
            jnp.dot(both, basis_ref[block, 0], preferred_element_type=F32),
            jnp.dot(both, basis_ref[block, 1], preferred_element_type=F32),
            jnp.dot(weights, basis_ref[block, 2], preferred_element_type=F32),
            jnp.dot(weights, basis_ref[block, 3], preferred_element_type=F32),
            total,
            level,
        )
        out(block).start()
        return carry

    lax.fori_loop(0, blocks, spectrum, 0, unroll=UNROLL)
    kept.wait()
    for block in range(blocks):
        out(block).wait()


SIN_TERMS = [(-1.0) ** n / math.factorial(2 * n + 1) for n in range(7)]
COS_TERMS = [(-1.0) ** n / math.factorial(2 * n) for n in range(8)]


def series(square, terms):
    value = jnp.full_like(square, terms[-1])
    for term in terms[-2::-1]:
        value = value * square + term
    return value


def basis_of(cycles):
    cycles = cycles - jnp.floor(cycles)
    turn = jnp.where(cycles >= 0.5, cycles - 1.0, cycles)
    angle = (2.0 * math.pi) * (jnp.abs(turn) - 0.25)
    square = angle * angle
    cosine = -angle * series(square, SIN_TERMS)
    size = series(square, COS_TERMS)
    sine = jnp.where(turn < 0.0, -size, size)
    return cosine, sine, 2.0 * cosine * cosine - 1.0, 2.0 * sine * cosine


def powers(by_cos, by_sin, cosine_two, sine_two, total, level):
    count = cosine_two.shape[0]
    cosine, sine = by_cos[:count], by_sin[:count]
    inverse = 1.0 / total
    mean_level = level * inverse
    ycos = by_cos[count:] - mean_level * cosine
    ysin = by_sin[count:] - mean_level * sine
    cc_term = 0.5 * (total + cosine_two) - cosine * cosine * inverse + RIDGE * total
    ss_term = 0.5 * (total - cosine_two) - sine * sine * inverse + RIDGE * total
    cs_term = 0.5 * sine_two - cosine * sine * inverse
    determinant = cc_term * ss_term - cs_term * cs_term
    return (
        ss_term * ycos * ycos + cc_term * ysin * ysin - 2.0 * cs_term * ycos * ysin
    ) / determinant


def per_device(light_curves, valid, pixel, inv_sigma, modes_init, epoch_jitter, freq_index):
    obj_n = lax.axis_size("obj")
    ep_n = lax.axis_size("ep")
    order = modes_init.shape[1]
    rows, cols = light_curves.shape
    share = rows // ep_n
    epochs = epoch_jitter.shape[0]
    planes = obj_n // GROUP
    tiles = GROUP + 1
    half = cols // 2
    depth = order * order // 2 + order // 2 + order
    quarter = -(-depth // (GROUP * SUB)) * SUB
    chips = GROUP // 2 * ep_n
    inner = GROUP * ep_n - 1
    vmem = pl.BlockSpec(memory_space=pltpu.VMEM)
    hbm = pl.BlockSpec(memory_space=pltpu.HBM)
    sem = pltpu.SemaphoreType.DMA
    count = freq_index.shape[0]
    parts = 4 * ITERS
    left, ready, basis = pl.pallas_call(
        functools.partial(detrend_kernel, obj_n, ep_n, order),
        out_shape=(
            jax.ShapeDtypeStruct((rows, cols), F32),
            jax.ShapeDtypeStruct((2, share, epochs), BF16),
            jax.ShapeDtypeStruct((parts, 4, epochs, count // parts), BF16),
        ),
        in_specs=[hbm] * 7,
        out_specs=(vmem,) * 3,
        scratch_shapes=[
            pltpu.VMEM((rows, cols), F32),
            pltpu.VMEM((rows, cols), jnp.int32),
            pltpu.VMEM((1, rows), jnp.int32),
            pltpu.VMEM((1, rows), F32),
            pltpu.VMEM((1, epochs), F32),
            pltpu.VMEM((1, count), jnp.int32),
            pltpu.VMEM((epochs, LANES), F32),
            pltpu.VMEM((ep_n, GROUP, cols + SUB, rows), F32),
            pltpu.VMEM((half + SUB, rows), F32),
            pltpu.VMEM((2, ep_n, half + SUB, rows), F32),
            pltpu.VMEM((ep_n, order, cols), F32),
            pltpu.VMEM((tiles, epochs, rows), F32),
            pltpu.VMEM((tiles, epochs, rows), F32),
            pltpu.VMEM((tiles, epochs, rows), F32),
            pltpu.VMEM((tiles * order, rows), F32),
            pltpu.VMEM((order, epochs), F32),
            pltpu.VMEM((tiles * depth, rows), F32),
            pltpu.VMEM((epochs, LANES), BF16),
            pltpu.VMEM((tiles, 1, rows), F32),
            pltpu.VMEM((ITERS, quarter, rows), F32),
            pltpu.VMEM((ITERS, planes - 1, quarter, rows), F32),
            pltpu.VMEM((order, rows), F32),
            pltpu.VMEM((ITERS, order, rows), F32),
            pltpu.VMEM((ITERS, ep_n, GROUP, order, rows), F32),
            pltpu.VMEM((2, rows, epochs), BF16),
            sem((7,)),
            sem((chips,)),
            sem((chips,)),
            sem((ep_n, GROUP)),
            sem((chips,)),
            sem((ep_n,)),
            sem((2, ep_n)),
            sem((2, ep_n)),
            sem((2, ITERS, planes - 1)),
            sem((2, ITERS, inner)),
        ],
        compiler_params=pltpu.CompilerParams(
            collective_id=0, has_side_effects=True, vmem_limit_bytes=ROOM
        ),
    )(
        *(pltpu.with_memory_space_constraint(given, pltpu.HBM) for given in (
            light_curves, valid, pixel[None], inv_sigma[None], modes_init.T,
            epoch_jitter[None], freq_index[None],
        ))
    )
    return pl.pallas_call(
        spectrum_kernel,
        out_shape=(
            jax.ShapeDtypeStruct((rows, cols), F32),
            jax.ShapeDtypeStruct((share, count), F32),
        ),
        in_specs=[vmem] * 3,
        out_specs=(hbm,) * 2,
        scratch_shapes=[
            pltpu.VMEM((parts, share, count // parts), F32),
            sem((parts + 1,)),
        ],
        compiler_params=pltpu.CompilerParams(vmem_limit_bytes=ROOM // 2),
    )(left, ready, basis)


def solution(mesh):
    in_specs = (P("obj", "ep"), P("obj", "ep"), P("obj"), P("obj"), P("ep", None), P(), P())
    out_specs = (P("obj", "ep"), P(("obj", "ep"), None))
    return jax.shard_map(
        per_device, mesh=mesh, in_specs=in_specs, out_specs=out_specs, check_vma=False
    )
```

```python
import functools
import math

import jax
import jax.numpy as jnp
from jax import lax
from jax.experimental import pallas as pl
from jax.experimental.pallas import tpu as pltpu
from jax.sharding import PartitionSpec as P

ITERS = 2


HUBER = 1.345
DAMP = 2.0
RIDGE = 0.05
HIGHEST = lax.Precision.HIGHEST
LANES = 128
SUB = 8
UNROLL = 4
ROOM = 24 << 20
GROUP = 4
ABSENT = 1e30
F32 = jnp.float32
BF16 = jnp.bfloat16
STRIP = 32
MESH = pl.DeviceIdType.MESH


def halves(values):
    high = values.astype(BF16)
    return high, (values - high.astype(F32)).astype(BF16)


def left_parts(parts, axis):
    return jnp.concatenate([parts[0], parts[1], parts[0]], axis=axis)


def right_parts(parts, axis):
    return jnp.concatenate([parts[0], parts[0], parts[1]], axis=axis)


def cyclic_outer(vectors):
    order = vectors.shape[0]
    parts = [vectors * vectors]
    for shift in range(1, order // 2 + 1):
        turned = jnp.concatenate([vectors[shift:], vectors[:shift]], axis=0)
        part = vectors * turned
        parts.append(part if shift < order // 2 else part[: order // 2])
    return jnp.concatenate(parts, axis=0)


def cyclic_row(i, j, order):
    ahead = (j - i) % order
    if ahead == order // 2:
        return ahead * order + min(i, j)
    return ahead * order + i if ahead < order // 2 else (order - ahead) * order + j


def damped_solve(load, order):
    pairs = order * order // 2 + order // 2
    entry = {}
    for i in range(order):
        for j in range(i + 1):
            entry[i, j] = load(cyclic_row(i, j, order))
        entry[i, i] = entry[i, i] + DAMP
    remain = [load(pairs + i) for i in range(order)]
    factor = {}
    for k in range(order):
        inverse = 1.0 / entry[k, k]
        for i in range(k + 1, order):
            factor[i, k] = entry[i, k] * inverse
            for j in range(k + 1, i + 1):
                entry[i, j] = entry[i, j] - factor[i, k] * entry[j, k]
            remain[i] = remain[i] - factor[i, k] * remain[k]
        remain[k] = remain[k] * inverse
    for k in reversed(range(order)):
        for j in range(k):
            remain[j] = remain[j] - factor[k, j] * remain[k]
    return remain


def as_column(row):
    return jnp.broadcast_to(row, (LANES, row.shape[1])).T


def detrend_kernel(
    obj_n, ep_n, order, lc_hbm, valid_hbm, pixel_hbm, sigma_hbm, modes_hbm,
    jitter_hbm, freq_hbm, resid_ref, ready_ref, basis_s,
    lc_ref, valid_ref, pixel_ref, sigma_ref, jitter_ref, freq_ref, times_s,
    blk, halo_send, halo, first, lens, mens, sres, coef_s, modes_s, gram_s, tall_s, square_s,
    part_send, part_recv, solved_s, mode_send, mode_recv, final_s,
    load_sem, near_sem, forward_sem, blk_sem, halo_out, halo_forward, halo_sem, first_sem,
    part_sem, mode_sem,
):
    me_o, me_e = lax.axis_index("obj"), lax.axis_index("ep")
    rows, cols = lc_ref.shape
    planes = obj_n // GROUP
    q, r = me_o // GROUP, lax.rem(me_o, GROUP)
    p, core = r // 2, lax.rem(r, 2)
    share = rows // ep_n
    epochs = cols * ep_n
    half = cols // 2
    tiles = GROUP + 1
    slab = cols // GROUP
    pairs = order * order // 2 + order // 2
    depth = pairs + order
    quarter = part_send.shape[1]
    pixels = 4 * obj_n

    def device(plane, chip, side, ep):
        return {"obj": plane * GROUP + chip * 2 + side, "ep": ep}

    def remote(src, dst, send, recv, where):
        return pltpu.make_async_remote_copy(
            src_ref=src, dst_ref=dst, send_sem=send, recv_sem=recv,
            device_id=where, device_id_type=MESH,
        )

    chips = sorted(
        ((dp, de) for dp in range(GROUP // 2) for de in range(ep_n)),
        key=lambda step: (min(step[0], 1) + min(step[1], 1)) % 3 * -1,
    )
    inner = [(dr, de) for dr in range(GROUP) for de in range(ep_n) if (dr, de) != (0, 0)]

    def turned(dp, de):
        return lax.rem(p + dp, GROUP // 2), lax.rem(me_e + de, ep_n)

    has_prev, has_next = q > 0, q < planes - 1
    barrier = pltpu.get_barrier_semaphore()

    def greet(where):
        pl.semaphore_signal(barrier, inc=1, device_id=where, device_id_type=MESH)

    for dr, de in inner:
        greet({"obj": q * GROUP + lax.rem(r + dr, GROUP), "ep": lax.rem(me_e + de, ep_n)})
    for k in range(1, planes):
        greet({"obj": lax.rem(me_o + k * GROUP, obj_n), "ep": me_e})
    for there, exists in ((q - 1, has_prev), (q + 1, has_next)):
        @pl.when(exists)
        def _():
            for dp, de in chips:
                chip, ep = turned(dp, de)
                greet(device(there, chip, core, ep))

    loads = [
        pltpu.make_async_copy(source, target, load_sem.at[n])
        for n, (source, target) in enumerate((
            (lc_hbm, lc_ref), (valid_hbm, valid_ref), (pixel_hbm, pixel_ref),
            (sigma_hbm, sigma_ref), (modes_hbm, first.at[me_e]), (jitter_hbm, jitter_ref),
            (freq_hbm, freq_ref),
        ))
    ]
    for load in loads:
        load.start()
    for load in loads:
        load.wait()

    width = basis_s.shape[3]
    times_s[...] = as_column(
        lax.broadcasted_iota(jnp.int32, (1, epochs), 1).astype(F32) + jitter_ref[...]
    )

    def fill_basis(block):
        begin = pl.multiple_of(block * width, width)
        freqs = (freq_ref[:, pl.ds(begin, width)] + 1).astype(F32) / (4.0 * epochs)

        def strip(step, carry):
            at = pl.ds(pl.multiple_of(step * STRIP, STRIP), STRIP)
            times = jnp.concatenate([times_s[at, :]] * (width // LANES), axis=1)
            for kind, values in enumerate(basis_of(times * freqs)):
                basis_s[block, kind, at, :] = values.astype(BF16)
            return carry

        lax.fori_loop(0, epochs // STRIP, strip, 0)

    blocks = basis_s.shape[0]
    lane = lax.broadcasted_iota(jnp.int32, (1, rows), 1)
    low_half = lane < rows // 2
    own = jnp.where(valid_ref[...] != 0, lc_ref[...], ABSENT).T
    marks = jnp.concatenate(
        [pixel_ref[...].astype(F32), sigma_ref[...], jnp.zeros((SUB - 2, rows), F32)], axis=0
    )
    mine = blk.at[me_e, r]
    blk[me_e, r, :cols] = own
    blk[me_e, r, cols:] = marks
    upper, lower = own[:half], own[half:]
    is_last = r == GROUP - 1
    turned_upper, turned_lower = pltpu.roll(upper, rows // 2, 1), pltpu.roll(lower, rows // 2, 1)
    halo_send[:half] = jnp.where(
        is_last,
        jnp.where(low_half, turned_upper, lower),
        jnp.where(low_half, upper, turned_lower),
    )
    halo_send[half:] = jnp.where(is_last, pltpu.roll(marks, rows // 2, 1), marks)
    missing = jnp.concatenate(
        [jnp.full((half, rows), ABSENT, F32), jnp.full((1, rows), -1.0, F32),
         jnp.ones((SUB - 1, rows), F32)], axis=0,
    )
    for kind, exists in ((0, has_prev), (1, has_next)):
        @pl.when(jnp.logical_not(exists))
        def _():
            for ep in range(ep_n):
                halo[kind, ep] = missing

    def early(block, carry):
        fill_basis(block)
        return carry

    lax.fori_loop(0, blocks // 4, early, 0)
    pl.semaphore_wait(
        barrier,
        len(inner) + planes - 1 + len(chips) * (has_prev.astype(jnp.int32) + has_next.astype(jnp.int32)),
    )

    partner = device(q, p, 1 - core, me_e)
    near = []
    for n, (dp, de) in enumerate(chips):
        if (dp, de) != (0, 0):
            chip, ep = turned(dp, de)
            near.append(remote(mine, mine, near_sem.at[n], blk_sem.at[me_e, r], device(q, chip, core, ep)))
            near[-1].start()
    forwards = [remote(mine, mine, forward_sem.at[0], blk_sem.at[me_e, r], partner)]
    forwards[0].start()
    greetings = []
    for de in range(1, ep_n):
        greetings.append(remote(
            first.at[me_e], first.at[me_e], first_sem.at[0, de], first_sem.at[1, me_e],
            device(q, p, core, lax.rem(me_e + de, ep_n)),
        ))
        greetings[-1].start()

    halo_kinds = (
        (0, q + 1, jnp.logical_and(r == GROUP - 1, has_next), has_prev, core == 1),
        (1, q - 1, jnp.logical_and(r == 0, has_prev), has_next, core == 0),
    )

    def halo_copies(kind, there):
        made = []
        for n, (dp, de) in enumerate(chips):
            chip, ep = turned(dp, de)
            made.append(remote(
                halo_send, halo.at[kind, me_e], halo_out.at[n], halo_sem.at[kind, me_e],
                device(there, chip, core, ep),
            ))
        return made

    for kind, there, sends, _, _ in halo_kinds:
        @pl.when(sends)
        def _():
            for copy in halo_copies(kind, there):
                copy.start()

    def late(block, carry):
        fill_basis(block)
        return carry

    lax.fori_loop(blocks // 4, blocks // 2, late, 0)

    def halo_step(kind, ep):
        slot = halo.at[kind, ep]
        return remote(slot, slot, halo_forward.at[ep], halo_sem.at[kind, ep], partner)

    for n, (dp, de) in enumerate(chips):
        if (dp, de) != (0, 0):
            chip, ep = turned(dp, de)
            slot = blk.at[ep, chip * 2 + core]
            forward = remote(slot, slot, forward_sem.at[n], blk_sem.at[ep, chip * 2 + core], partner)
            forward.wait_recv()
            forward.start()
            forwards.append(forward)
    for kind, _, _, arrives, passes in halo_kinds:
        @pl.when(jnp.logical_and(arrives, passes))
        def _():
            for ep in range(ep_n):
                step = halo_step(kind, ep)
                step.wait_recv()
                step.start()

    def unpack(t, values, sigma):
        total = square = jnp.zeros((1, rows), F32)
        for ep, value in enumerate(values):
            seen = value < 0.5 * ABSENT
            scale = jnp.where(seen, sigma, 0.0)
            at = slice(ep * cols, (ep + 1) * cols)
            mens[t, at] = scale
            scaled = value * scale
            lens[t, at] = scaled
            sres[t, at] = scaled
            square = square + jnp.sum(scaled * scaled, axis=0, keepdims=True)
            total = total + jnp.sum(seen.astype(F32), axis=0, keepdims=True)
        square_s[t] = square
        return total

    def unpack_block(side):
        for dp in range(GROUP // 2):
            t = lax.rem(p + dp, GROUP // 2) * 2 + side
            total = unpack(
                t, [blk[ep, t, :cols] for ep in range(ep_n)], blk[0, t, cols + 1 : cols + 2]
            )
            totals.append(total)
            total_pixels.append(blk[0, t, cols : cols + 1])

    totals, total_pixels = [], []
    unpack_block(core)
    for dp, de in chips:
        chip, ep = turned(dp, de)
        slot = blk.at[ep, chip * 2 + 1 - core]
        remote(slot, slot, forward_sem.at[0], blk_sem.at[ep, chip * 2 + 1 - core], partner).wait_recv()
    for kind, _, _, arrives, passes in halo_kinds:
        @pl.when(jnp.logical_and(arrives, jnp.logical_not(passes)))
        def _():
            for ep in range(ep_n):
                halo_step(kind, ep).wait_recv()
    for de in range(1, ep_n):
        ep = lax.rem(me_e + de, ep_n)
        remote(first.at[ep], first.at[ep], first_sem.at[0, de], first_sem.at[1, ep], partner).wait_recv()
    for copy in near + forwards + greetings:
        copy.wait_send()
    for kind, there, sends, _, _ in halo_kinds:
        @pl.when(sends)
        def _():
            for copy in halo_copies(kind, there):
                copy.wait_send()
    for kind, _, _, arrives, passes in halo_kinds:
        @pl.when(jnp.logical_and(arrives, passes))
        def _():
            for ep in range(ep_n):
                halo_step(kind, ep).wait_send()

    unpack_block(1 - core)
    pixel_level = lax.broadcasted_iota(jnp.int32, (pixels, rows), 0).astype(F32)
    marked = [blk[0, t, cols:] for t in range(GROUP)]
    before, after = halo[0, 0, half:], pltpu.roll(halo[1, 0, half:], rows // 2, 1)
    marked.append(jnp.where(low_half, before, after))
    pixel_row = [m[0:1] for m in marked]
    sigma_row = [m[1:2] for m in marked]
    around = []
    for ep in range(ep_n):
        prev, follow = halo[0, ep, :half], halo[1, ep, :half]
        around.append(jnp.concatenate([
            jnp.where(low_half, prev, pltpu.roll(follow, rows // 2, 1)),
            jnp.where(low_half, pltpu.roll(prev, rows // 2, 1), follow),
        ], axis=0))
    totals.append(unpack(GROUP, around, sigma_row[GROUP]))
    total_pixels.append(pixel_row[GROUP])
    def by_pixel(tile_rows, tile_pixels):
        gathered = jnp.zeros((pixels, rows), F32)
        for row, where in zip(tile_rows, tile_pixels):
            gathered = gathered + jnp.where(where == pixel_level, row, 0.0)
        return jnp.sum(gathered, axis=1, keepdims=True)

    inverse_count = 1.0 / jnp.maximum(by_pixel(totals, total_pixels), 1.0)

    def limits(squares, tile_pixels, wanted):
        sums = by_pixel(squares, tile_pixels)
        spread = HUBER * jnp.sqrt(sums * inverse_count + 1e-06)
        return [
            jnp.maximum(
                jnp.sum(jnp.where(where == pixel_level, spread, 0.0), axis=0, keepdims=True), 1e-3
            )
            for where in wanted
        ]

    def modes_factor():
        high, low = halves(modes_s[...])
        stacked = jnp.concatenate([high, high, low], axis=0).astype(F32)
        stacked = jnp.concatenate(
            [stacked, jnp.zeros((LANES - 3 * order, epochs), F32)], axis=0
        )
        tall_s[...] = stacked.T.astype(BF16)

    def fitted(coef):
        high, low = halves(coef)
        wide = jnp.concatenate(
            [high, low, high, jnp.zeros((LANES - 3 * order, coef.shape[1]), BF16)], axis=0
        )
        return jnp.dot(tall_s[...], wide, preferred_element_type=F32)

    runs = [list(range(t, min(t + 2, tiles))) for t in range(0, tiles, 2)]

    def scaled_residuals():
        squares = []
        for group in runs:
            fit = fitted(jnp.concatenate(
                [coef_s[t * order : (t + 1) * order] for t in group], axis=1
            ))
            for n, t in enumerate(group):
                left = lens[t] - mens[t] * fit[:, n * rows : (n + 1) * rows]
                sres[t] = left
                squares.append(jnp.sum(left * left, axis=0, keepdims=True))
        return squares

    def reach(left, limit, sigma):
        return (sigma * limit) / jnp.maximum(jnp.abs(left), limit)

    for ep in range(ep_n):
        modes_s[:, ep * cols : (ep + 1) * cols] = first[ep]
    modes_factor()

    def iteration(it, carry):
        @pl.when(it > 0)
        def _():
            for t, square in enumerate(scaled_residuals()):
                square_s[t] = square

        limit = limits([square_s[t] for t in range(tiles)], pixel_row, pixel_row)
        modes = modes_s[...]
        outers = left_parts(halves(cyclic_outer(modes)), 1)
        factors = left_parts(halves(modes), 1)
        for group in runs:
            weight, value = [], []
            for t in group:
                factor = reach(sres[t], limit[t], sigma_row[t])
                weight.append(right_parts(halves(mens[t] * factor), 0))
                value.append(right_parts(halves(lens[t] * factor), 0))
            gram = jnp.dot(outers, jnp.concatenate(weight, axis=1), preferred_element_type=F32)
            target = jnp.dot(factors, jnp.concatenate(value, axis=1), preferred_element_type=F32)
            for n, t in enumerate(group):
                at = slice(n * rows, (n + 1) * rows)
                gram_s[t * depth : t * depth + pairs] = gram[:, at]
                gram_s[t * depth + pairs : (t + 1) * depth] = target[:, at]
        solved = damped_solve(lambda row: gram_s[pl.ds(row, tiles, stride=depth), :], order)
        for k in range(order):
            coef_s[pl.ds(k, tiles, stride=order), :] = solved[k]

        limit = limits(scaled_residuals(), pixel_row, pixel_row[:GROUP])
        at = pl.ds(pl.multiple_of(me_e * cols + r * slab, slab), slab)
        weights, values, outers, coefs = [], [], [], []
        for t in range(GROUP):
            factor = reach(sres[t, at], limit[t], sigma_row[t])
            weights.append(halves(mens[t, at] * factor))
            values.append(halves(lens[t, at] * factor))
            coef = coef_s[t * order : (t + 1) * order]
            outers.append(halves(cyclic_outer(coef)))
            coefs.append(halves(coef))

        def beside(parts):
            return [jnp.concatenate([pair[n] for pair in parts], axis=1) for n in range(2)]

        def across(left, right):
            copied = jnp.concatenate([right_parts(beside(right), 1)] * GROUP, axis=0)
            return lax.dot_general(
                left_parts(beside(left), 1), copied, (((1,), (1,)), ((), ())),
                preferred_element_type=F32,
            )

        gram, target = across(outers, weights), across(coefs, values)
        whole = jnp.concatenate(
            [gram, target, jnp.zeros((GROUP * quarter - depth, rows), F32)], axis=0
        )
        packed = whole[:quarter]
        for k in range(1, GROUP):
            packed = jnp.where(lane >= k * slab, whole[k * quarter : (k + 1) * quarter], packed)
        part_send[it] = packed
        copies = []
        for k in range(1, planes):
            copies.append(remote(
                part_send.at[it], part_recv.at[it, k - 1],
                part_sem.at[0, it, k - 1], part_sem.at[1, it, k - 1],
                {"obj": lax.rem(me_o + k * GROUP, obj_n), "ep": me_e},
            ))
            copies[-1].start()
        fill_basis(blocks // 2 + 2 * it)
        for k in range(1, planes):
            copies[k - 1].wait()
            packed = packed + part_recv[it, k - 1]
        gram_s[:quarter] = packed
        for k in range(1, GROUP):
            gram_s[k * quarter : (k + 1) * quarter] = pltpu.roll(packed, rows - k * slab, 1)
        solved = damped_solve(lambda row: gram_s[row : row + 1, :], order)
        for k in range(order):
            solved_s[k : k + 1] = solved[k]
        fresh = jnp.where(
            lane < slab, solved_s[: order // 2], pltpu.roll(solved_s[order // 2 :], slab, 1)
        )
        mode_send[it] = fresh
        mode_recv[it, me_e, r] = fresh
        copies = []
        for n, (dr, de) in enumerate(inner):
            copies.append(remote(
                mode_send.at[it], mode_recv.at[it, me_e, r],
                mode_sem.at[0, it, n], mode_sem.at[1, it, n],
                {"obj": q * GROUP + lax.rem(r + dr, GROUP), "ep": lax.rem(me_e + de, ep_n)},
            ))
            copies[-1].start()
        fill_basis(blocks // 2 + 2 * it + 1)
        for copy in copies:
            copy.wait()
        for ep in range(ep_n):
            sent = [mode_recv[it, ep, k] for k in range(GROUP)]
            for part in range(2):
                placed = [
                    sent[k] if k == part else pltpu.roll(sent[k], (k - part) * slab % rows, 1)
                    for k in range(GROUP)
                ]
                whole = placed[0]
                for k in range(1, GROUP):
                    whole = jnp.where(lane >= k * slab, placed[k], whole)
                at = slice(part * order // 2, (part + 1) * order // 2)
                modes_s[at, ep * cols : (ep + 1) * cols] = whole
        modes_factor()
        return carry

    lax.fori_loop(0, ITERS, iteration, 0)
    own_coef = coef_s[pl.ds(pl.multiple_of(r * order, order), order), :]
    beside = jnp.where(
        me_e < ep_n // 2, jnp.where(r == 0, GROUP, r - 1), r + 1
    )
    side_coef = coef_s[pl.ds(pl.multiple_of(beside * order, order), order), :]
    both_pixels, squares = [], []
    lefts = []
    for t, coef in ((r, own_coef), (beside, side_coef)):
        left = lens[t] - mens[t] * fitted(coef)
        lefts.append(left)
        squares.append(jnp.sum(left * left, axis=0, keepdims=True))
    for t, name in ((r, 0), (beside, 1)):
        chosen = pixel_row[0]
        for k in range(1, tiles):
            chosen = jnp.where(t == k, pixel_row[k], chosen)
        both_pixels.append(chosen)
    own_sigma = sigma_ref[...]
    (limit,) = limits(squares, both_pixels, both_pixels[:1])
    factor = reach(lefts[0], limit, own_sigma)
    final_s[0] = (mens[r] * factor).T.astype(BF16)
    final_s[1] = (lefts[0] * factor).T.astype(BF16)
    own_modes = modes_s[:, pl.ds(pl.multiple_of(me_e * cols, cols), cols)]
    resid_ref[...] = lc_ref[...] - lax.dot_general(
        own_coef, own_modes, (((0,), (0,)), ((), ())),
        precision=HIGHEST, preferred_element_type=F32,
    )
    mine_at = pl.ds(pl.multiple_of(me_e * share, share), share)
    ready_ref[...] = final_s[:, mine_at, :]


def spectrum_kernel(left_ref, ready_ref, basis_ref, resid_hbm, power_hbm, power_s, sems):
    weights, values = ready_ref[0], ready_ref[1]
    blocks, width = power_s.shape[0], power_s.shape[2]
    kept = pltpu.make_async_copy(left_ref, resid_hbm, sems.at[blocks])
    kept.start()
    both = jnp.concatenate([weights, values], axis=0)
    total = jnp.sum(weights.astype(F32), axis=1, keepdims=True)
    level = jnp.sum(values.astype(F32), axis=1, keepdims=True)

    def out(block):
        at = pl.ds(pl.multiple_of(block * width, width), width)
        return pltpu.make_async_copy(power_s.at[block], power_hbm.at[:, at], sems.at[block])

    def spectrum(block, carry):
        power_s[block] = powers(
            jnp.dot(both, basis_ref[block, 0], preferred_element_type=F32),
            jnp.dot(both, basis_ref[block, 1], preferred_element_type=F32),
            jnp.dot(weights, basis_ref[block, 2], preferred_element_type=F32),
            jnp.dot(weights, basis_ref[block, 3], preferred_element_type=F32),
            total,
            level,
        )
        out(block).start()
        return carry

    lax.fori_loop(0, blocks, spectrum, 0, unroll=UNROLL)
    kept.wait()
    for block in range(blocks):
        out(block).wait()


SIN_TERMS = [(-1.0) ** n / math.factorial(2 * n + 1) for n in range(7)]
COS_TERMS = [(-1.0) ** n / math.factorial(2 * n) for n in range(8)]


def series(square, terms):
    value = jnp.full_like(square, terms[-1])
    for term in terms[-2::-1]:
        value = value * square + term
    return value


def basis_of(cycles):
    cycles = cycles - jnp.floor(cycles)
    turn = jnp.where(cycles >= 0.5, cycles - 1.0, cycles)
    angle = (2.0 * math.pi) * (jnp.abs(turn) - 0.25)
    square = angle * angle
    cosine = -angle * series(square, SIN_TERMS)
    size = series(square, COS_TERMS)
    sine = jnp.where(turn < 0.0, -size, size)
    return cosine, sine, 2.0 * cosine * cosine - 1.0, 2.0 * sine * cosine


def powers(by_cos, by_sin, cosine_two, sine_two, total, level):
    count = cosine_two.shape[0]
    cosine, sine = by_cos[:count], by_sin[:count]
    inverse = 1.0 / total
    mean_level = level * inverse
    ycos = by_cos[count:] - mean_level * cosine
    ysin = by_sin[count:] - mean_level * sine
    cc_term = 0.5 * (total + cosine_two) - cosine * cosine * inverse + RIDGE * total
    ss_term = 0.5 * (total - cosine_two) - sine * sine * inverse + RIDGE * total
    cs_term = 0.5 * sine_two - cosine * sine * inverse
    determinant = cc_term * ss_term - cs_term * cs_term
    return (
        ss_term * ycos * ycos + cc_term * ysin * ysin - 2.0 * cs_term * ycos * ysin
    ) / determinant


def per_device(light_curves, valid, pixel, inv_sigma, modes_init, epoch_jitter, freq_index):
    obj_n = lax.axis_size("obj")
    ep_n = lax.axis_size("ep")
    order = modes_init.shape[1]
    rows, cols = light_curves.shape
    share = rows // ep_n
    epochs = epoch_jitter.shape[0]
    planes = obj_n // GROUP
    tiles = GROUP + 1
    half = cols // 2
    depth = order * order // 2 + order // 2 + order
    quarter = -(-depth // (GROUP * SUB)) * SUB
    chips = GROUP // 2 * ep_n
    inner = GROUP * ep_n - 1
    vmem = pl.BlockSpec(memory_space=pltpu.VMEM)
    hbm = pl.BlockSpec(memory_space=pltpu.HBM)
    sem = pltpu.SemaphoreType.DMA
    count = freq_index.shape[0]
    parts = 4 * ITERS
    left, ready, basis = pl.pallas_call(
        functools.partial(detrend_kernel, obj_n, ep_n, order),
        out_shape=(
            jax.ShapeDtypeStruct((rows, cols), F32),
            jax.ShapeDtypeStruct((2, share, epochs), BF16),
            jax.ShapeDtypeStruct((parts, 4, epochs, count // parts), BF16),
        ),
        in_specs=[hbm] * 7,
        out_specs=(vmem,) * 3,
        scratch_shapes=[
            pltpu.VMEM((rows, cols), F32),
            pltpu.VMEM((rows, cols), jnp.int32),
            pltpu.VMEM((1, rows), jnp.int32),
            pltpu.VMEM((1, rows), F32),
            pltpu.VMEM((1, epochs), F32),
            pltpu.VMEM((1, count), jnp.int32),
            pltpu.VMEM((epochs, LANES), F32),
            pltpu.VMEM((ep_n, GROUP, cols + SUB, rows), F32),
            pltpu.VMEM((half + SUB, rows), F32),
            pltpu.VMEM((2, ep_n, half + SUB, rows), F32),
            pltpu.VMEM((ep_n, order, cols), F32),
            pltpu.VMEM((tiles, epochs, rows), F32),
            pltpu.VMEM((tiles, epochs, rows), F32),
            pltpu.VMEM((tiles, epochs, rows), F32),
            pltpu.VMEM((tiles * order, rows), F32),
            pltpu.VMEM((order, epochs), F32),
            pltpu.VMEM((tiles * depth, rows), F32),
            pltpu.VMEM((epochs, LANES), BF16),
            pltpu.VMEM((tiles, 1, rows), F32),
            pltpu.VMEM((ITERS, quarter, rows), F32),
            pltpu.VMEM((ITERS, planes - 1, quarter, rows), F32),
            pltpu.VMEM((order, rows), F32),
            pltpu.VMEM((ITERS, order // 2, rows), F32),
            pltpu.VMEM((ITERS, ep_n, GROUP, order // 2, rows), F32),
            pltpu.VMEM((2, rows, epochs), BF16),
            sem((7,)),
            sem((chips,)),
            sem((chips,)),
            sem((ep_n, GROUP)),
            sem((chips,)),
            sem((ep_n,)),
            sem((2, ep_n)),
            sem((2, ep_n)),
            sem((2, ITERS, planes - 1)),
            sem((2, ITERS, inner)),
        ],
        compiler_params=pltpu.CompilerParams(
            collective_id=0, has_side_effects=True, vmem_limit_bytes=ROOM
        ),
    )(
        *(pltpu.with_memory_space_constraint(given, pltpu.HBM) for given in (
            light_curves, valid, pixel[None], inv_sigma[None], modes_init.T,
            epoch_jitter[None], freq_index[None],
        ))
    )
    return pl.pallas_call(
        spectrum_kernel,
        out_shape=(
            jax.ShapeDtypeStruct((rows, cols), F32),
            jax.ShapeDtypeStruct((share, count), F32),
        ),
        in_specs=[vmem] * 3,
        out_specs=(hbm,) * 2,
        scratch_shapes=[
            pltpu.VMEM((parts, share, count // parts), F32),
            sem((parts + 1,)),
        ],
        compiler_params=pltpu.CompilerParams(vmem_limit_bytes=ROOM // 2),
    )(left, ready, basis)


def solution(mesh):
    in_specs = (P("obj", "ep"), P("obj", "ep"), P("obj"), P("obj"), P("ep", None), P(), P())
    out_specs = (P("obj", "ep"), P(("obj", "ep"), None))
    return jax.shard_map(
        per_device, mesh=mesh, in_specs=in_specs, out_specs=out_specs, check_vma=False
    )
```

```python
import functools
import math

import jax
import jax.numpy as jnp
from jax import lax
from jax.experimental import pallas as pl
from jax.experimental.pallas import tpu as pltpu
from jax.sharding import PartitionSpec as P

ITERS = 2


HUBER = 1.345
DAMP = 2.0
RIDGE = 0.05
HIGHEST = lax.Precision.HIGHEST
LANES = 128
SUB = 8
UNROLL = 8
ROOM = 24 << 20
GROUP = 4
ABSENT = 1e30
F32 = jnp.float32
BF16 = jnp.bfloat16
STRIP = 32
MESH = pl.DeviceIdType.MESH


def halves(values):
    high = values.astype(BF16)
    return high, (values - high.astype(F32)).astype(BF16)


def left_parts(parts, axis):
    return jnp.concatenate([parts[0], parts[1], parts[0]], axis=axis)


def right_parts(parts, axis):
    return jnp.concatenate([parts[0], parts[0], parts[1]], axis=axis)


def cyclic_outer(vectors):
    order = vectors.shape[0]
    parts = [vectors * vectors]
    for shift in range(1, order // 2 + 1):
        turned = jnp.concatenate([vectors[shift:], vectors[:shift]], axis=0)
        part = vectors * turned
        parts.append(part if shift < order // 2 else part[: order // 2])
    return jnp.concatenate(parts, axis=0)


def cyclic_row(i, j, order):
    ahead = (j - i) % order
    if ahead == order // 2:
        return ahead * order + min(i, j)
    return ahead * order + i if ahead < order // 2 else (order - ahead) * order + j


def damped_solve(load, order):
    pairs = order * order // 2 + order // 2
    entry = {}
    for i in range(order):
        for j in range(i + 1):
            entry[i, j] = load(cyclic_row(i, j, order))
        entry[i, i] = entry[i, i] + DAMP
    remain = [load(pairs + i) for i in range(order)]
    factor = {}
    for k in range(order):
        inverse = 1.0 / entry[k, k]
        for i in range(k + 1, order):
            factor[i, k] = entry[i, k] * inverse
            for j in range(k + 1, i + 1):
                entry[i, j] = entry[i, j] - factor[i, k] * entry[j, k]
            remain[i] = remain[i] - factor[i, k] * remain[k]
        remain[k] = remain[k] * inverse
    for k in reversed(range(order)):
        for j in range(k):
            remain[j] = remain[j] - factor[k, j] * remain[k]
    return remain


def as_column(row):
    return jnp.broadcast_to(row, (LANES, row.shape[1])).T


def detrend_kernel(
    obj_n, ep_n, order, lc_hbm, valid_hbm, pixel_hbm, sigma_hbm, modes_hbm,
    jitter_hbm, freq_hbm, resid_ref, ready_ref, basis_s,
    lc_ref, valid_ref, pixel_ref, sigma_ref, jitter_ref, freq_ref, times_s,
    blk, halo_send, halo, first, lens, mens, sres, coef_s, modes_s, gram_s, tall_s, square_s, wide_s,
    part_send, part_recv, solved_s, mode_send, mode_recv, final_s,
    load_sem, near_sem, forward_sem, blk_sem, halo_out, halo_forward, halo_sem, first_sem,
    part_sem, mode_sem,
):
    me_o, me_e = lax.axis_index("obj"), lax.axis_index("ep")
    rows, cols = lc_ref.shape
    planes = obj_n // GROUP
    q, r = me_o // GROUP, lax.rem(me_o, GROUP)
    p, core = r // 2, lax.rem(r, 2)
    share = rows // ep_n
    epochs = cols * ep_n
    half = cols // 2
    tiles = GROUP + 1
    slab = cols // GROUP
    pairs = order * order // 2 + order // 2
    depth = pairs + order
    quarter = part_send.shape[1]
    pixels = 4 * obj_n

    def device(plane, chip, side, ep):
        return {"obj": plane * GROUP + chip * 2 + side, "ep": ep}

    def remote(src, dst, send, recv, where):
        return pltpu.make_async_remote_copy(
            src_ref=src, dst_ref=dst, send_sem=send, recv_sem=recv,
            device_id=where, device_id_type=MESH,
        )

    chips = sorted(
        ((dp, de) for dp in range(GROUP // 2) for de in range(ep_n)),
        key=lambda step: (min(step[0], 1) + min(step[1], 1)) % 3 * -1,
    )
    inner = [(dr, de) for dr in range(GROUP) for de in range(ep_n) if (dr, de) != (0, 0)]

    def turned(dp, de):
        return lax.rem(p + dp, GROUP // 2), lax.rem(me_e + de, ep_n)

    has_prev, has_next = q > 0, q < planes - 1
    barrier = pltpu.get_barrier_semaphore()

    def greet(where):
        pl.semaphore_signal(barrier, inc=1, device_id=where, device_id_type=MESH)

    for dr, de in inner:
        greet({"obj": q * GROUP + lax.rem(r + dr, GROUP), "ep": lax.rem(me_e + de, ep_n)})
    for k in range(1, planes):
        greet({"obj": lax.rem(me_o + k * GROUP, obj_n), "ep": me_e})
    for there, exists in ((q - 1, has_prev), (q + 1, has_next)):
        @pl.when(exists)
        def _():
            for dp, de in chips:
                chip, ep = turned(dp, de)
                greet(device(there, chip, core, ep))

    loads = [
        pltpu.make_async_copy(source, target, load_sem.at[n])
        for n, (source, target) in enumerate((
            (lc_hbm, lc_ref), (valid_hbm, valid_ref), (pixel_hbm, pixel_ref),
            (sigma_hbm, sigma_ref), (modes_hbm, first.at[me_e]), (jitter_hbm, jitter_ref),
            (freq_hbm, freq_ref),
        ))
    ]
    for load in loads:
        load.start()
    for load in loads:
        load.wait()

    width = basis_s.shape[3]
    times_s[...] = as_column(
        lax.broadcasted_iota(jnp.int32, (1, epochs), 1).astype(F32) + jitter_ref[...]
    )

    def fill_basis(block):
        begin = block * width if isinstance(block, int) else pl.multiple_of(block * width, width)
        freqs = (freq_ref[:, pl.ds(begin, width)] + 1).astype(F32) / (4.0 * epochs)

        def strip(step, carry):
            at = pl.ds(pl.multiple_of(step * STRIP, STRIP), STRIP)
            times = jnp.concatenate([times_s[at, :]] * (width // LANES), axis=1)
            for kind, values in enumerate(basis_of(times * freqs)):
                basis_s[block, kind, at, :] = values.astype(BF16)
            return carry

        lax.fori_loop(0, epochs // STRIP, strip, 0)

    blocks = basis_s.shape[0]
    lane = lax.broadcasted_iota(jnp.int32, (1, rows), 1)
    low_half = lane < rows // 2
    own = jnp.where(valid_ref[...] != 0, lc_ref[...], ABSENT).T
    marks = jnp.concatenate(
        [pixel_ref[...].astype(F32), sigma_ref[...], jnp.zeros((SUB - 2, rows), F32)], axis=0
    )
    mine = blk.at[me_e, r]
    blk[me_e, r, :cols] = own
    blk[me_e, r, cols:] = marks
    upper, lower = own[:half], own[half:]
    is_last = r == GROUP - 1
    turned_upper, turned_lower = pltpu.roll(upper, rows // 2, 1), pltpu.roll(lower, rows // 2, 1)
    halo_send[:half] = jnp.where(
        is_last,
        jnp.where(low_half, turned_upper, lower),
        jnp.where(low_half, upper, turned_lower),
    )
    halo_send[half:] = jnp.where(is_last, pltpu.roll(marks, rows // 2, 1), marks)
    missing = jnp.concatenate(
        [jnp.full((half, rows), ABSENT, F32), jnp.full((1, rows), -1.0, F32),
         jnp.ones((SUB - 1, rows), F32)], axis=0,
    )
    for kind, exists in ((0, has_prev), (1, has_next)):
        @pl.when(jnp.logical_not(exists))
        def _():
            for ep in range(ep_n):
                halo[kind, ep] = missing

    def early(block, carry):
        fill_basis(block)
        return carry

    lax.fori_loop(0, blocks // 4, early, 0)
    pl.semaphore_wait(
        barrier,
        len(inner) + planes - 1 + len(chips) * (has_prev.astype(jnp.int32) + has_next.astype(jnp.int32)),
    )

    partner = device(q, p, 1 - core, me_e)
    near = []
    for n, (dp, de) in enumerate(chips):
        if (dp, de) != (0, 0):
            chip, ep = turned(dp, de)
            near.append(remote(mine, mine, near_sem.at[n], blk_sem.at[me_e, r], device(q, chip, core, ep)))
            near[-1].start()
    forwards = [remote(mine, mine, forward_sem.at[0], blk_sem.at[me_e, r], partner)]
    forwards[0].start()
    greetings = []
    for de in range(1, ep_n):
        greetings.append(remote(
            first.at[me_e], first.at[me_e], first_sem.at[0, de], first_sem.at[1, me_e],
            device(q, p, core, lax.rem(me_e + de, ep_n)),
        ))
        greetings[-1].start()

    halo_kinds = (
        (0, q + 1, jnp.logical_and(r == GROUP - 1, has_next), has_prev, core == 1),
        (1, q - 1, jnp.logical_and(r == 0, has_prev), has_next, core == 0),
    )

    def halo_copies(kind, there):
        made = []
        for n, (dp, de) in enumerate(chips):
            chip, ep = turned(dp, de)
            made.append(remote(
                halo_send, halo.at[kind, me_e], halo_out.at[n], halo_sem.at[kind, me_e],
                device(there, chip, core, ep),
            ))
        return made

    for kind, there, sends, _, _ in halo_kinds:
        @pl.when(sends)
        def _():
            for copy in halo_copies(kind, there):
                copy.start()

    def late(block, carry):
        fill_basis(block)
        return carry

    lax.fori_loop(blocks // 4, blocks // 2, late, 0)

    def halo_step(kind, ep):
        slot = halo.at[kind, ep]
        return remote(slot, slot, halo_forward.at[ep], halo_sem.at[kind, ep], partner)

    for n, (dp, de) in enumerate(chips):
        if (dp, de) != (0, 0):
            chip, ep = turned(dp, de)
            slot = blk.at[ep, chip * 2 + core]
            forward = remote(slot, slot, forward_sem.at[n], blk_sem.at[ep, chip * 2 + core], partner)
            forward.wait_recv()
            forward.start()
            forwards.append(forward)
    for kind, _, _, arrives, passes in halo_kinds:
        @pl.when(jnp.logical_and(arrives, passes))
        def _():
            for ep in range(ep_n):
                step = halo_step(kind, ep)
                step.wait_recv()
                step.start()

    def unpack(t, values, sigma):
        total = square = jnp.zeros((1, rows), F32)
        for ep, value in enumerate(values):
            seen = value < 0.5 * ABSENT
            scale = jnp.where(seen, sigma, 0.0)
            at = slice(ep * cols, (ep + 1) * cols)
            mens[t, at] = scale
            scaled = value * scale
            lens[t, at] = scaled
            sres[t, at] = scaled
            square = square + jnp.sum(scaled * scaled, axis=0, keepdims=True)
            total = total + jnp.sum(seen.astype(F32), axis=0, keepdims=True)
        square_s[t] = square
        return total

    def unpack_block(side):
        for dp in range(GROUP // 2):
            t = lax.rem(p + dp, GROUP // 2) * 2 + side
            total = unpack(
                t, [blk[ep, t, :cols] for ep in range(ep_n)], blk[0, t, cols + 1 : cols + 2]
            )
            totals.append(total)
            total_pixels.append(blk[0, t, cols : cols + 1])

    def modes_factor():
        high, low = halves(modes_s[...])
        stacked = jnp.concatenate([high, high, low], axis=0).astype(F32)
        stacked = jnp.concatenate(
            [stacked, jnp.zeros((LANES - 3 * order, epochs), F32)], axis=0
        )
        tall_s[...] = stacked.T.astype(BF16)

    for de in range(1, ep_n):
        ep = lax.rem(me_e + de, ep_n)
        remote(first.at[ep], first.at[ep], first_sem.at[0, de], first_sem.at[1, ep], partner).wait_recv()
    wide_s[...] = jnp.zeros_like(wide_s)
    for ep in range(ep_n):
        modes_s[:, ep * cols : (ep + 1) * cols] = first[ep]
    modes_factor()
    totals, total_pixels = [], []
    unpack_block(core)
    for dp, de in chips:
        chip, ep = turned(dp, de)
        slot = blk.at[ep, chip * 2 + 1 - core]
        remote(slot, slot, forward_sem.at[0], blk_sem.at[ep, chip * 2 + 1 - core], partner).wait_recv()
    for kind, _, _, arrives, passes in halo_kinds:
        @pl.when(jnp.logical_and(arrives, jnp.logical_not(passes)))
        def _():
            for ep in range(ep_n):
                halo_step(kind, ep).wait_recv()
    for copy in near + forwards + greetings:
        copy.wait_send()
    for kind, there, sends, _, _ in halo_kinds:
        @pl.when(sends)
        def _():
            for copy in halo_copies(kind, there):
                copy.wait_send()
    for kind, _, _, arrives, passes in halo_kinds:
        @pl.when(jnp.logical_and(arrives, passes))
        def _():
            for ep in range(ep_n):
                halo_step(kind, ep).wait_send()

    unpack_block(1 - core)
    pixel_level = lax.broadcasted_iota(jnp.int32, (pixels, rows), 0).astype(F32)
    marked = [blk[0, t, cols:] for t in range(GROUP)]
    before, after = halo[0, 0, half:], pltpu.roll(halo[1, 0, half:], rows // 2, 1)
    marked.append(jnp.where(low_half, before, after))
    pixel_row = [m[0:1] for m in marked]
    sigma_row = [m[1:2] for m in marked]
    around = []
    for ep in range(ep_n):
        prev, follow = halo[0, ep, :half], halo[1, ep, :half]
        around.append(jnp.concatenate([
            jnp.where(low_half, prev, pltpu.roll(follow, rows // 2, 1)),
            jnp.where(low_half, pltpu.roll(prev, rows // 2, 1), follow),
        ], axis=0))
    totals.append(unpack(GROUP, around, sigma_row[GROUP]))
    total_pixels.append(pixel_row[GROUP])
    def by_pixel(tile_rows, tile_pixels):
        gathered = jnp.zeros((pixels, rows), F32)
        for row, where in zip(tile_rows, tile_pixels):
            gathered = gathered + jnp.where(where == pixel_level, row, 0.0)
        return jnp.sum(gathered, axis=1, keepdims=True)

    inverse_count = 1.0 / jnp.maximum(by_pixel(totals, total_pixels), 1.0)

    def limits(squares, tile_pixels, wanted):
        sums = by_pixel(squares, tile_pixels)
        spread = HUBER * jnp.sqrt(sums * inverse_count + 1e-06)
        return [
            jnp.maximum(
                jnp.sum(jnp.where(where == pixel_level, spread, 0.0), axis=0, keepdims=True), 1e-3
            )
            for where in wanted
        ]

    def widen():
        for t in range(tiles):
            high, low = halves(coef_s[t * order : (t + 1) * order])
            wide_s[t, : 3 * order] = jnp.concatenate([high, low, high], axis=0)

    def fitted(wide):
        return jnp.dot(tall_s[...], wide, preferred_element_type=F32)

    runs = [list(range(t, min(t + 2, tiles))) for t in range(0, tiles, 2)]

    def scaled_residuals():
        squares = []
        for group in runs:
            fit = fitted(jnp.concatenate([wide_s[t] for t in group], axis=1))
            for n, t in enumerate(group):
                left = lens[t] - mens[t] * fit[:, n * rows : (n + 1) * rows]
                sres[t] = left
                squares.append(jnp.sum(left * left, axis=0, keepdims=True))
        return squares

    def reach(left, limit, sigma):
        return (sigma * limit) / jnp.maximum(jnp.abs(left), limit)


    def iteration(it, carry):
        if it > 0:
            for t, square in enumerate(scaled_residuals()):
                square_s[t] = square

        limit = limits([square_s[t] for t in range(tiles)], pixel_row, pixel_row)
        modes = modes_s[...]
        outers = left_parts(halves(cyclic_outer(modes)), 1)
        factors = left_parts(halves(modes), 1)
        for group in runs:
            weight, value = [], []
            for t in group:
                factor = reach(sres[t], limit[t], sigma_row[t])
                weight.append(right_parts(halves(mens[t] * factor), 0))
                value.append(right_parts(halves(lens[t] * factor), 0))
            gram = jnp.dot(outers, jnp.concatenate(weight, axis=1), preferred_element_type=F32)
            target = jnp.dot(factors, jnp.concatenate(value, axis=1), preferred_element_type=F32)
            for n, t in enumerate(group):
                at = slice(n * rows, (n + 1) * rows)
                gram_s[t * depth : t * depth + pairs] = gram[:, at]
                gram_s[t * depth + pairs : (t + 1) * depth] = target[:, at]
        solved = damped_solve(lambda row: gram_s[pl.ds(row, tiles, stride=depth), :], order)
        for k in range(order):
            coef_s[pl.ds(k, tiles, stride=order), :] = solved[k]
        widen()

        limit = limits(scaled_residuals(), pixel_row, pixel_row[:GROUP])
        at = pl.ds(pl.multiple_of(me_e * cols + r * slab, slab), slab)
        weights, values, outers, coefs = [], [], [], []
        for t in range(GROUP):
            factor = reach(sres[t, at], limit[t], sigma_row[t])
            weights.append(halves(mens[t, at] * factor))
            values.append(halves(lens[t, at] * factor))
            coef = coef_s[t * order : (t + 1) * order]
            outers.append(halves(cyclic_outer(coef)))
            coefs.append(halves(coef))

        def beside(parts):
            return [jnp.concatenate([pair[n] for pair in parts], axis=1) for n in range(2)]

        def across(left, right):
            copied = jnp.concatenate([right_parts(beside(right), 1)] * GROUP, axis=0)
            return lax.dot_general(
                left_parts(beside(left), 1), copied, (((1,), (1,)), ((), ())),
                preferred_element_type=F32,
            )

        gram, target = across(outers, weights), across(coefs, values)
        whole = jnp.concatenate(
            [gram, target, jnp.zeros((GROUP * quarter - depth, rows), F32)], axis=0
        )
        packed = whole[:quarter]
        for k in range(1, GROUP):
            packed = jnp.where(lane >= k * slab, whole[k * quarter : (k + 1) * quarter], packed)
        part_send[it] = packed
        copies = []
        for k in range(1, planes):
            copies.append(remote(
                part_send.at[it], part_recv.at[it, k - 1],
                part_sem.at[0, it, k - 1], part_sem.at[1, it, k - 1],
                {"obj": lax.rem(me_o + k * GROUP, obj_n), "ep": me_e},
            ))
            copies[-1].start()
        fill_basis(blocks // 2 + 2 * it)
        for k in range(1, planes):
            copies[k - 1].wait()
            packed = packed + part_recv[it, k - 1]
        gram_s[:quarter] = packed
        for k in range(1, GROUP):
            gram_s[k * quarter : (k + 1) * quarter] = pltpu.roll(packed, rows - k * slab, 1)
        solved = damped_solve(lambda row: gram_s[row : row + 1, :], order)
        for k in range(order):
            solved_s[k : k + 1] = solved[k]
        fresh = jnp.where(
            lane < slab, solved_s[: order // 2], pltpu.roll(solved_s[order // 2 :], slab, 1)
        )
        mode_send[it] = fresh
        mode_recv[it, me_e, r] = fresh
        copies = []
        for n, (dr, de) in enumerate(inner):
            copies.append(remote(
                mode_send.at[it], mode_recv.at[it, me_e, r],
                mode_sem.at[0, it, n], mode_sem.at[1, it, n],
                {"obj": q * GROUP + lax.rem(r + dr, GROUP), "ep": lax.rem(me_e + de, ep_n)},
            ))
            copies[-1].start()
        fill_basis(blocks // 2 + 2 * it + 1)
        for copy in copies:
            copy.wait()
        for ep in range(ep_n):
            sent = [mode_recv[it, ep, k] for k in range(GROUP)]
            for part in range(2):
                placed = [
                    sent[k] if k == part else pltpu.roll(sent[k], (k - part) * slab % rows, 1)
                    for k in range(GROUP)
                ]
                whole = placed[0]
                for k in range(1, GROUP):
                    whole = jnp.where(lane >= k * slab, placed[k], whole)
                at = slice(part * order // 2, (part + 1) * order // 2)
                modes_s[at, ep * cols : (ep + 1) * cols] = whole
        modes_factor()
        return carry

    for it in range(ITERS):
        iteration(it, 0)
    own_coef = coef_s[pl.ds(pl.multiple_of(r * order, order), order), :]
    beside = jnp.where(
        me_e < ep_n // 2, jnp.where(r == 0, GROUP, r - 1), r + 1
    )
    both_pixels, squares = [], []
    lefts = []
    for t in (r, beside):
        left = lens[t] - mens[t] * fitted(wide_s[t])
        lefts.append(left)
        squares.append(jnp.sum(left * left, axis=0, keepdims=True))
    for t, name in ((r, 0), (beside, 1)):
        chosen = pixel_row[0]
        for k in range(1, tiles):
            chosen = jnp.where(t == k, pixel_row[k], chosen)
        both_pixels.append(chosen)
    own_sigma = sigma_ref[...]
    (limit,) = limits(squares, both_pixels, both_pixels[:1])
    factor = reach(lefts[0], limit, own_sigma)
    final_s[0] = (mens[r] * factor).T.astype(BF16)
    final_s[1] = (lefts[0] * factor).T.astype(BF16)
    own_modes = modes_s[:, pl.ds(pl.multiple_of(me_e * cols, cols), cols)]
    resid_ref[...] = lc_ref[...] - lax.dot_general(
        own_coef, own_modes, (((0,), (0,)), ((), ())),
        precision=HIGHEST, preferred_element_type=F32,
    )
    mine_at = pl.ds(pl.multiple_of(me_e * share, share), share)
    ready_ref[...] = final_s[:, mine_at, :]


def spectrum_kernel(left_ref, ready_ref, basis_ref, resid_hbm, power_hbm, power_s, sems):
    weights, values = ready_ref[0], ready_ref[1]
    blocks, width = power_s.shape[0], power_s.shape[2]
    kept = pltpu.make_async_copy(left_ref, resid_hbm, sems.at[blocks])
    kept.start()
    both = jnp.concatenate([weights, values], axis=0)
    total = jnp.sum(weights.astype(F32), axis=1, keepdims=True)
    level = jnp.sum(values.astype(F32), axis=1, keepdims=True)

    def out(block):
        at = pl.ds(pl.multiple_of(block * width, width), width)
        return pltpu.make_async_copy(power_s.at[block], power_hbm.at[:, at], sems.at[block])

    def spectrum(block, carry):
        power_s[block] = powers(
            jnp.dot(both, basis_ref[block, 0], preferred_element_type=F32),
            jnp.dot(both, basis_ref[block, 1], preferred_element_type=F32),
            jnp.dot(weights, basis_ref[block, 2], preferred_element_type=F32),
            jnp.dot(weights, basis_ref[block, 3], preferred_element_type=F32),
            total,
            level,
        )
        out(block).start()
        return carry

    lax.fori_loop(0, blocks, spectrum, 0, unroll=UNROLL)
    kept.wait()
    for block in range(blocks):
        out(block).wait()


SIN_TERMS = [(-1.0) ** n / math.factorial(2 * n + 1) for n in range(7)]
COS_TERMS = [(-1.0) ** n / math.factorial(2 * n) for n in range(8)]


def series(square, terms):
    value = jnp.full_like(square, terms[-1])
    for term in terms[-2::-1]:
        value = value * square + term
    return value


def basis_of(cycles):
    cycles = cycles - jnp.floor(cycles)
    turn = jnp.where(cycles >= 0.5, cycles - 1.0, cycles)
    angle = (2.0 * math.pi) * (jnp.abs(turn) - 0.25)
    square = angle * angle
    cosine = -angle * series(square, SIN_TERMS)
    size = series(square, COS_TERMS)
    sine = jnp.where(turn < 0.0, -size, size)
    return cosine, sine, 2.0 * cosine * cosine - 1.0, 2.0 * sine * cosine


def powers(by_cos, by_sin, cosine_two, sine_two, total, level):
    count = cosine_two.shape[0]
    cosine, sine = by_cos[:count], by_sin[:count]
    inverse = 1.0 / total
    mean_level = level * inverse
    ycos = by_cos[count:] - mean_level * cosine
    ysin = by_sin[count:] - mean_level * sine
    cc_term = 0.5 * (total + cosine_two) - cosine * cosine * inverse + RIDGE * total
    ss_term = 0.5 * (total - cosine_two) - sine * sine * inverse + RIDGE * total
    cs_term = 0.5 * sine_two - cosine * sine * inverse
    determinant = cc_term * ss_term - cs_term * cs_term
    return (
        ss_term * ycos * ycos + cc_term * ysin * ysin - 2.0 * cs_term * ycos * ysin
    ) / determinant


def per_device(light_curves, valid, pixel, inv_sigma, modes_init, epoch_jitter, freq_index):
    obj_n = lax.axis_size("obj")
    ep_n = lax.axis_size("ep")
    order = modes_init.shape[1]
    rows, cols = light_curves.shape
    share = rows // ep_n
    epochs = epoch_jitter.shape[0]
    planes = obj_n // GROUP
    tiles = GROUP + 1
    half = cols // 2
    depth = order * order // 2 + order // 2 + order
    quarter = -(-depth // (GROUP * SUB)) * SUB
    chips = GROUP // 2 * ep_n
    inner = GROUP * ep_n - 1
    vmem = pl.BlockSpec(memory_space=pltpu.VMEM)
    hbm = pl.BlockSpec(memory_space=pltpu.HBM)
    sem = pltpu.SemaphoreType.DMA
    count = freq_index.shape[0]
    parts = 4 * ITERS
    left, ready, basis = pl.pallas_call(
        functools.partial(detrend_kernel, obj_n, ep_n, order),
        out_shape=(
            jax.ShapeDtypeStruct((rows, cols), F32),
            jax.ShapeDtypeStruct((2, share, epochs), BF16),
            jax.ShapeDtypeStruct((parts, 4, epochs, count // parts), BF16),
        ),
        in_specs=[hbm] * 7,
        out_specs=(vmem,) * 3,
        scratch_shapes=[
            pltpu.VMEM((rows, cols), F32),
            pltpu.VMEM((rows, cols), jnp.int32),
            pltpu.VMEM((1, rows), jnp.int32),
            pltpu.VMEM((1, rows), F32),
            pltpu.VMEM((1, epochs), F32),
            pltpu.VMEM((1, count), jnp.int32),
            pltpu.VMEM((epochs, LANES), F32),
            pltpu.VMEM((ep_n, GROUP, cols + SUB, rows), F32),
            pltpu.VMEM((half + SUB, rows), F32),
            pltpu.VMEM((2, ep_n, half + SUB, rows), F32),
            pltpu.VMEM((ep_n, order, cols), F32),
            pltpu.VMEM((tiles, epochs, rows), F32),
            pltpu.VMEM((tiles, epochs, rows), F32),
            pltpu.VMEM((tiles, epochs, rows), F32),
            pltpu.VMEM((tiles * order, rows), F32),
            pltpu.VMEM((order, epochs), F32),
            pltpu.VMEM((tiles * depth, rows), F32),
            pltpu.VMEM((epochs, LANES), BF16),
            pltpu.VMEM((tiles, 1, rows), F32),
            pltpu.VMEM((tiles, LANES, rows), BF16),
            pltpu.VMEM((ITERS, quarter, rows), F32),
            pltpu.VMEM((ITERS, planes - 1, quarter, rows), F32),
            pltpu.VMEM((order, rows), F32),
            pltpu.VMEM((ITERS, order // 2, rows), F32),
            pltpu.VMEM((ITERS, ep_n, GROUP, order // 2, rows), F32),
            pltpu.VMEM((2, rows, epochs), BF16),
            sem((7,)),
            sem((chips,)),
            sem((chips,)),
            sem((ep_n, GROUP)),
            sem((chips,)),
            sem((ep_n,)),
            sem((2, ep_n)),
            sem((2, ep_n)),
            sem((2, ITERS, planes - 1)),
            sem((2, ITERS, inner)),
        ],
        compiler_params=pltpu.CompilerParams(
            collective_id=0, has_side_effects=True, vmem_limit_bytes=ROOM
        ),
    )(
        *(pltpu.with_memory_space_constraint(given, pltpu.HBM) for given in (
            light_curves, valid, pixel[None], inv_sigma[None], modes_init.T,
            epoch_jitter[None], freq_index[None],
        ))
    )
    return pl.pallas_call(
        spectrum_kernel,
        out_shape=(
            jax.ShapeDtypeStruct((rows, cols), F32),
            jax.ShapeDtypeStruct((share, count), F32),
        ),
        in_specs=[vmem] * 3,
        out_specs=(hbm,) * 2,
        scratch_shapes=[
            pltpu.VMEM((parts, share, count // parts), F32),
            sem((parts + 1,)),
        ],
        compiler_params=pltpu.CompilerParams(vmem_limit_bytes=ROOM // 2),
    )(left, ready, basis)


def solution(mesh):
    in_specs = (P("obj", "ep"), P("obj", "ep"), P("obj"), P("obj"), P("ep", None), P(), P())
    out_specs = (P("obj", "ep"), P(("obj", "ep"), None))
    return jax.shard_map(
        per_device, mesh=mesh, in_specs=in_specs, out_specs=out_specs, check_vma=False
    )
```

```python
import functools
import math

import jax
import jax.numpy as jnp
from jax import lax
from jax.experimental import pallas as pl
from jax.experimental.pallas import tpu as pltpu
from jax.sharding import PartitionSpec as P

ITERS = 2


HUBER = 1.345
DAMP = 2.0
RIDGE = 0.05
HIGHEST = lax.Precision.HIGHEST
LANES = 128
SUB = 8
UNROLL = 8
ROOM = 24 << 20
GROUP = 4
ABSENT = 1e30
F32 = jnp.float32
BF16 = jnp.bfloat16
STRIP = 32
MESH = pl.DeviceIdType.MESH


def halves(values):
    high = values.astype(BF16)
    return high, (values - high.astype(F32)).astype(BF16)


def left_parts(parts, axis):
    return jnp.concatenate([parts[0], parts[1], parts[0]], axis=axis)


def right_parts(parts, axis):
    return jnp.concatenate([parts[0], parts[0], parts[1]], axis=axis)


def cyclic_outer(vectors):
    order = vectors.shape[0]
    parts = [vectors * vectors]
    for shift in range(1, order // 2 + 1):
        turned = jnp.concatenate([vectors[shift:], vectors[:shift]], axis=0)
        part = vectors * turned
        parts.append(part if shift < order // 2 else part[: order // 2])
    return jnp.concatenate(parts, axis=0)


def cyclic_row(i, j, order):
    ahead = (j - i) % order
    if ahead == order // 2:
        return ahead * order + min(i, j)
    return ahead * order + i if ahead < order // 2 else (order - ahead) * order + j


def damped_solve(load, order):
    pairs = order * order // 2 + order // 2
    entry = {}
    for i in range(order):
        for j in range(i + 1):
            entry[i, j] = load(cyclic_row(i, j, order))
        entry[i, i] = entry[i, i] + DAMP
    remain = [load(pairs + i) for i in range(order)]
    factor = {}
    for k in range(order):
        inverse = 1.0 / entry[k, k]
        for i in range(k + 1, order):
            factor[i, k] = entry[i, k] * inverse
            for j in range(k + 1, i + 1):
                entry[i, j] = entry[i, j] - factor[i, k] * entry[j, k]
            remain[i] = remain[i] - factor[i, k] * remain[k]
        remain[k] = remain[k] * inverse
    for k in reversed(range(order)):
        for j in range(k):
            remain[j] = remain[j] - factor[k, j] * remain[k]
    return remain


def as_column(row):
    return jnp.broadcast_to(row, (LANES, row.shape[1])).T


def detrend_kernel(
    obj_n, ep_n, order, lc_hbm, valid_hbm, pixel_hbm, sigma_hbm, modes_hbm,
    jitter_hbm, freq_hbm, resid_ref, ready_ref, basis_s,
    lc_ref, valid_ref, pixel_ref, sigma_ref, jitter_ref, freq_ref, times_s,
    blk, halo_send, halo, first, lens, mens, sres, coef_s, modes_s, gram_s, tall_s, square_s, wide_s,
    part_send, part_recv, solved_s, mode_send, mode_recv, final_s,
    load_sem, near_sem, forward_sem, blk_sem, halo_out, halo_forward, halo_sem, first_sem,
    part_sem, mode_sem,
):
    me_o, me_e = lax.axis_index("obj"), lax.axis_index("ep")
    rows, cols = lc_ref.shape
    planes = obj_n // GROUP
    q, r = me_o // GROUP, lax.rem(me_o, GROUP)
    p, core = r // 2, lax.rem(r, 2)
    share = rows // ep_n
    epochs = cols * ep_n
    half = cols // 2
    tiles = GROUP + 1
    slab = cols // GROUP
    pairs = order * order // 2 + order // 2
    depth = pairs + order
    quarter = part_send.shape[1]
    pixels = 4 * obj_n

    def device(plane, chip, side, ep):
        return {"obj": plane * GROUP + chip * 2 + side, "ep": ep}

    def remote(src, dst, send, recv, where):
        return pltpu.make_async_remote_copy(
            src_ref=src, dst_ref=dst, send_sem=send, recv_sem=recv,
            device_id=where, device_id_type=MESH,
        )

    chips = sorted(
        ((dp, de) for dp in range(GROUP // 2) for de in range(ep_n)),
        key=lambda step: (min(step[0], 1) + min(step[1], 1)) % 3 * -1,
    )
    inner = [(dr, de) for dr in range(GROUP) for de in range(ep_n) if (dr, de) != (0, 0)]

    def turned(dp, de):
        return lax.rem(p + dp, GROUP // 2), lax.rem(me_e + de, ep_n)

    has_prev, has_next = q > 0, q < planes - 1
    barrier = pltpu.get_barrier_semaphore()

    def greet(where):
        pl.semaphore_signal(barrier, inc=1, device_id=where, device_id_type=MESH)

    for dr, de in inner:
        greet({"obj": q * GROUP + lax.rem(r + dr, GROUP), "ep": lax.rem(me_e + de, ep_n)})
    for k in range(1, planes):
        greet({"obj": lax.rem(me_o + k * GROUP, obj_n), "ep": me_e})
    for there, exists in ((q - 1, has_prev), (q + 1, has_next)):
        @pl.when(exists)
        def _():
            for dp, de in chips:
                chip, ep = turned(dp, de)
                greet(device(there, chip, core, ep))

    loads = [
        pltpu.make_async_copy(source, target, load_sem.at[n])
        for n, (source, target) in enumerate((
            (lc_hbm, lc_ref), (valid_hbm, valid_ref), (pixel_hbm, pixel_ref),
            (sigma_hbm, sigma_ref), (modes_hbm, first.at[me_e]), (jitter_hbm, jitter_ref),
            (freq_hbm, freq_ref),
        ))
    ]
    for load in loads:
        load.start()
    for load in loads:
        load.wait()

    width = basis_s.shape[3]
    times_s[...] = as_column(
        lax.broadcasted_iota(jnp.int32, (1, epochs), 1).astype(F32) + jitter_ref[...]
    )

    def fill_basis(block):
        begin = block * width if isinstance(block, int) else pl.multiple_of(block * width, width)
        freqs = (freq_ref[:, pl.ds(begin, width)] + 1).astype(F32) / (4.0 * epochs)

        def strip(step, carry):
            at = pl.ds(pl.multiple_of(step * STRIP, STRIP), STRIP)
            times = jnp.concatenate([times_s[at, :]] * (width // LANES), axis=1)
            for kind, values in enumerate(basis_of(times * freqs)):
                basis_s[block, kind, at, :] = values.astype(BF16)
            return carry

        lax.fori_loop(0, epochs // STRIP, strip, 0)

    blocks = basis_s.shape[0]
    lane = lax.broadcasted_iota(jnp.int32, (1, rows), 1)
    low_half = lane < rows // 2
    own = jnp.where(valid_ref[...] != 0, lc_ref[...], ABSENT).T
    marks = jnp.concatenate(
        [pixel_ref[...].astype(F32), sigma_ref[...], jnp.zeros((SUB - 2, rows), F32)], axis=0
    )
    mine = blk.at[me_e, r]
    blk[me_e, r, :cols] = own
    blk[me_e, r, cols:] = marks
    upper, lower = own[:half], own[half:]
    is_last = r == GROUP - 1
    turned_upper, turned_lower = pltpu.roll(upper, rows // 2, 1), pltpu.roll(lower, rows // 2, 1)
    halo_send[:half] = jnp.where(
        is_last,
        jnp.where(low_half, turned_upper, lower),
        jnp.where(low_half, upper, turned_lower),
    )
    halo_send[half:] = jnp.where(is_last, pltpu.roll(marks, rows // 2, 1), marks)
    missing = jnp.concatenate(
        [jnp.full((half, rows), ABSENT, F32), jnp.full((1, rows), -1.0, F32),
         jnp.ones((SUB - 1, rows), F32)], axis=0,
    )
    for kind, exists in ((0, has_prev), (1, has_next)):
        @pl.when(jnp.logical_not(exists))
        def _():
            for ep in range(ep_n):
                halo[kind, ep] = missing

    def early(block, carry):
        fill_basis(block)
        return carry

    lax.fori_loop(0, blocks // 4, early, 0)
    pl.semaphore_wait(
        barrier,
        len(inner) + planes - 1 + len(chips) * (has_prev.astype(jnp.int32) + has_next.astype(jnp.int32)),
    )

    partner = device(q, p, 1 - core, me_e)
    near = []
    for n, (dp, de) in enumerate(chips):
        if (dp, de) != (0, 0):
            chip, ep = turned(dp, de)
            near.append(remote(mine, mine, near_sem.at[n], blk_sem.at[me_e, r], device(q, chip, core, ep)))
            near[-1].start()
    forwards = [remote(mine, mine, forward_sem.at[0], blk_sem.at[me_e, r], partner)]
    forwards[0].start()
    greetings = []
    for de in range(1, ep_n):
        greetings.append(remote(
            first.at[me_e], first.at[me_e], first_sem.at[0, de], first_sem.at[1, me_e],
            device(q, p, core, lax.rem(me_e + de, ep_n)),
        ))
        greetings[-1].start()

    halo_kinds = (
        (0, q + 1, jnp.logical_and(r == GROUP - 1, has_next), has_prev, core == 1),
        (1, q - 1, jnp.logical_and(r == 0, has_prev), has_next, core == 0),
    )

    def halo_copies(kind, there):
        made = []
        for n, (dp, de) in enumerate(chips):
            chip, ep = turned(dp, de)
            made.append(remote(
                halo_send, halo.at[kind, me_e], halo_out.at[n], halo_sem.at[kind, me_e],
                device(there, chip, core, ep),
            ))
        return made

    for kind, there, sends, _, _ in halo_kinds:
        @pl.when(sends)
        def _():
            for copy in halo_copies(kind, there):
                copy.start()

    def late(block, carry):
        fill_basis(block)
        return carry

    lax.fori_loop(blocks // 4, blocks // 2, late, 0)

    def halo_step(kind, ep):
        slot = halo.at[kind, ep]
        return remote(slot, slot, halo_forward.at[ep], halo_sem.at[kind, ep], partner)

    for n, (dp, de) in enumerate(chips):
        if (dp, de) != (0, 0):
            chip, ep = turned(dp, de)
            slot = blk.at[ep, chip * 2 + core]
            forward = remote(slot, slot, forward_sem.at[n], blk_sem.at[ep, chip * 2 + core], partner)
            forward.wait_recv()
            forward.start()
            forwards.append(forward)
    for kind, _, _, arrives, passes in halo_kinds:
        @pl.when(jnp.logical_and(arrives, passes))
        def _():
            for ep in range(ep_n):
                step = halo_step(kind, ep)
                step.wait_recv()
                step.start()

    def unpack(t, values, sigma):
        total = square = jnp.zeros((1, rows), F32)
        for ep, value in enumerate(values):
            seen = value < 0.5 * ABSENT
            scale = jnp.where(seen, sigma, 0.0)
            at = slice(ep * cols, (ep + 1) * cols)
            mens[t, at] = scale
            scaled = value * scale
            lens[t, at] = scaled
            sres[t, at] = scaled
            square = square + jnp.sum(scaled * scaled, axis=0, keepdims=True)
            total = total + jnp.sum(seen.astype(F32), axis=0, keepdims=True)
        square_s[t] = square
        return total

    def unpack_block(side):
        for dp in range(GROUP // 2):
            t = lax.rem(p + dp, GROUP // 2) * 2 + side
            total = unpack(
                t, [blk[ep, t, :cols] for ep in range(ep_n)], blk[0, t, cols + 1 : cols + 2]
            )
            totals.append(total)
            total_pixels.append(blk[0, t, cols : cols + 1])

    def modes_factor():
        high, low = halves(modes_s[...])
        stacked = jnp.concatenate([high, high, low], axis=0).astype(F32)
        stacked = jnp.concatenate(
            [stacked, jnp.zeros((LANES - 3 * order, epochs), F32)], axis=0
        )
        tall_s[...] = stacked.T.astype(BF16)

    for de in range(1, ep_n):
        ep = lax.rem(me_e + de, ep_n)
        remote(first.at[ep], first.at[ep], first_sem.at[0, de], first_sem.at[1, ep], partner).wait_recv()
    wide_s[...] = jnp.zeros_like(wide_s)
    for ep in range(ep_n):
        modes_s[:, ep * cols : (ep + 1) * cols] = first[ep]
    modes_factor()
    totals, total_pixels = [], []
    unpack_block(core)
    for dp, de in chips:
        chip, ep = turned(dp, de)
        slot = blk.at[ep, chip * 2 + 1 - core]
        remote(slot, slot, forward_sem.at[0], blk_sem.at[ep, chip * 2 + 1 - core], partner).wait_recv()
    for kind, _, _, arrives, passes in halo_kinds:
        @pl.when(jnp.logical_and(arrives, jnp.logical_not(passes)))
        def _():
            for ep in range(ep_n):
                halo_step(kind, ep).wait_recv()
    unpack_block(1 - core)
    pixel_level = lax.broadcasted_iota(jnp.int32, (pixels, rows), 0).astype(F32)
    marked = [blk[0, t, cols:] for t in range(GROUP)]
    before, after = halo[0, 0, half:], pltpu.roll(halo[1, 0, half:], rows // 2, 1)
    marked.append(jnp.where(low_half, before, after))
    pixel_row = [m[0:1] for m in marked]
    sigma_row = [m[1:2] for m in marked]
    around = []
    for ep in range(ep_n):
        prev, follow = halo[0, ep, :half], halo[1, ep, :half]
        around.append(jnp.concatenate([
            jnp.where(low_half, prev, pltpu.roll(follow, rows // 2, 1)),
            jnp.where(low_half, pltpu.roll(prev, rows // 2, 1), follow),
        ], axis=0))
    totals.append(unpack(GROUP, around, sigma_row[GROUP]))
    total_pixels.append(pixel_row[GROUP])
    def by_pixel(tile_rows, tile_pixels):
        gathered = jnp.zeros((pixels, rows), F32)
        for row, where in zip(tile_rows, tile_pixels):
            gathered = gathered + jnp.where(where == pixel_level, row, 0.0)
        return jnp.sum(gathered, axis=1, keepdims=True)

    inverse_count = 1.0 / jnp.maximum(by_pixel(totals, total_pixels), 1.0)

    def limits(squares, tile_pixels, wanted):
        sums = by_pixel(squares, tile_pixels)
        spread = HUBER * jnp.sqrt(sums * inverse_count + 1e-06)
        return [
            jnp.maximum(
                jnp.sum(jnp.where(where == pixel_level, spread, 0.0), axis=0, keepdims=True), 1e-3
            )
            for where in wanted
        ]

    def widen():
        for t in range(tiles):
            high, low = halves(coef_s[t * order : (t + 1) * order])
            wide_s[t, : 3 * order] = jnp.concatenate([high, low, high], axis=0)

    def fitted(wide):
        return jnp.dot(tall_s[...], wide, preferred_element_type=F32)

    runs = [list(range(t, min(t + 2, tiles))) for t in range(0, tiles, 2)]

    def scaled_residuals():
        squares = []
        for group in runs:
            fit = fitted(jnp.concatenate([wide_s[t] for t in group], axis=1))
            for n, t in enumerate(group):
                left = lens[t] - mens[t] * fit[:, n * rows : (n + 1) * rows]
                sres[t] = left
                squares.append(jnp.sum(left * left, axis=0, keepdims=True))
        return squares

    def reach(left, limit, sigma):
        return (sigma * limit) / jnp.maximum(jnp.abs(left), limit)


    def iteration(it, carry):
        if it > 0:
            for t, square in enumerate(scaled_residuals()):
                square_s[t] = square

        limit = limits([square_s[t] for t in range(tiles)], pixel_row, pixel_row)
        modes = modes_s[...]
        outers = left_parts(halves(cyclic_outer(modes)), 1)
        factors = left_parts(halves(modes), 1)
        for group in runs:
            weight, value = [], []
            for t in group:
                factor = reach(sres[t], limit[t], sigma_row[t])
                weight.append(right_parts(halves(mens[t] * factor), 0))
                value.append(right_parts(halves(lens[t] * factor), 0))
            gram = jnp.dot(outers, jnp.concatenate(weight, axis=1), preferred_element_type=F32)
            target = jnp.dot(factors, jnp.concatenate(value, axis=1), preferred_element_type=F32)
            for n, t in enumerate(group):
                at = slice(n * rows, (n + 1) * rows)
                gram_s[t * depth : t * depth + pairs] = gram[:, at]
                gram_s[t * depth + pairs : (t + 1) * depth] = target[:, at]
        solved = damped_solve(lambda row: gram_s[pl.ds(row, tiles, stride=depth), :], order)
        for k in range(order):
            coef_s[pl.ds(k, tiles, stride=order), :] = solved[k]
        widen()

        limit = limits(scaled_residuals(), pixel_row, pixel_row[:GROUP])
        at = pl.ds(pl.multiple_of(me_e * cols + r * slab, slab), slab)
        weights, values, outers, coefs = [], [], [], []
        for t in range(GROUP):
            factor = reach(sres[t, at], limit[t], sigma_row[t])
            weights.append(halves(mens[t, at] * factor))
            values.append(halves(lens[t, at] * factor))
            coef = coef_s[t * order : (t + 1) * order]
            outers.append(halves(cyclic_outer(coef)))
            coefs.append(halves(coef))

        def beside(parts):
            return [jnp.concatenate([pair[n] for pair in parts], axis=1) for n in range(2)]

        def across(left, right):
            copied = jnp.concatenate([right_parts(beside(right), 1)] * GROUP, axis=0)
            return lax.dot_general(
                left_parts(beside(left), 1), copied, (((1,), (1,)), ((), ())),
                preferred_element_type=F32,
            )

        gram, target = across(outers, weights), across(coefs, values)
        whole = jnp.concatenate(
            [gram, target, jnp.zeros((GROUP * quarter - depth, rows), F32)], axis=0
        )
        packed = whole[:quarter]
        for k in range(1, GROUP):
            packed = jnp.where(lane >= k * slab, whole[k * quarter : (k + 1) * quarter], packed)
        part_send[it] = packed
        copies = []
        for k in range(1, planes):
            copies.append(remote(
                part_send.at[it], part_recv.at[it, k - 1],
                part_sem.at[0, it, k - 1], part_sem.at[1, it, k - 1],
                {"obj": lax.rem(me_o + k * GROUP, obj_n), "ep": me_e},
            ))
            copies[-1].start()
        fill_basis(blocks // 2 + 2 * it)
        for k in range(1, planes):
            copies[k - 1].wait_recv()
            packed = packed + part_recv[it, k - 1]
        sent.extend(copies)
        gram_s[:quarter] = packed
        for k in range(1, GROUP):
            gram_s[k * quarter : (k + 1) * quarter] = pltpu.roll(packed, rows - k * slab, 1)
        solved = damped_solve(lambda row: gram_s[row : row + 1, :], order)
        for k in range(order):
            solved_s[k : k + 1] = solved[k]
        fresh = jnp.where(
            lane < slab, solved_s[: order // 2], pltpu.roll(solved_s[order // 2 :], slab, 1)
        )
        mode_send[it] = fresh
        mode_recv[it, me_e, r] = fresh
        copies = []
        for n, (dr, de) in enumerate(inner):
            copies.append(remote(
                mode_send.at[it], mode_recv.at[it, me_e, r],
                mode_sem.at[0, it, n], mode_sem.at[1, it, n],
                {"obj": q * GROUP + lax.rem(r + dr, GROUP), "ep": lax.rem(me_e + de, ep_n)},
            ))
            copies[-1].start()
        fill_basis(blocks // 2 + 2 * it + 1)
        sent.extend(copies)
        for copy in copies:
            copy.wait_recv()
        for ep in range(ep_n):
            heard = [mode_recv[it, ep, k] for k in range(GROUP)]
            for part in range(2):
                placed = [
                    heard[k] if k == part else pltpu.roll(heard[k], (k - part) * slab % rows, 1)
                    for k in range(GROUP)
                ]
                whole = placed[0]
                for k in range(1, GROUP):
                    whole = jnp.where(lane >= k * slab, placed[k], whole)
                at = slice(part * order // 2, (part + 1) * order // 2)
                modes_s[at, ep * cols : (ep + 1) * cols] = whole
        modes_factor()
        return carry

    sent = []
    for it in range(ITERS):
        iteration(it, 0)
    own_coef = coef_s[pl.ds(pl.multiple_of(r * order, order), order), :]
    beside = jnp.where(
        me_e < ep_n // 2, jnp.where(r == 0, GROUP, r - 1), r + 1
    )
    both_pixels, squares = [], []
    lefts = []
    for t in (r, beside):
        left = lens[t] - mens[t] * fitted(wide_s[t])
        lefts.append(left)
        squares.append(jnp.sum(left * left, axis=0, keepdims=True))
    for t, name in ((r, 0), (beside, 1)):
        chosen = pixel_row[0]
        for k in range(1, tiles):
            chosen = jnp.where(t == k, pixel_row[k], chosen)
        both_pixels.append(chosen)
    own_sigma = sigma_ref[...]
    (limit,) = limits(squares, both_pixels, both_pixels[:1])
    factor = reach(lefts[0], limit, own_sigma)
    final_s[0] = (mens[r] * factor).T.astype(BF16)
    final_s[1] = (lefts[0] * factor).T.astype(BF16)
    own_modes = modes_s[:, pl.ds(pl.multiple_of(me_e * cols, cols), cols)]
    resid_ref[...] = lc_ref[...] - lax.dot_general(
        own_coef, own_modes, (((0,), (0,)), ((), ())),
        precision=HIGHEST, preferred_element_type=F32,
    )
    mine_at = pl.ds(pl.multiple_of(me_e * share, share), share)
    ready_ref[...] = final_s[:, mine_at, :]
    for copy in sent:
        copy.wait_send()
    for copy in near + forwards + greetings:
        copy.wait_send()
    for kind, there, sends, _, _ in halo_kinds:
        @pl.when(sends)
        def _():
            for copy in halo_copies(kind, there):
                copy.wait_send()
    for kind, _, _, arrives, passes in halo_kinds:
        @pl.when(jnp.logical_and(arrives, passes))
        def _():
            for ep in range(ep_n):
                halo_step(kind, ep).wait_send()


def spectrum_kernel(left_ref, ready_ref, basis_ref, resid_hbm, power_hbm, power_s, sems):
    weights, values = ready_ref[0], ready_ref[1]
    blocks, width = power_s.shape[0], power_s.shape[2]
    kept = pltpu.make_async_copy(left_ref, resid_hbm, sems.at[blocks])
    kept.start()
    both = jnp.concatenate([weights, values], axis=0)
    total = jnp.sum(weights.astype(F32), axis=1, keepdims=True)
    level = jnp.sum(values.astype(F32), axis=1, keepdims=True)

    def out(block):
        at = pl.ds(pl.multiple_of(block * width, width), width)
        return pltpu.make_async_copy(power_s.at[block], power_hbm.at[:, at], sems.at[block])

    def spectrum(block, carry):
        power_s[block] = powers(
            jnp.dot(both, basis_ref[block, 0], preferred_element_type=F32),
            jnp.dot(both, basis_ref[block, 1], preferred_element_type=F32),
            jnp.dot(weights, basis_ref[block, 2], preferred_element_type=F32),
            jnp.dot(weights, basis_ref[block, 3], preferred_element_type=F32),
            total,
            level,
        )
        out(block).start()
        return carry

    lax.fori_loop(0, blocks, spectrum, 0, unroll=UNROLL)
    kept.wait()
    for block in range(blocks):
        out(block).wait()


SIN_TERMS = [(-1.0) ** n / math.factorial(2 * n + 1) for n in range(7)]
COS_TERMS = [(-1.0) ** n / math.factorial(2 * n) for n in range(8)]


def series(square, terms):
    value = jnp.full_like(square, terms[-1])
    for term in terms[-2::-1]:
        value = value * square + term
    return value


def basis_of(cycles):
    cycles = cycles - jnp.floor(cycles)
    turn = jnp.where(cycles >= 0.5, cycles - 1.0, cycles)
    angle = (2.0 * math.pi) * (jnp.abs(turn) - 0.25)
    square = angle * angle
    cosine = -angle * series(square, SIN_TERMS)
    size = series(square, COS_TERMS)
    sine = jnp.where(turn < 0.0, -size, size)
    return cosine, sine, 2.0 * cosine * cosine - 1.0, 2.0 * sine * cosine


def powers(by_cos, by_sin, cosine_two, sine_two, total, level):
    count = cosine_two.shape[0]
    cosine, sine = by_cos[:count], by_sin[:count]
    inverse = 1.0 / total
    mean_level = level * inverse
    ycos = by_cos[count:] - mean_level * cosine
    ysin = by_sin[count:] - mean_level * sine
    cc_term = 0.5 * (total + cosine_two) - cosine * cosine * inverse + RIDGE * total
    ss_term = 0.5 * (total - cosine_two) - sine * sine * inverse + RIDGE * total
    cs_term = 0.5 * sine_two - cosine * sine * inverse
    determinant = cc_term * ss_term - cs_term * cs_term
    return (
        ss_term * ycos * ycos + cc_term * ysin * ysin - 2.0 * cs_term * ycos * ysin
    ) / determinant


def per_device(light_curves, valid, pixel, inv_sigma, modes_init, epoch_jitter, freq_index):
    obj_n = lax.axis_size("obj")
    ep_n = lax.axis_size("ep")
    order = modes_init.shape[1]
    rows, cols = light_curves.shape
    share = rows // ep_n
    epochs = epoch_jitter.shape[0]
    planes = obj_n // GROUP
    tiles = GROUP + 1
    half = cols // 2
    depth = order * order // 2 + order // 2 + order
    quarter = -(-depth // (GROUP * SUB)) * SUB
    chips = GROUP // 2 * ep_n
    inner = GROUP * ep_n - 1
    vmem = pl.BlockSpec(memory_space=pltpu.VMEM)
    hbm = pl.BlockSpec(memory_space=pltpu.HBM)
    sem = pltpu.SemaphoreType.DMA
    count = freq_index.shape[0]
    parts = 4 * ITERS
    left, ready, basis = pl.pallas_call(
        functools.partial(detrend_kernel, obj_n, ep_n, order),
        out_shape=(
            jax.ShapeDtypeStruct((rows, cols), F32),
            jax.ShapeDtypeStruct((2, share, epochs), BF16),
            jax.ShapeDtypeStruct((parts, 4, epochs, count // parts), BF16),
        ),
        in_specs=[hbm] * 7,
        out_specs=(vmem,) * 3,
        scratch_shapes=[
            pltpu.VMEM((rows, cols), F32),
            pltpu.VMEM((rows, cols), jnp.int32),
            pltpu.VMEM((1, rows), jnp.int32),
            pltpu.VMEM((1, rows), F32),
            pltpu.VMEM((1, epochs), F32),
            pltpu.VMEM((1, count), jnp.int32),
            pltpu.VMEM((epochs, LANES), F32),
            pltpu.VMEM((ep_n, GROUP, cols + SUB, rows), F32),
            pltpu.VMEM((half + SUB, rows), F32),
            pltpu.VMEM((2, ep_n, half + SUB, rows), F32),
            pltpu.VMEM((ep_n, order, cols), F32),
            pltpu.VMEM((tiles, epochs, rows), F32),
            pltpu.VMEM((tiles, epochs, rows), F32),
            pltpu.VMEM((tiles, epochs, rows), F32),
            pltpu.VMEM((tiles * order, rows), F32),
            pltpu.VMEM((order, epochs), F32),
            pltpu.VMEM((tiles * depth, rows), F32),
            pltpu.VMEM((epochs, LANES), BF16),
            pltpu.VMEM((tiles, 1, rows), F32),
            pltpu.VMEM((tiles, LANES, rows), BF16),
            pltpu.VMEM((ITERS, quarter, rows), F32),
            pltpu.VMEM((ITERS, planes - 1, quarter, rows), F32),
            pltpu.VMEM((order, rows), F32),
            pltpu.VMEM((ITERS, order // 2, rows), F32),
            pltpu.VMEM((ITERS, ep_n, GROUP, order // 2, rows), F32),
            pltpu.VMEM((2, rows, epochs), BF16),
            sem((7,)),
            sem((chips,)),
            sem((chips,)),
            sem((ep_n, GROUP)),
            sem((chips,)),
            sem((ep_n,)),
            sem((2, ep_n)),
            sem((2, ep_n)),
            sem((2, ITERS, planes - 1)),
            sem((2, ITERS, inner)),
        ],
        compiler_params=pltpu.CompilerParams(
            collective_id=0, has_side_effects=True, vmem_limit_bytes=ROOM
        ),
    )(
        *(pltpu.with_memory_space_constraint(given, pltpu.HBM) for given in (
            light_curves, valid, pixel[None], inv_sigma[None], modes_init.T,
            epoch_jitter[None], freq_index[None],
        ))
    )
    return pl.pallas_call(
        spectrum_kernel,
        out_shape=(
            jax.ShapeDtypeStruct((rows, cols), F32),
            jax.ShapeDtypeStruct((share, count), F32),
        ),
        in_specs=[vmem] * 3,
        out_specs=(hbm,) * 2,
        scratch_shapes=[
            pltpu.VMEM((parts, share, count // parts), F32),
            sem((parts + 1,)),
        ],
        compiler_params=pltpu.CompilerParams(vmem_limit_bytes=ROOM // 2),
    )(left, ready, basis)


def solution(mesh):
    in_specs = (P("obj", "ep"), P("obj", "ep"), P("obj"), P("obj"), P("ep", None), P(), P())
    out_specs = (P("obj", "ep"), P(("obj", "ep"), None))
    return jax.shard_map(
        per_device, mesh=mesh, in_specs=in_specs, out_specs=out_specs, check_vma=False
    )
```
